32 devices in a mesh: ctx: 8 (over y, x, core), wsh: 4 (over z).
Axes of the slice: x: 2, y: 2, z: 4, core: 2. Of those that a mesh axis runs over, the one named last changes fastest.
Arguments:
- block_input: float32 [4, 1024, 1024], P('wsh', 'ctx'), may hold values from -6 to 6
- out_cotangent: float32 [4, 1024, 1024], P('wsh', 'ctx'), may hold values from -6 to 6
- lengths: int32 [4, 2], P('wsh'), may hold values from 256 to 768, as said below
- slot_block: int32 [16], replicated, may hold values from 0 to 15, as said below
- norm_gains: bfloat16 [2, 1024], P(None, 'wsh'), may hold values from 0.5 to 1.5
- short_filter: float32 [5, 1792], replicated, may hold values from -3 to 3
- step_bias: float32 [24], replicated, may hold values from -3 to -1
- log_rate: float32 [24], replicated, may hold values from -7 to -1.5
- skip_gain: float32 [24], replicated, may hold values from 0.5 to 1.5
- mixer_in: bfloat16 [1024, 3352], P('wsh'), may hold values from -0.1875 to 0.1875
- mixer_out: bfloat16 [1536, 1024], P(None, 'wsh'), may hold values from -0.0390625 to 0.0390625
- attend_in: bfloat16 [1024, 768], P('wsh'), may hold values from -1 to 1
- attend_out: bfloat16 [512, 1024], P(None, 'wsh'), may hold values from -2 to 2
- gate_up: bfloat16 [2, 1024, 2048], P(None, None, 'wsh'), may hold values from -0.1875 to 0.1875
- down_weight: bfloat16 [2048, 1024], P('wsh'), may hold values from -0.125 to 0.125
Outputs:
- block_output: float32 [4, 1024, 1024], P('wsh', 'ctx')
- input_grad: float32 [4, 1024, 1024], P('wsh', 'ctx')
- gains_grad: float32 [2, 1024], P(None, ('ctx', 'wsh'))
- filter_grad: float32 [5, 1792], replicated
- step_bias_grad: float32 [24], replicated
- log_rate_grad: float32 [24], replicated
- skip_grad: float32 [24], replicated
- mixer_in_grad: float32 [1024, 3352], P(('ctx', 'wsh'))
- mixer_out_grad: float32 [1536, 1024], P(None, ('ctx', 'wsh'))
- attend_in_grad: float32 [1024, 768], P(('ctx', 'wsh'))
- attend_out_grad: float32 [512, 1024], P(None, ('ctx', 'wsh'))
- gate_up_grad: float32 [2, 1024, 2048], P(None, 'ctx', 'wsh')
- down_grad: float32 [2048, 1024], P('wsh', 'ctx')
The draws below stay inside these ranges and needn't reach their ends.
Inputs may be any that keep to these rules, and one draw needn't show every extreme that they name: Both lengths of a group are multiples of 64 and sum to 1024. `slot_block`: A permutation of the 16 logical blocks; for every c the slots 2c and 2c + 1 hold blocks k and 15 - k for some k, in either order.
All inputs are finite; a program needn't handle non-finite values.
Results may differ from the reference program's by a relative error of at most 0.015.
Values may be sent and summed in bfloat16 or wider, within the bound.
No kernel may reach another device: no remote copies, remote signals or barrier semaphores. Data moves between devices by JAX's collectives and lax.ppermute only.
A program may use at most 256 MiB of HBM per device.

```python
import math
from functools import partial
import jax
import jax.numpy as jnp
from jax import lax

D = 1024
MHEADS = 24
HEAD_M = 64
NSTATE = 128
QH = 8
KVH = 2
HD = 64
FF = 2048
KERNEL = 4
DSSM = 1536
CONV = 1792
PROJ = 3352
AQ = 512
GRP = 4
QKV = 768
BLK = 64
NB = 16
TG = 1024
GROUPS = 4


def slot_layout(key):
    order = jax.random.permutation(jax.random.fold_in(key, 11), NB // 2)
    flips = jax.random.randint(jax.random.fold_in(key, 12), (NB // 2,), 0, 2)
    early = jnp.where(flips == 1, order, NB - 1 - order)
    late = NB - 1 - early
    return jnp.stack([early, late], axis=1).reshape(NB).astype(jnp.int32)


def draw_lengths(key, part):
    first = jax.random.randint(key, (GROUPS,), NB // 4, NB - NB // 4 + 1) * BLK
    first = first.at[0].set(NB // 4 * BLK)
    return jnp.stack([first, TG - first], axis=1).astype(jnp.int32)


def draw_slot_block(key, part):
    return slot_layout(key)


def draw_block_input(key, part):
    whole_shape = (GROUPS, TG, D)
    return jax.random.truncated_normal(key, -6.0, 6.0, whole_shape, jnp.float32)


def draw_attend_in(key, part):
    return (jax.random.truncated_normal(key, -6.0, 6.0, (D, QKV), jnp.float32) / math.sqrt(D)).astype(jnp.bfloat16)


def levels(key, extent, split, least, high):
    loudness = 1.0
    for position, parts in split:
        heights = jax.random.uniform(jax.random.fold_in(jax.random.fold_in(key, 6), position), (parts,), jnp.float32, least / len(split), high / len(split))
        loudness = loudness * jnp.repeat(jnp.exp(heights), extent[position] // parts).reshape((-1,) + (1,) * (len(extent) - 1 - position))
    return loudness


def noise(key, dims, scale, reach, pieces=(), kind=jnp.bfloat16):
    level = levels(key, dims, pieces, -0.22, 0.18) if pieces else 1.0
    values = jax.random.normal(key, dims, jnp.float32) * scale * level
    return jnp.minimum(jnp.maximum(values, -reach), reach).astype(kind)


def setup_inputs(seed: int = 0) -> dict:
    streams_of = jax.random.split(jax.random.key(seed), 16)
    block_input = draw_block_input(jax.random.fold_in(streams_of[15], 71), 0)
    out_cotangent = noise(streams_of[1], (GROUPS, TG, D), 1.0, 6.0, ((0, 4), (1, 8)), jnp.float32)
    lengths = draw_lengths(jax.random.fold_in(streams_of[15], 71), 0)
    slot_block = draw_slot_block(jax.random.fold_in(streams_of[15], 71), 0)
    norm_gains = jnp.clip(1.0 + 0.1 * jax.random.normal(streams_of[4], (2, D), jnp.float32), 0.5, 1.5).astype(jnp.bfloat16)
    short_filter = noise(streams_of[5], (KERNEL + 1, CONV), 4 ** -0.5, 3.0, (), jnp.float32)
    step_bias = jnp.clip(jax.random.uniform(streams_of[6], (MHEADS,), jnp.float32, -3.0, -1.0), -3.0, -1.0)
    log_rate = jnp.clip(jax.random.uniform(streams_of[7], (MHEADS,), jnp.float32, -7.0, -1.5), -7.0, -1.5)
    skip_gain = jnp.clip(jax.random.uniform(streams_of[8], (MHEADS,), jnp.float32, 0.5, 1.5), 0.5, 1.5)
    mixer_in = noise(streams_of[9], (D, PROJ), D ** -0.5, 0.1875, ((0, 4),))
    mixer_out = noise(streams_of[10], (DSSM, D), (DSSM * 16) ** -0.5, 0.0390625, ((1, 4),))
    attend_in = draw_attend_in(jax.random.fold_in(streams_of[15], 71), 0)
    attend_out = noise(streams_of[12], (AQ, D), 8 ** -0.5, 2.0, ((1, 4),))
    gate_up = noise(streams_of[13], (2, D, FF), D ** -0.5, 0.1875, ((2, 4),))
    down_weight = noise(streams_of[14], (FF, D), FF ** -0.5, 0.125, ((0, 4),))
    return {"block_input": block_input, "out_cotangent": out_cotangent, "lengths": lengths, "slot_block": slot_block, "norm_gains": norm_gains, "short_filter": short_filter, "step_bias": step_bias, "log_rate": log_rate, "skip_gain": skip_gain, "mixer_in": mixer_in, "mixer_out": mixer_out, "attend_in": attend_in, "attend_out": attend_out, "gate_up": gate_up, "down_weight": down_weight}


EPS = 1e-05
ROPE_BASE = 100000000000.0
HIGH = lax.Precision.HIGHEST
NEG_LARGE = -1e+30

def rms_norm(values, gain):
    scale = lax.rsqrt(lax.optimization_barrier(jnp.mean(values * values, axis=-1, keepdims=True)) + EPS)
    return values * scale * gain

def to_wire(values):
    return lax.optimization_barrier(values.astype(jnp.bfloat16)).astype(jnp.float32)

def silu_slope(values):
    sigmoid_value = jax.nn.sigmoid(values)
    return sigmoid_value * (1.0 + values * (1.0 - sigmoid_value))

def rope_tables(positions):
    half = HD // 2
    freqs = jnp.exp(jnp.arange(half, dtype=jnp.float32) * (-2.0 * math.log(ROPE_BASE) / HD))
    angles = positions.astype(jnp.float32)[:, None] * freqs[None, :]
    return (jnp.cos(angles)[:, None, :], jnp.sin(angles)[:, None, :])

def rotate(values, cosines, sines):
    half = values.shape[-1] // 2
    first = values[..., :half]
    second = values[..., half:]
    return jnp.concatenate([first * cosines - second * sines, second * cosines + first * sines], axis=-1)

def matmul_t(left, right):
    return lax.dot_general(left, right, (((0,), (0,)), ((), ())), preferred_element_type=jnp.float32)

def matmul_back(left, right):
    return lax.dot_general(left, right, (((1,), (1,)), ((), ())), preferred_element_type=jnp.float32)

def mixer_prep(conv_input, step_raw, filter_rows, step_bias, log_rate, seq_pos):
    conv = filter_rows[KERNEL] + filter_rows[KERNEL - 1] * conv_input
    for tap_index in range(KERNEL - 1):
        shift = KERNEL - 1 - tap_index
        moved = jnp.concatenate([jnp.zeros((shift, conv_input.shape[1]), conv_input.dtype), conv_input[:-shift]], axis=0)
        conv = conv + filter_rows[tap_index] * jnp.where((seq_pos >= shift)[:, None], moved, 0.0)
    activated = jax.nn.silu(conv)
    step = jax.nn.softplus(step_raw + step_bias)
    return (activated, step, -step * jnp.exp(log_rate))

def ssd_emit(heads_x, b_in, step, log_decay):
    cumulative = jnp.cumsum(log_decay, axis=0)
    weight = jnp.exp(cumulative[-1][None, :] - cumulative) * step
    emitted = jnp.einsum('shp,sn->hpn', heads_x * weight[:, :, None], b_in, precision=HIGH)
    return (emitted, cumulative[-1])

def ssd_output(heads_x, b_in, c_in, step, log_decay, state_in, skip_gain):
    cumulative = jnp.cumsum(log_decay, axis=0)
    count = heads_x.shape[0]
    lower = (jnp.arange(count)[:, None] >= jnp.arange(count)[None, :])[:, :, None]
    gaps = jnp.where(lower, cumulative[:, None, :] - cumulative[None, :, :], 0.0)
    kernel = jnp.where(lower, jnp.exp(gaps), 0.0) * jnp.dot(c_in, b_in.T, precision=HIGH)[:, :, None]
    inner = jnp.einsum('tsh,shp->thp', kernel, heads_x * step[:, :, None], precision=HIGH)
    carried = jnp.einsum('hpn,tn->thp', state_in, c_in, precision=HIGH) * jnp.exp(cumulative)[:, :, None]
    return inner + carried + skip_gain[None, :, None] * heads_x

def group_pass(tokens, cotangent, first_len, norm_gains, short_filter, step_bias, log_rate, skip_gain, mixer_in, mixer_out, attend_in, attend_out, gate_up, down_weight):
    positions = jnp.arange(TG, dtype=jnp.int32)
    logical_ids = jnp.arange(NB, dtype=jnp.int32)
    second = positions >= first_len
    seq_pos = positions - jnp.where(second, first_len, 0)
    scale = 1.0 / math.sqrt(HD)
    kv_width = KVH * HD
    gain_first = norm_gains[0].astype(jnp.float32)
    gain_second = norm_gains[1].astype(jnp.float32)
    normed, first_norm_vjp = jax.vjp(rms_norm, tokens, gain_first)
    normed_first = normed.astype(jnp.bfloat16)
    mixed = jnp.dot(normed_first, mixer_in, preferred_element_type=jnp.float32)
    gate_z = mixed[:, :DSSM]
    conv_input = mixed[:, DSSM:DSSM + CONV]
    step_raw = mixed[:, DSSM + CONV:]
    (activated, step, log_decay), prep_vjp = jax.vjp(partial(mixer_prep, seq_pos=seq_pos), conv_input, step_raw, short_filter, step_bias, log_rate)
    heads_x = activated[:, :DSSM].reshape(NB, BLK, MHEADS, HEAD_M)
    b_in = activated[:, DSSM:DSSM + NSTATE].reshape(NB, BLK, NSTATE)
    c_in = activated[:, DSSM + NSTATE:].reshape(NB, BLK, NSTATE)
    step_blocks = step.reshape(NB, BLK, MHEADS)
    decay_blocks = log_decay.reshape(NB, BLK, MHEADS)
    starts = (logical_ids == 0) | (logical_ids * BLK == first_len)
    zero_state = jnp.zeros((MHEADS, HEAD_M, NSTATE), jnp.float32)

    def forward_step(state, inputs):
        heads_b, b_blk, c_blk, step_b, decay_b, is_start = inputs
        state_in = jnp.where(is_start, 0.0, state)
        out_y = ssd_output(heads_b, b_blk, c_blk, step_b, decay_b, state_in, skip_gain)
        emitted, total = ssd_emit(heads_b, b_blk, step_b, decay_b)
        return (jnp.exp(total)[:, None, None] * state_in + to_wire(emitted), (out_y, state_in))
    _, (mixer_y, states_in) = lax.scan(forward_step, zero_state, (heads_x, b_in, c_in, step_blocks, decay_blocks, starts))
    mixer_flat = mixer_y.reshape(TG, DSSM)
    gated = (mixer_flat * jax.nn.silu(gate_z)).astype(jnp.bfloat16)
    mixer_branch = jnp.dot(gated, mixer_out, preferred_element_type=jnp.float32)
    projected = jnp.dot(normed_first, attend_in, preferred_element_type=jnp.float32)
    cosines, sines = rope_tables(seq_pos)
    queries = rotate(projected[:, :AQ].reshape(TG, QH, HD), cosines, sines).astype(jnp.bfloat16)
    keys_rot = rotate(projected[:, AQ:AQ + kv_width].reshape(TG, KVH, HD), cosines, sines).astype(jnp.bfloat16)
    values = projected[:, AQ + kv_width:].astype(jnp.bfloat16).reshape(TG, KVH, HD)
    keys_f = keys_rot.astype(jnp.float32)
    values_f = values.astype(jnp.float32)

    def block_scores(index):
        query_block = lax.dynamic_slice_in_dim(queries, index * BLK, BLK).astype(jnp.float32).reshape(BLK, KVH, GRP, HD)
        query_pos = index * BLK + jnp.arange(BLK, dtype=jnp.int32)
        allowed = (positions[None, :] <= query_pos[:, None]) & (second[None, :] == (query_pos >= first_len)[:, None])
        scores = jnp.einsum('tkgd,skd->kgts', query_block, keys_f, precision=HIGH) * scale
        return (query_block, allowed, scores)

    def attend_forward(index):
        _, allowed, scores = block_scores(index)
        masked = jnp.where(allowed, scores, NEG_LARGE)
        top = lax.optimization_barrier(jnp.max(masked, axis=-1))
        weights = jnp.where(allowed, jnp.exp(masked - top[..., None]), 0.0)
        denominator = lax.optimization_barrier(jnp.sum(weights, axis=-1))
        probs = weights / denominator[..., None]
        out_heads = jnp.einsum('kgts,skd->tkgd', probs, values_f, precision=HIGH)
        return (out_heads.reshape(BLK, AQ), top + jnp.log(denominator))
    attn_blocks, log_total = lax.map(attend_forward, logical_ids)
    attn_rows = attn_blocks.reshape(TG, AQ)
    attn_b = attn_rows.astype(jnp.bfloat16)
    attn_branch = jnp.dot(attn_b, attend_out, preferred_element_type=jnp.float32)
    hidden = tokens + mixer_branch + attn_branch
    normed2, second_norm_vjp = jax.vjp(rms_norm, hidden, gain_second)
    normed_second = normed2.astype(jnp.bfloat16)
    gate_part = jnp.dot(normed_second, gate_up[0], preferred_element_type=jnp.float32)
    up_part = jnp.dot(normed_second, gate_up[1], preferred_element_type=jnp.float32)
    mlp_act = (jax.nn.silu(gate_part) * up_part).astype(jnp.bfloat16)
    output = hidden + jnp.dot(mlp_act, down_weight, preferred_element_type=jnp.float32)
    cot_b = cotangent.astype(jnp.bfloat16)
    down_grad = matmul_t(mlp_act, cot_b)
    d_mlp = matmul_back(cot_b, down_weight)
    d_gate = (d_mlp * up_part * silu_slope(gate_part)).astype(jnp.bfloat16)
    d_up = (d_mlp * jax.nn.silu(gate_part)).astype(jnp.bfloat16)
    gate_up_grad = jnp.stack([matmul_t(normed_second, d_gate), matmul_t(normed_second, d_up)], axis=0)
    d_normed_second = matmul_back(d_gate, gate_up[0]) + matmul_back(d_up, gate_up[1])
    d_hidden_norm, d_gain_second = second_norm_vjp(d_normed_second)
    hidden_grad = cotangent + d_hidden_norm
    hidden_b = hidden_grad.astype(jnp.bfloat16)
    attend_out_grad = matmul_t(attn_b, hidden_b)
    mixer_out_grad = matmul_t(gated, hidden_b)
    d_attn_b = matmul_back(hidden_b, attend_out).astype(jnp.bfloat16)
    d_gated = matmul_back(hidden_b, mixer_out)
    d_heads_f = d_attn_b.astype(jnp.float32).reshape(TG, KVH, GRP, HD)
    delta_all = lax.optimization_barrier(jnp.sum(d_heads_f * attn_rows.reshape(TG, KVH, GRP, HD), axis=-1))

    def attend_backward(carry, inputs):
        index, lse_block = inputs
        key_grad, value_grad = carry
        query_block, allowed, scores = block_scores(index)
        probs = jnp.where(allowed, jnp.exp(jnp.where(allowed, scores, 0.0) - lse_block[..., None]), 0.0)
        d_block = lax.dynamic_slice_in_dim(d_heads_f, index * BLK, BLK)
        delta = jnp.transpose(lax.dynamic_slice_in_dim(delta_all, index * BLK, BLK), (1, 2, 0))
        d_probs = jnp.einsum('tkgd,skd->kgts', d_block, values_f, precision=HIGH)
        d_scores = probs * (d_probs - delta[..., None]) * scale
        query_grad = jnp.einsum('kgts,skd->tkgd', d_scores, keys_f, precision=HIGH)
        key_grad = key_grad + jnp.einsum('kgts,tkgd->skd', d_scores, query_block, precision=HIGH)
        value_grad = value_grad + jnp.einsum('kgts,tkgd->skd', probs, d_block, precision=HIGH)
        return ((key_grad, value_grad), query_grad.reshape(BLK, AQ))
    zero_keys = jnp.zeros((TG, KVH, HD), jnp.float32)
    (key_grad, value_grad), query_grad = lax.scan(attend_backward, (zero_keys, zero_keys), (logical_ids, log_total))
    d_query = rotate(query_grad.reshape(TG, QH, HD), cosines, -sines).reshape(TG, AQ)
    d_key = rotate(key_grad, cosines, -sines).reshape(TG, kv_width)
    d_attend = jnp.concatenate([d_query, d_key, value_grad.reshape(TG, kv_width)], axis=1).astype(jnp.bfloat16)
    attend_in_grad = matmul_t(normed_first, d_attend)
    d_normed_attend = matmul_back(d_attend, attend_in)
    d_mixer = (d_gated * jax.nn.silu(gate_z)).reshape(NB, BLK, MHEADS, HEAD_M)
    d_z = d_gated * mixer_flat * silu_slope(gate_z)

    def backward_step(later, inputs):
        heads_b, b_blk, c_blk, step_b, decay_b, state_in, d_y, is_start = inputs
        _, out_vjp = jax.vjp(ssd_output, heads_b, b_blk, c_blk, step_b, decay_b, state_in, skip_gain)
        g_heads, g_b, g_c, g_step, g_decay, g_state, g_skip = out_vjp(d_y)
        (_, total), emit_vjp = jax.vjp(ssd_emit, heads_b, b_blk, step_b, decay_b)
        d_total = jnp.exp(total) * lax.optimization_barrier(jnp.sum(later * state_in, axis=(1, 2)))
        e_heads, e_b, e_step, e_decay = emit_vjp((later, d_total))
        new_later = jnp.where(is_start, 0.0, to_wire(g_state) + jnp.exp(total)[:, None, None] * later)
        return (new_later, (g_heads + e_heads, g_b + e_b, g_c, g_step + e_step, g_decay + e_decay, g_skip))
    _, (d_heads_x, d_b, d_c, d_step, d_decay, d_skip) = lax.scan(backward_step, zero_state, (heads_x, b_in, c_in, step_blocks, decay_blocks, states_in, d_mixer, starts), reverse=True)
    skip_grad = lax.optimization_barrier(jnp.sum(d_skip, axis=0))
    d_activated = jnp.concatenate([d_heads_x.reshape(TG, DSSM), d_b.reshape(TG, NSTATE), d_c.reshape(TG, NSTATE)], axis=1)
    d_conv_input, d_step_raw, filter_grad, step_bias_grad, log_rate_grad = prep_vjp((d_activated, d_step.reshape(TG, MHEADS), d_decay.reshape(TG, MHEADS)))
    d_mixed = jnp.concatenate([d_z, d_conv_input, d_step_raw], axis=1).astype(jnp.bfloat16)
    mixer_in_grad = matmul_t(normed_first, d_mixed)
    d_normed_mix = matmul_back(d_mixed, mixer_in)
    d_tokens_norm, d_gain_first = first_norm_vjp(d_normed_mix + d_normed_attend)
    input_grad = hidden_grad + d_tokens_norm
    gains_grad = jnp.stack([d_gain_first, d_gain_second], axis=0)
    grads = (gains_grad, filter_grad, step_bias_grad, log_rate_grad, skip_grad, mixer_in_grad, mixer_out_grad, attend_in_grad, attend_out_grad, gate_up_grad, down_grad)
    return (output, input_grad, grads)

def reference(block_input, out_cotangent, lengths, slot_block, norm_gains, short_filter, step_bias, log_rate, skip_gain, mixer_in, mixer_out, attend_in, attend_out, gate_up, down_weight):
    logical_ids = jnp.arange(NB, dtype=jnp.int32)
    slot_of_block = jnp.zeros((NB,), jnp.int32).at[slot_block].set(logical_ids)
    zero_grads = (jnp.zeros((2, D), jnp.float32), jnp.zeros((KERNEL + 1, CONV), jnp.float32), jnp.zeros((MHEADS,), jnp.float32), jnp.zeros((MHEADS,), jnp.float32), jnp.zeros((MHEADS,), jnp.float32), jnp.zeros((D, PROJ), jnp.float32), jnp.zeros((DSSM, D), jnp.float32), jnp.zeros((D, QKV), jnp.float32), jnp.zeros((AQ, D), jnp.float32), jnp.zeros((2, D, FF), jnp.float32), jnp.zeros((FF, D), jnp.float32))

    def one_group(grads, group):
        tokens_slot, cot_slot, group_lengths = group
        tokens = tokens_slot.reshape(NB, BLK, D)[slot_of_block].reshape(TG, D)
        cotangent = cot_slot.reshape(NB, BLK, D)[slot_of_block].reshape(TG, D)
        output, in_grad, group_grads = group_pass(tokens, cotangent, group_lengths[0], norm_gains, short_filter, step_bias, log_rate, skip_gain, mixer_in, mixer_out, attend_in, attend_out, gate_up, down_weight)
        grads = jax.tree.map(lambda left, right: left + right, grads, group_grads)
        out_slot = output.reshape(NB, BLK, D)[slot_block].reshape(TG, D)
        grad_slot = in_grad.reshape(NB, BLK, D)[slot_block].reshape(TG, D)
        return (grads, (out_slot, grad_slot))
    grads, (outputs, input_grads) = lax.scan(one_group, zero_grads, (block_input, out_cotangent, lengths))
    gains_grad, filter_grad, step_bias_grad, log_rate_grad, skip_grad, mixer_in_grad, mixer_out_grad, attend_in_grad, attend_out_grad, gate_up_grad, down_grad = grads
    return (outputs, input_grads, gains_grad, filter_grad, step_bias_grad, log_rate_grad, skip_grad, mixer_in_grad, mixer_out_grad, attend_in_grad, attend_out_grad, gate_up_grad, down_grad)
```

```python
import math

import jax
import jax.numpy as jnp
from jax import lax
from jax.sharding import PartitionSpec as P

MHEADS = 24
HEAD_M = 64
NSTATE = 128
QH = 8
KVH = 2
HD = 64
KERNEL = 4
DSSM = 1536
CONV = 1792
AQ = 512
GRP = 4


EPS = 1e-05
ROPE_BASE = 100000000000.0
HIGH = lax.Precision.HIGHEST
NEG_LARGE = -1e30


def rms_norm(values, gain):
    scale = lax.rsqrt(jnp.mean(values * values, axis=-1, keepdims=True) + EPS)
    return values * scale * gain


def silu_slope(values):
    sigmoid_value = jax.nn.sigmoid(values)
    return sigmoid_value * (1.0 + values * (1.0 - sigmoid_value))


def rope_tables(positions):
    half = HD // 2
    freqs = jnp.exp(jnp.arange(half, dtype=jnp.float32) * (-2.0 * math.log(ROPE_BASE) / HD))
    angles = positions.astype(jnp.float32)[:, None] * freqs[None, :]
    return (jnp.cos(angles)[:, None, :], jnp.sin(angles)[:, None, :])


def rotate(values, cosines, sines):
    half = values.shape[-1] // 2
    first = values[..., :half]
    second = values[..., half:]
    return jnp.concatenate(
        [first * cosines - second * sines, second * cosines + first * sines], axis=-1
    )


def matmul_t(left, right):
    return lax.dot_general(
        left, right, (((0,), (0,)), ((), ())), preferred_element_type=jnp.float32
    )


def matmul_back(left, right):
    return lax.dot_general(
        left, right, (((1,), (1,)), ((), ())), preferred_element_type=jnp.float32
    )


def step_prep(step_raw, step_bias, log_rate):
    step = jax.nn.softplus(step_raw + step_bias)
    return (step, -step * jnp.exp(log_rate))


def conv_prep(conv_blocks, tails_in, filter_rows):
    count = conv_blocks.shape[1]
    extended = jnp.concatenate([tails_in, conv_blocks], axis=1)
    conv = filter_rows[KERNEL] + filter_rows[KERNEL - 1] * conv_blocks
    for tap_index in range(KERNEL - 1):
        conv = conv + filter_rows[tap_index] * extended[:, tap_index : tap_index + count]
    return jax.nn.silu(conv)


def ssd_emit(heads_x, b_in, step, log_decay):
    cumulative = jnp.cumsum(log_decay, axis=0)
    weight = jnp.exp(cumulative[-1][None, :] - cumulative) * step
    emitted = jnp.einsum("shp,sn->hpn", heads_x * weight[:, :, None], b_in, precision=HIGH)
    return (emitted, cumulative[-1])


def ssd_output(heads_x, b_in, c_in, step, log_decay, state_in, skip_gain):
    cumulative = jnp.cumsum(log_decay, axis=0)
    count = heads_x.shape[0]
    lower = (jnp.arange(count)[:, None] >= jnp.arange(count)[None, :])[:, :, None]
    gaps = jnp.where(lower, cumulative[:, None, :] - cumulative[None, :, :], 0.0)
    kernel = (
        jnp.where(lower, jnp.exp(gaps), 0.0) * jnp.dot(c_in, b_in.T, precision=HIGH)[:, :, None]
    )
    inner = jnp.einsum("tsh,shp->thp", kernel, heads_x * step[:, :, None], precision=HIGH)
    carried = (
        jnp.einsum("hpn,tn->thp", state_in, c_in, precision=HIGH) * jnp.exp(cumulative)[:, :, None]
    )
    return inner + carried + skip_gain[None, :, None] * heads_x


def chain_fold(slot_block, my_blocks, block_second, first_len, block_rows, prefix, later):

    def fold(total, piece, start):
        count = piece.shape[0]
        same = (slot_block * block_rows >= first_len)[None, :] == block_second[:, None]
        if later:
            valid = same & (slot_block[None, :] > my_blocks[:, None])
            gaps = (
                jnp.take(prefix, slot_block, axis=0)[None, :, :]
                - jnp.take(prefix, my_blocks + 1, axis=0)[:, None, :]
            )
        else:
            valid = same & (slot_block[None, :] < my_blocks[:, None])
            gaps = (
                jnp.take(prefix, my_blocks, axis=0)[:, None, :]
                - jnp.take(prefix, slot_block + 1, axis=0)[None, :, :]
            )
        factors = jnp.where(
            valid[:, :, None], jnp.exp(jnp.where(valid[:, :, None], gaps, 0.0)), 0.0
        )
        step_size = math.gcd(count, 8)

        def add_rows(index, running):
            rows_piece = lax.dynamic_slice_in_dim(piece, index * step_size, step_size).astype(
                jnp.float32
            )
            factor_rows = lax.dynamic_slice_in_dim(factors, index * step_size, step_size, 1)
            return running + jnp.einsum("bsh,shpn->bhpn", factor_rows, rows_piece, precision=HIGH)

        return lax.fori_loop(0, count // step_size, add_rows, total)

    return fold


def in_blocks(step_fn, carry, piece):
    count = piece.shape[0]
    block_size = math.gcd(count, 512)

    def visit(block_index, state):
        sub_piece = lax.dynamic_slice_in_dim(piece, block_index * block_size, block_size)
        return step_fn(state, sub_piece, block_index * block_size)

    return lax.fori_loop(0, count // block_size, visit, carry)


def on_device(
    block_input,
    out_cotangent,
    lengths,
    slot_block,
    norm_gains,
    short_filter,
    step_bias,
    log_rate,
    skip_gain,
    mixer_in,
    mixer_out,
    attend_in,
    attend_out,
    gate_up,
    down_weight,
):
    gains_all, in_mix, out_mix, in_attend, out_attend = (
        lax.all_gather(norm_gains, "wsh", axis=1, tiled=True),
        lax.all_gather(mixer_in, "wsh", axis=0, tiled=True),
        lax.all_gather(mixer_out, "wsh", axis=1, tiled=True),
        lax.all_gather(attend_in, "wsh", axis=0, tiled=True),
        lax.all_gather(attend_out, "wsh", axis=1, tiled=True),
    )
    ctx_count = lax.axis_size("ctx")
    block_count = 2 * ctx_count
    rows = block_input.shape[1]
    block_rows = rows // 2
    kv_width = KVH * HD
    scale = 1.0 / math.sqrt(HD)
    tokens = block_input[0]
    cotangent = out_cotangent[0]
    first_len = lengths[0, 0]
    logical_ids = jnp.arange(block_count, dtype=jnp.int32)
    my_blocks = lax.dynamic_slice_in_dim(slot_block, 2 * lax.axis_index("ctx"), 2)
    block_offsets = jnp.arange(block_rows, dtype=jnp.int32)
    my_pos = (my_blocks[:, None] * block_rows + block_offsets[None, :]).reshape(rows)
    my_second = my_pos >= first_len
    seq_pos = my_pos - jnp.where(my_second, first_len, 0)
    block_second = my_blocks * block_rows >= first_len
    is_start = (my_blocks == 0) | (my_blocks * block_rows == first_len)
    key_pos = (slot_block[:, None] * block_rows + block_offsets[None, :]).reshape(
        block_count * block_rows
    )
    gain_first = gains_all[0].astype(jnp.float32)
    gain_second = gains_all[1].astype(jnp.float32)
    normed, first_norm_vjp = jax.vjp(rms_norm, tokens, gain_first)
    normed_first = normed.astype(jnp.bfloat16)
    mixed = jnp.dot(normed_first, in_mix, preferred_element_type=jnp.float32)
    gate_z = mixed[:, :DSSM]
    conv_input = mixed[:, DSSM : DSSM + CONV]
    step_raw = mixed[:, DSSM + CONV :]
    (step, log_decay), step_vjp = jax.vjp(step_prep, step_raw, step_bias, log_rate)
    step_blocks = step.reshape(2, block_rows, MHEADS)
    decay_blocks = log_decay.reshape(2, block_rows, MHEADS)
    totals = jnp.sum(decay_blocks, axis=1)
    conv_blocks = conv_input.reshape(2, block_rows, CONV)
    tails = conv_blocks[:, block_rows - (KERNEL - 1) :, :]
    all_tails, all_totals = (
        lax.all_gather(tails, "ctx", axis=0, tiled=True),
        lax.all_gather(totals, "ctx", axis=0, tiled=True),
    )
    one_hot = (slot_block[None, :] == logical_ids[:, None]).astype(jnp.float32)
    totals_logical = jnp.dot(one_hot, all_totals, precision=HIGH)
    prefix = jnp.concatenate(
        [jnp.zeros((1, MHEADS), jnp.float32), jnp.cumsum(totals_logical, axis=0)], axis=0
    )
    pred_slot = jnp.sum(
        jnp.where(slot_block[None, :] == (my_blocks - 1)[:, None], logical_ids[None, :], 0), axis=1
    )
    keep_tail = jnp.where(is_start, 0.0, 1.0).astype(jnp.float32)
    tails_in = jnp.take(all_tails, pred_slot, axis=0) * keep_tail[:, None, None]
    activated, conv_vjp = jax.vjp(conv_prep, conv_blocks, tails_in, short_filter)
    heads_x = activated[:, :, :DSSM].reshape(2, block_rows, MHEADS, HEAD_M)
    b_in = activated[:, :, DSSM : DSSM + NSTATE]
    c_in = activated[:, :, DSSM + NSTATE :]
    (emitted, emit_totals), emit_vjp = jax.vjp(
        jax.vmap(ssd_emit), heads_x, b_in, step_blocks, decay_blocks
    )
    zero_states = jnp.zeros((2, MHEADS, HEAD_M, NSTATE), jnp.float32)
    chain_forward = chain_fold(
        slot_block, my_blocks, block_second, first_len, block_rows, prefix, False
    )
    state_in = chain_forward(
        zero_states,
        lax.all_gather(emitted.astype(jnp.bfloat16), "ctx", axis=0, tiled=True),
        jnp.int32(0),
    )
    mixer_y, out_vjp = jax.vjp(
        jax.vmap(ssd_output, in_axes=(0, 0, 0, 0, 0, 0, None)),
        heads_x,
        b_in,
        c_in,
        step_blocks,
        decay_blocks,
        state_in,
        skip_gain,
    )
    mixer_flat = mixer_y.reshape(rows, DSSM)
    gated = (mixer_flat * jax.nn.silu(gate_z)).astype(jnp.bfloat16)
    mixer_branch = jnp.dot(gated, out_mix, preferred_element_type=jnp.float32)
    projected = jnp.dot(normed_first, in_attend, preferred_element_type=jnp.float32)
    cosines, sines = rope_tables(seq_pos)
    queries = rotate(projected[:, :AQ].reshape(rows, QH, HD), cosines, sines).astype(jnp.bfloat16)
    keys_rot = rotate(
        projected[:, AQ : AQ + kv_width].reshape(rows, KVH, HD), cosines, sines
    ).astype(jnp.bfloat16)
    values = projected[:, AQ + kv_width :].astype(jnp.bfloat16)
    kv_local = jnp.concatenate([keys_rot.reshape(rows, kv_width), values], axis=1)
    query_heads = queries.reshape(rows, KVH, GRP, HD)

    def allowed_at(start, count):
        piece_pos = lax.dynamic_slice_in_dim(key_pos, start, count)
        return (piece_pos[None, :] <= my_pos[:, None]) & (
            (piece_pos >= first_len)[None, :] == my_second[:, None]
        )

    def split_piece(piece):
        count = piece.shape[0]
        return (
            piece[:, :kv_width].reshape(count, KVH, HD),
            piece[:, kv_width:].reshape(count, KVH, HD),
        )

    def attend_step(carry, piece, start):
        top, denominator, running = carry
        keys_piece, values_piece = split_piece(piece)
        allowed = allowed_at(start, piece.shape[0])
        scores = (
            jnp.einsum(
                "tkgd,skd->kgts", query_heads, keys_piece, preferred_element_type=jnp.float32
            )
            * scale
        )
        masked = jnp.where(allowed, scores, NEG_LARGE)
        new_top = jnp.maximum(top, jnp.max(masked, axis=-1))
        weights = jnp.where(allowed, jnp.exp(masked - new_top[..., None]), 0.0)
        factor = jnp.exp(top - new_top)
        denominator = denominator * factor + jnp.sum(weights, axis=-1)
        running = running * factor[..., None] + jnp.einsum(
            "kgts,skd->kgtd", weights, values_piece.astype(jnp.float32), precision=HIGH
        )
        return (new_top, denominator, running)

    start_carry = (
        jnp.full((KVH, GRP, rows), NEG_LARGE, jnp.float32),
        jnp.zeros((KVH, GRP, rows), jnp.float32),
        jnp.zeros((KVH, GRP, rows, HD), jnp.float32),
    )
    top, denominator, running = in_blocks(
        attend_step, start_carry, lax.all_gather(kv_local, "ctx", axis=0, tiled=True)
    )
    log_total = top + jnp.log(denominator)
    attn_heads = running / denominator[..., None]
    attn_rows = jnp.transpose(attn_heads, (2, 0, 1, 3)).reshape(rows, AQ)
    attn_b = attn_rows.astype(jnp.bfloat16)
    attn_branch = jnp.dot(attn_b, out_attend, preferred_element_type=jnp.float32)
    hidden = tokens + mixer_branch + attn_branch
    normed2, second_norm_vjp = jax.vjp(rms_norm, hidden, gain_second)
    normed_second = normed2.astype(jnp.bfloat16)
    cot_b = cotangent.astype(jnp.bfloat16)
    gate_whole, down_rows = (
        lax.all_gather(gate_up, "wsh", axis=2, tiled=True),
        lax.all_gather(down_weight, "wsh", axis=0, tiled=True),
    )
    gate_cols = gate_whole[0]
    up_cols = gate_whole[1]
    gate_part = jnp.dot(normed_second, gate_cols, preferred_element_type=jnp.float32)
    up_part = jnp.dot(normed_second, up_cols, preferred_element_type=jnp.float32)
    mlp_act = (jax.nn.silu(gate_part) * up_part).astype(jnp.bfloat16)
    mlp_out = jnp.dot(mlp_act, down_rows, preferred_element_type=jnp.float32)
    output = hidden + mlp_out
    down_local = matmul_t(mlp_act, cot_b)
    d_mlp = matmul_back(cot_b, down_rows)
    d_gate = (d_mlp * up_part * silu_slope(gate_part)).astype(jnp.bfloat16)
    d_up = (d_mlp * jax.nn.silu(gate_part)).astype(jnp.bfloat16)
    gate_up_local = jnp.stack(
        [matmul_t(normed_second, d_gate), matmul_t(normed_second, d_up)], axis=0
    )
    d_normed_second = matmul_back(d_gate, gate_cols) + matmul_back(d_up, up_cols)
    d_hidden_norm, d_gain_second = second_norm_vjp(d_normed_second)
    hidden_grad = cotangent + d_hidden_norm
    hidden_b = hidden_grad.astype(jnp.bfloat16)
    attend_out_grad = matmul_t(attn_b, hidden_b)
    mixer_out_grad = matmul_t(gated, hidden_b)
    d_attn_b = matmul_back(hidden_b, out_attend).astype(jnp.bfloat16)
    d_gated = matmul_back(hidden_b, out_mix)
    d_heads = d_attn_b.reshape(rows, KVH, GRP, HD)
    d_heads_f = d_heads.astype(jnp.float32)
    query_f = queries.astype(jnp.float32).reshape(rows, KVH, GRP, HD)
    delta = jnp.sum(jnp.transpose(d_heads_f, (1, 2, 0, 3)) * attn_heads, axis=-1)

    def attend_back(carry, piece, start):
        query_grad, kv_grad = carry
        count = piece.shape[0]
        keys_piece, values_piece = split_piece(piece)
        allowed = allowed_at(start, count)
        scores = (
            jnp.einsum(
                "tkgd,skd->kgts", query_heads, keys_piece, preferred_element_type=jnp.float32
            )
            * scale
        )
        probs = jnp.where(
            allowed, jnp.exp(jnp.where(allowed, scores, 0.0) - log_total[..., None]), 0.0
        )
        d_probs = jnp.einsum(
            "tkgd,skd->kgts", d_heads, values_piece, preferred_element_type=jnp.float32
        )
        d_scores = probs * (d_probs - delta[..., None]) * scale
        query_grad = query_grad + jnp.einsum(
            "kgts,skd->tkgd", d_scores, keys_piece.astype(jnp.float32), precision=HIGH
        )
        key_grad = jnp.einsum("kgts,tkgd->skd", d_scores, query_f, precision=HIGH)
        value_grad = jnp.einsum("kgts,tkgd->skd", probs, d_heads_f, precision=HIGH)
        update = jnp.concatenate(
            [key_grad.reshape(count, kv_width), value_grad.reshape(count, kv_width)], axis=1
        )
        kv_grad = lax.dynamic_update_slice_in_dim(kv_grad, update, start, 0)
        return (query_grad, kv_grad)

    back_carry = (
        jnp.zeros((rows, KVH, GRP, HD), jnp.float32),
        jnp.zeros((block_count * block_rows, 2 * kv_width), jnp.float32),
    )
    query_grad, kv_grad = in_blocks(
        attend_back, back_carry, lax.all_gather(kv_local, "ctx", axis=0, tiled=True)
    )
    d_mixer = (d_gated * jax.nn.silu(gate_z)).reshape(2, block_rows, MHEADS, HEAD_M)
    d_z = d_gated * mixer_flat * silu_slope(gate_z)
    g_heads, g_b, g_c, g_step, g_decay, g_state, g_skip = out_vjp(d_mixer)
    chain_backward = chain_fold(
        slot_block, my_blocks, block_second, first_len, block_rows, prefix, True
    )
    later_sum = chain_backward(
        zero_states,
        lax.all_gather(g_state.astype(jnp.bfloat16), "ctx", axis=0, tiled=True),
        jnp.int32(0),
    )
    d_totals = jnp.exp(emit_totals) * jnp.sum(later_sum * state_in, axis=(2, 3))
    e_heads, e_b, e_step, e_decay = emit_vjp((later_sum, d_totals))
    d_activated = jnp.concatenate(
        [(g_heads + e_heads).reshape(2, block_rows, DSSM), g_b + e_b, g_c], axis=2
    )
    d_conv_blocks, d_tails, filter_grad = conv_vjp(d_activated)
    tail_buffer = (
        jnp.zeros((block_count, KERNEL - 1, CONV), jnp.float32)
        .at[pred_slot]
        .add(d_tails * keep_tail[:, None, None])
    )
    d_step_raw, step_bias_grad, log_rate_grad = step_vjp(
        ((g_step + e_step).reshape(rows, MHEADS), (g_decay + e_decay).reshape(rows, MHEADS))
    )
    kv_mine, tail_back, gate_up_part, down_part = (
        lax.psum_scatter(
            kv_grad.astype(jnp.bfloat16), "ctx", scatter_dimension=0, tiled=True
        ).astype(jnp.float32),
        lax.psum_scatter(
            tail_buffer.astype(jnp.bfloat16), "ctx", scatter_dimension=0, tiled=True
        ).astype(jnp.float32),
        lax.psum_scatter(
            gate_up_local.astype(jnp.bfloat16), "ctx", scatter_dimension=1, tiled=True
        ).astype(jnp.float32),
        lax.psum_scatter(
            down_local.astype(jnp.bfloat16), "ctx", scatter_dimension=1, tiled=True
        ).astype(jnp.float32),
    )
    d_query = rotate(query_grad.reshape(rows, QH, HD), cosines, -sines).reshape(rows, AQ)
    d_key = rotate(kv_mine[:, :kv_width].reshape(rows, KVH, HD), cosines, -sines).reshape(
        rows, kv_width
    )
    d_attend = jnp.concatenate([d_query, d_key, kv_mine[:, kv_width:]], axis=1).astype(jnp.bfloat16)
    attend_in_grad = matmul_t(normed_first, d_attend)
    d_normed_attend = matmul_back(d_attend, in_attend)
    d_conv_blocks = d_conv_blocks.at[:, block_rows - (KERNEL - 1) :, :].add(tail_back)
    d_mixed = jnp.concatenate([d_z, d_conv_blocks.reshape(rows, CONV), d_step_raw], axis=1).astype(
        jnp.bfloat16
    )
    mixer_in_grad = matmul_t(normed_first, d_mixed)
    d_normed_mix = matmul_back(d_mixed, in_mix)
    d_tokens_norm, d_gain_first = first_norm_vjp(d_normed_mix + d_normed_attend)
    input_grad = hidden_grad + d_tokens_norm
    gains_grad = jnp.stack([d_gain_first, d_gain_second], axis=0)
    step_bias_grad, log_rate_grad, skip_grad, filter_grad = lax.psum(
        (step_bias_grad, log_rate_grad, g_skip, filter_grad), ("ctx", "wsh")
    )
    gate_up_grad, down_grad = (
        lax.psum_scatter(
            gate_up_part.astype(jnp.bfloat16), "wsh", scatter_dimension=2, tiled=True
        ).astype(jnp.float32),
        lax.psum_scatter(
            down_part.astype(jnp.bfloat16), "wsh", scatter_dimension=0, tiled=True
        ).astype(jnp.float32),
    )
    results = (
        lax.psum_scatter(gains_grad, ("ctx", "wsh"), scatter_dimension=1, tiled=True),
        lax.psum_scatter(mixer_in_grad, ("ctx", "wsh"), scatter_dimension=0, tiled=True),
        lax.psum_scatter(mixer_out_grad, ("ctx", "wsh"), scatter_dimension=1, tiled=True),
        lax.psum_scatter(attend_in_grad, ("ctx", "wsh"), scatter_dimension=0, tiled=True),
        lax.psum_scatter(attend_out_grad, ("ctx", "wsh"), scatter_dimension=1, tiled=True),
    )
    return (
        output[None],
        input_grad[None],
        results[0],
        filter_grad,
        step_bias_grad,
        log_rate_grad,
        skip_grad,
        results[1],
        results[2],
        results[3],
        results[4],
        gate_up_grad,
        down_grad,
    )


def xor_pairs(count, bits):
    return [(index, index ^ bits) for index in range(count)]


def gather_ctx(values):
    count = lax.axis_size("ctx")
    first_core = lax.axis_index("ctx") % 2 == 0
    near_x = lax.ppermute(values, "ctx", xor_pairs(count, 2))
    near_y = lax.ppermute(values, "ctx", xor_pairs(count, 4))
    far = lax.ppermute(
        jnp.where(first_core, near_x, near_y),
        "ctx",
        [(index, index ^ (4 if index % 2 == 0 else 2)) for index in range(count)],
    )
    mine = [values, near_x, near_y, far]
    other = [lax.ppermute(piece, "ctx", xor_pairs(count, 1)) for piece in mine]
    return jnp.stack([piece for pair in zip(mine, other) for piece in pair], axis=0)


def scatter_ctx(parts):
    count = lax.axis_size("ctx")
    first_core = lax.axis_index("ctx") % 2 == 0
    wire = lambda piece: piece.astype(jnp.bfloat16)
    sums = [
        parts[k] + lax.ppermute(wire(parts[k + 1]), "ctx", xor_pairs(count, 1)).astype(jnp.float32)
        for k in (6, 2, 4, 0)
    ]
    far, near_x, near_y, own = sums
    passed = lax.ppermute(
        wire(far), "ctx", [(index, index ^ (2 if index % 2 == 0 else 4)) for index in range(count)]
    ).astype(jnp.float32)
    near_y = near_y + jnp.where(first_core, passed, 0.0)
    near_x = near_x + jnp.where(first_core, 0.0, passed)
    return (
        own
        + lax.ppermute(wire(near_x), "ctx", xor_pairs(count, 2)).astype(jnp.float32)
        + lax.ppermute(wire(near_y), "ctx", xor_pairs(count, 4)).astype(jnp.float32)
    )


def swap_all(parts, axis_name):
    count = lax.axis_size(axis_name)
    return [parts[0]] + [
        lax.ppermute(parts[k], axis_name, xor_pairs(count, k)) for k in range(1, count)
    ]


def natural(stacked, axis_name):
    count = lax.axis_size(axis_name)
    order = lax.axis_index(axis_name) ^ jnp.arange(count, dtype=jnp.int32)
    return jnp.take(stacked, order, axis=0, mode="clip")


def gather_wsh(values):
    count = lax.axis_size("wsh")
    return natural(jnp.stack(swap_all([values] * count, "wsh"), axis=0), "wsh")


def on_device_heads(
    block_input,
    out_cotangent,
    lengths,
    slot_block,
    norm_gains,
    short_filter,
    step_bias,
    log_rate,
    skip_gain,
    mixer_in,
    mixer_out,
    attend_in,
    attend_out,
    gate_up,
    down_weight,
):
    count = lax.axis_size("ctx")
    groups = lax.axis_size("wsh")
    ctx = lax.axis_index("ctx")
    wsh = lax.axis_index("wsh")
    rows, width = block_input.shape[1:]
    block_rows = rows // 2
    blocks = 2 * count
    total_rows = count * rows
    heads = MHEADS // count
    chans = heads * HEAD_M
    kv_width = KVH * HD
    kv_head = ctx * KVH // count
    units = gate_up.shape[2] // count
    scale = 1.0 / math.sqrt(HD)
    first_len = lengths[0, 0]
    tokens = block_input[0]
    cotangent = out_cotangent[0]
    cols = lambda array, start, size: lax.dynamic_slice_in_dim(array, start, size, array.ndim - 1)
    step_pad = -(chans * 2 + 2 * NSTATE + 3 * HD + heads) % 128

    in_cols = jnp.concatenate(
        [
            cols(mixer_in, ctx * chans, chans),
            cols(mixer_in, DSSM + ctx * chans, chans),
            mixer_in[:, 2 * DSSM : 2 * DSSM + 2 * NSTATE],
            cols(attend_in, ctx * HD, HD),
            cols(attend_in, AQ + kv_head * HD, HD),
            cols(attend_in, AQ + kv_width + kv_head * HD, HD),
            cols(mixer_in, DSSM + CONV + ctx * heads, heads),
            jnp.zeros((mixer_in.shape[0], step_pad), jnp.bfloat16),
        ],
        axis=1,
    )
    gains_all = gather_wsh(norm_gains)
    gains = jnp.transpose(gains_all, (1, 0, 2)).reshape(2, width).astype(jnp.float32)
    in_all = gather_wsh(in_cols).reshape(width, in_cols.shape[1])
    out_rows = jnp.concatenate(
        [
            lax.dynamic_slice_in_dim(mixer_out, ctx * chans, chans, 0),
            lax.dynamic_slice_in_dim(attend_out, ctx * HD, HD, 0),
        ],
        axis=0,
    )
    out_mine = jnp.transpose(gather_wsh(out_rows), (1, 0, 2)).reshape(chans + HD, width)
    out_all = gather_ctx(out_mine)
    mlp_cols = cols(gate_up, ctx * units, units)
    mlp_rows = lax.dynamic_slice_in_dim(down_weight, ctx * units, units, 0)
    mlp_parts = swap_all([mlp_cols] * groups, "wsh")
    down_all = jnp.concatenate(swap_all([mlp_rows] * groups, "wsh"), axis=0)
    gate_cols = jnp.concatenate([part[0] for part in mlp_parts], axis=1)
    up_cols = jnp.concatenate([part[1] for part in mlp_parts], axis=1)
    gate_up_cols = jnp.concatenate([gate_cols, up_cols], axis=1)

    peers = ctx ^ jnp.arange(count, dtype=jnp.int32)
    held = jnp.take(slot_block.reshape(count, 2), peers, axis=0, mode="clip").reshape(blocks)
    logical_ids = jnp.arange(blocks, dtype=jnp.int32)
    place = jnp.sum(
        jnp.where(held[None, :] == logical_ids[:, None], logical_ids[None, :], 0), axis=1
    )

    def to_logical(array):
        pieces = array.reshape((blocks, block_rows) + array.shape[2:])
        return jnp.take(pieces, place, axis=0, mode="clip").reshape(
            (total_rows,) + array.shape[2:]
        )

    def to_held(array):
        pieces = array.reshape((blocks, block_rows) + array.shape[1:])
        return jnp.take(pieces, held, axis=0, mode="clip").reshape(
            (count, rows) + array.shape[1:]
        )

    positions = jnp.arange(total_rows, dtype=jnp.int32)
    second = positions >= first_len
    seq_pos = positions - jnp.where(second, first_len, 0)

    first_scale = lax.rsqrt(jnp.mean(tokens * tokens, axis=-1, keepdims=True) + EPS)
    normed_first = to_logical(gather_ctx((tokens * first_scale * gains[0]).astype(jnp.bfloat16)))
    cot_b = cotangent.astype(jnp.bfloat16)
    cot_all = gather_ctx(cot_b).reshape(total_rows, width)
    projected = jnp.dot(normed_first, in_all, preferred_element_type=jnp.float32)
    edges = [chans, 2 * chans + 2 * NSTATE]
    edges += [edges[1] + HD, edges[1] + 2 * HD, edges[1] + 3 * HD, edges[1] + 3 * HD + heads]
    gate_z = projected[:, : edges[0]]
    conv_input = projected[:, edges[0] : edges[1]]
    step_raw = projected[:, edges[4] : edges[5]]

    filter_mine = jnp.concatenate(
        [cols(short_filter, ctx * chans, chans), short_filter[:, DSSM:]], axis=1
    )
    conv = filter_mine[KERNEL] + filter_mine[KERNEL - 1] * conv_input
    moved = []
    for shift in range(KERNEL - 1, 0, -1):
        shifted = jnp.concatenate(
            [jnp.zeros((shift, conv_input.shape[1]), jnp.float32), conv_input[:-shift]], axis=0
        )
        moved.append(jnp.where((seq_pos >= shift)[:, None], shifted, 0.0))
        conv = conv + filter_mine[KERNEL - 1 - shift] * moved[-1]
    activated = jax.nn.silu(conv)
    in_heads = lambda array: jnp.transpose(
        array.reshape(blocks, block_rows, heads, HEAD_M), (2, 0, 1, 3)
    )
    from_heads = lambda array: jnp.transpose(array, (1, 2, 0, 3)).reshape(total_rows, chans)
    heads_x = in_heads(activated[:, :chans])
    b_in = activated[:, chans : chans + NSTATE].reshape(blocks, block_rows, NSTATE)
    c_in = activated[:, chans + NSTATE :].reshape(blocks, block_rows, NSTATE)
    bias_mine = lax.dynamic_slice_in_dim(step_bias, ctx * heads, heads)
    rate_mine = jnp.exp(lax.dynamic_slice_in_dim(log_rate, ctx * heads, heads))
    skip_mine = lax.dynamic_slice_in_dim(skip_gain, ctx * heads, heads)
    step_in = jnp.transpose(step_raw).reshape(heads, blocks, block_rows) + bias_mine[:, None, None]
    step = jax.nn.softplus(step_in)
    log_decay = -step * rate_mine[:, None, None]

    ein = lambda spec, left, right: jnp.einsum(spec, left, right, precision=HIGH)
    lower = jnp.arange(block_rows)[:, None] >= jnp.arange(block_rows)[None, :]
    cumulative = ein("hbs,ts->hbt", log_decay, lower.astype(jnp.float32))
    totals = cumulative[:, :, -1]
    growth = jnp.exp(cumulative)
    tail = jnp.exp(totals[:, :, None] - cumulative)
    decays = jnp.where(
        lower,
        jnp.exp(jnp.where(lower, cumulative[..., :, None] - cumulative[..., None, :], 0.0)),
        0.0,
    )
    mixing = decays * ein("btn,bsn->bts", c_in, b_in)[None]
    fed = heads_x * step[..., None]
    emitted = ein("hbsp,bsn->hbpn", fed * tail[..., None], b_in)
    before = jnp.concatenate(
        [jnp.zeros((heads, 1), jnp.float32), jnp.cumsum(totals, axis=1)], axis=1
    )
    block_second = logical_ids * block_rows >= first_len
    earlier = (block_second[:, None] == block_second[None, :]) & (
        logical_ids[:, None] > logical_ids[None, :]
    )
    chain = jnp.where(
        earlier,
        jnp.exp(jnp.where(earlier, before[:, :-1, None] - before[:, None, 1:], 0.0)),
        0.0,
    )
    state_in = ein("hbj,hjpn->hbpn", chain, emitted)
    inner = ein("hbts,hbsp->hbtp", mixing, fed) + (
        ein("hbpn,btn->hbtp", state_in, c_in) * growth[..., None]
    )
    mixer_y = from_heads(inner + skip_mine[:, None, None, None] * heads_x)
    silu_z = jax.nn.silu(gate_z)
    gated = (mixer_y * silu_z).astype(jnp.bfloat16)

    half = HD // 2
    freqs = jnp.exp(jnp.arange(half, dtype=jnp.float32) * (-2.0 * math.log(ROPE_BASE) / HD))
    angles = seq_pos.astype(jnp.float32)[:, None] * freqs[None, :]
    cosines = jnp.cos(angles)
    sines = jnp.sin(angles)
    query = rotate(projected[:, edges[1] : edges[2]], cosines, sines).astype(jnp.bfloat16)
    key = rotate(projected[:, edges[2] : edges[3]], cosines, sines).astype(jnp.bfloat16)
    value = projected[:, edges[3] : edges[4]].astype(jnp.bfloat16)
    allowed = (positions[None, :] <= positions[:, None]) & (second[None, :] == second[:, None])
    scores = jnp.where(allowed, matmul_back(query, key) * scale, NEG_LARGE)
    top = jnp.max(scores, axis=-1, keepdims=True)
    weights = jnp.where(allowed, jnp.exp(scores - top), 0.0)
    denominator = jnp.sum(weights, axis=-1, keepdims=True)
    log_total = top + jnp.log(denominator)
    attn_rows = (
        jnp.dot(weights.astype(jnp.bfloat16), value, preferred_element_type=jnp.float32)
        / denominator
    )
    mixed_b = jnp.concatenate([gated, attn_rows.astype(jnp.bfloat16)], axis=1)

    mixed_held = to_held(mixed_b)
    mixed_mine = jnp.stack(swap_all(mixed_held, "ctx"), axis=0)
    hidden = tokens + jnp.einsum(
        "ktc,kcd->td", mixed_mine, out_all, preferred_element_type=jnp.float32
    )

    second_scale = lax.rsqrt(jnp.mean(hidden * hidden, axis=-1, keepdims=True) + EPS)
    unit_hidden = hidden * second_scale
    normed_second = gather_ctx((unit_hidden * gains[1]).astype(jnp.bfloat16)).reshape(
        total_rows, width
    )
    both = jnp.dot(normed_second, gate_up_cols, preferred_element_type=jnp.float32)
    gate_part = both[:, : groups * units]
    up_part = both[:, groups * units :]
    silu_gate = jax.nn.silu(gate_part)
    mlp_act = (silu_gate * up_part).astype(jnp.bfloat16)
    d_mlp = matmul_back(cot_all, down_all)
    d_gate = (d_mlp * up_part * silu_slope(gate_part)).astype(jnp.bfloat16)
    d_up = (d_mlp * silu_gate).astype(jnp.bfloat16)
    d_both = jnp.concatenate([d_gate, d_up], axis=1)
    d_normed_second = scatter_ctx(matmul_back(d_both, gate_up_cols).reshape(count, rows, width))
    mlp_out = scatter_ctx(
        jnp.dot(mlp_act, down_all, preferred_element_type=jnp.float32).reshape(count, rows, width)
    )
    output = hidden + mlp_out

    def norm_back(d_normed, gain, unit, unit_scale):
        scaled = d_normed * gain
        return unit_scale * (scaled - unit * jnp.mean(scaled * unit, axis=-1, keepdims=True))

    hidden_grad = cotangent + norm_back(d_normed_second, gains[1], unit_hidden, second_scale)
    hidden_b = to_logical(gather_ctx(hidden_grad.astype(jnp.bfloat16)))

    both_grad = matmul_t(normed_second, d_both)
    down_grad_t = matmul_t(cot_all, mlp_act)
    gain_second_grad = jnp.sum(both_grad * gate_up_cols.astype(jnp.float32), axis=1) / gains[1]
    mlp_grads = [
        jnp.concatenate(
            [
                both_grad[:, k * units : (k + 1) * units],
                both_grad[:, (groups + k) * units : (groups + k + 1) * units],
                down_grad_t[:, k * units : (k + 1) * units],
            ],
            axis=1,
        ).astype(jnp.bfloat16)
        for k in range(groups)
    ]
    mlp_sum = sum(piece.astype(jnp.float32) for piece in swap_all(mlp_grads, "wsh"))
    mlp_sum = jnp.take(
        mlp_sum.astype(jnp.bfloat16).reshape(count, width // count, 3 * units),
        peers,
        axis=0,
        mode="clip",
    )
    mlp_final = natural(jnp.stack(swap_all(mlp_sum, "ctx"), axis=0), "ctx").astype(jnp.float32)
    side_by_side = lambda array: jnp.transpose(array, (1, 0, 2)).reshape(array.shape[1], -1)
    gate_up_grad = jnp.stack(
        [side_by_side(mlp_final[:, :, :units]), side_by_side(mlp_final[:, :, units : 2 * units])],
        axis=0,
    )
    down_grad = jnp.transpose(mlp_final[:, :, 2 * units :], (0, 2, 1)).reshape(
        count * units, width // count
    )

    d_mixed_out = matmul_back(hidden_b, out_mine)
    out_grad_t = matmul_t(hidden_b, mixed_b)
    d_gated = d_mixed_out[:, :chans]
    d_attn = d_mixed_out[:, chans:].astype(jnp.bfloat16)

    delta = jnp.sum(d_attn.astype(jnp.float32) * attn_rows, axis=-1, keepdims=True)
    probs = jnp.where(allowed, jnp.exp(scores - log_total), 0.0)
    d_scores = (probs * (matmul_back(d_attn, value) - delta) * scale).astype(jnp.bfloat16)
    d_query = rotate(
        jnp.dot(d_scores, key, preferred_element_type=jnp.float32), cosines, -sines
    )
    d_key = rotate(matmul_t(d_scores, query), cosines, -sines)
    d_value = matmul_t(probs.astype(jnp.bfloat16), d_attn)

    d_z = d_gated * mixer_y * silu_slope(gate_z)
    d_y = in_heads(d_gated * silu_z)
    grown = d_y * growth[..., None]
    state_grad = ein("hbtp,btn->hbpn", grown, c_in)
    later = ein("hcb,hcpn->hbpn", chain, state_grad)
    fed_inner = ein("hbts,hbtp->hbsp", mixing, d_y)
    fed_emit = ein("hbpn,bsn->hbsp", later, b_in) * tail[..., None]
    d_fed = fed_inner + fed_emit
    d_kernel = jnp.sum(ein("hbtp,hbsp->hbts", d_y, fed) * decays, axis=0)
    d_c = ein("bts,bsn->btn", d_kernel, b_in) + ein("hbtp,hbpn->btn", grown, state_in)
    d_b = ein("bts,btn->bsn", d_kernel, c_in) + ein(
        "hbsp,hbpn->bsn", fed * tail[..., None], later
    )
    d_heads = d_fed * step[..., None] + skip_mine[:, None, None, None] * d_y
    skip_grad = jnp.sum(d_y * heads_x, axis=(1, 2, 3))
    d_cumulative = jnp.sum(d_y * inner - fed * d_fed, axis=-1)
    d_totals = jnp.exp(totals) * jnp.sum(later * state_in, axis=(2, 3)) + jnp.sum(
        fed * fed_emit, axis=(2, 3)
    )
    d_decay = ein("hbt,ts->hbs", d_cumulative, lower.astype(jnp.float32)) + d_totals[..., None]
    d_step = jnp.sum(d_fed * heads_x, axis=-1) - d_decay * rate_mine[:, None, None]
    log_rate_grad = jnp.sum(d_decay * log_decay, axis=(1, 2))
    d_step_raw = d_step * jax.nn.sigmoid(step_in)
    step_bias_grad = jnp.sum(d_step_raw, axis=(1, 2))

    d_activated = jnp.concatenate(
        [from_heads(d_heads), d_b.reshape(total_rows, NSTATE), d_c.reshape(total_rows, NSTATE)],
        axis=1,
    )
    d_conv = d_activated * silu_slope(conv)
    d_conv_input = filter_mine[KERNEL - 1] * d_conv
    filter_grads = []
    for index, shift in enumerate(range(KERNEL - 1, 0, -1)):
        masked = jnp.where((seq_pos >= shift)[:, None], d_conv, 0.0)
        back = jnp.concatenate(
            [masked[shift:], jnp.zeros((shift, masked.shape[1]), jnp.float32)], axis=0
        )
        d_conv_input = d_conv_input + filter_mine[index] * back
        filter_grads.append(jnp.sum(d_conv * moved[index], axis=0))
    filter_grads.append(jnp.sum(d_conv * conv_input, axis=0))
    filter_grads.append(jnp.sum(d_conv, axis=0))
    filter_part = jnp.stack(filter_grads, axis=0)

    step_cols = jnp.transpose(d_step_raw.reshape(heads, total_rows))
    d_all = jnp.concatenate(
        [
            d_z,
            d_conv_input,
            d_query,
            d_key,
            d_value,
            step_cols,
            jnp.zeros((total_rows, step_pad), jnp.float32),
        ],
        axis=1,
    ).astype(jnp.bfloat16)
    d_held = to_held(d_all).reshape(total_rows, d_all.shape[1])
    d_normed_first = scatter_ctx(matmul_back(d_held, in_all).reshape(count, rows, width))
    unit_tokens = tokens * first_scale
    input_grad = hidden_grad + norm_back(d_normed_first, gains[0], unit_tokens, first_scale)

    in_grad = matmul_t(normed_first, d_all)
    gain_first_grad = jnp.sum(in_grad * in_all.astype(jnp.float32), axis=1) / gains[0]
    all_grad = jnp.concatenate(
        [
            in_grad[:, : edges[5]],
            gain_first_grad[:, None],
            gain_second_grad[:, None],
            jnp.zeros((width, step_pad - 2), jnp.float32),
            out_grad_t,
        ],
        axis=1,
    ).astype(jnp.bfloat16)
    share = width // (count * groups)
    to_groups = jnp.transpose(
        all_grad.reshape(count, groups, share, all_grad.shape[1]), (1, 0, 2, 3)
    )
    to_groups = jnp.take(
        to_groups, wsh ^ jnp.arange(groups, dtype=jnp.int32), axis=0, mode="clip"
    )
    grad_sum = sum(piece.astype(jnp.float32) for piece in swap_all(to_groups, "wsh"))
    grad_sum = jnp.take(grad_sum.astype(jnp.bfloat16), peers, axis=0, mode="clip")
    final = natural(jnp.stack(swap_all(grad_sum, "ctx"), axis=0), "ctx").astype(jnp.float32)
    wide = edges[5] + step_pad
    per_kv = lambda array: side_by_side(
        jnp.sum(array.reshape(KVH, count // KVH, share, HD), axis=1)
    )
    mixer_in_grad = jnp.concatenate(
        [
            side_by_side(final[:, :, :chans]),
            side_by_side(final[:, :, chans : 2 * chans]),
            jnp.sum(final[:, :, 2 * chans : edges[1]], axis=0),
            side_by_side(final[:, :, edges[4] : edges[5]]),
        ],
        axis=1,
    )
    attend_in_grad = jnp.concatenate(
        [
            side_by_side(final[:, :, edges[1] : edges[2]]),
            per_kv(final[:, :, edges[2] : edges[3]]),
            per_kv(final[:, :, edges[3] : edges[4]]),
        ],
        axis=1,
    )
    gains_grad = jnp.transpose(jnp.sum(final[:, :, edges[5] : edges[5] + 2], axis=0))
    stacked = lambda array: jnp.transpose(array, (0, 2, 1)).reshape(-1, share)
    mixer_out_grad = stacked(final[:, :, wide : wide + chans])
    attend_out_grad = stacked(final[:, :, wide + chans :])

    small = jnp.concatenate(
        [filter_part.reshape(-1), step_bias_grad, log_rate_grad, skip_grad], axis=0
    )
    small = jnp.pad(small, (0, -small.shape[0] % 1024)).reshape(-1, 128)
    small = jnp.sum(gather_wsh(small), axis=0)
    small = natural(gather_ctx(small), "ctx").reshape(count, -1)
    filters = small[:, : filter_part.size].reshape((count,) + filter_part.shape)
    filter_grad = jnp.concatenate(
        [side_by_side(filters[:, :, :chans]), jnp.sum(filters[:, :, chans:], axis=0)], axis=1
    )
    per_head = small[:, filter_part.size : filter_part.size + 3 * heads].reshape(count, 3, heads)
    step_bias_all, log_rate_all, skip_all = [per_head[:, i].reshape(-1) for i in range(3)]
    return (
        output[None],
        input_grad[None],
        gains_grad,
        filter_grad,
        step_bias_all,
        log_rate_all,
        skip_all,
        mixer_in_grad,
        mixer_out_grad,
        attend_in_grad,
        attend_out_grad,
        gate_up_grad,
        down_grad,
    )


def solution(mesh):
    placed = (
        P("wsh", "ctx", None),
        P("wsh", "ctx", None),
        P("wsh", None),
        P(),
        P(None, "wsh"),
        P(),
        P(),
        P(),
        P(),
        P("wsh", None),
        P(None, "wsh"),
        P("wsh", None),
        P(None, "wsh"),
        P(None, None, "wsh"),
        P("wsh", None),
    )
    per_heads = mesh.shape["ctx"] == QH
    return jax.shard_map(
        on_device_heads if per_heads else on_device,
        mesh=mesh,
        in_specs=placed,
        out_specs=(
            P("wsh", "ctx", None),
            P("wsh", "ctx", None),
            P(None, ("ctx", "wsh")),
            P(),
            P(),
            P(),
            P(),
            P(("ctx", "wsh"), None),
            P(None, ("ctx", "wsh")),
            P(("ctx", "wsh"), None),
            P(None, ("ctx", "wsh")),
            P(None, "ctx", "wsh"),
            P("wsh", "ctx"),
        ),
        check_vma=False,
    )
```

```python
import math
from functools import partial

import jax
import jax.numpy as jnp
from jax import lax
from jax.experimental import pallas as pl
from jax.experimental.pallas import tpu as pltpu
from jax.sharding import PartitionSpec as P

MHEADS = 24
HEAD_M = 64
NSTATE = 128
QH = 8
KVH = 2
HD = 64
KERNEL = 4
DSSM = 1536
CONV = 1792
AQ = 512
GRP = 4


EPS = 1e-05
ROPE_BASE = 100000000000.0
HIGH = lax.Precision.HIGHEST
SSD = HIGH
NEG_LARGE = -1e30


def rms_norm(values, gain):
    scale = lax.rsqrt(jnp.mean(values * values, axis=-1, keepdims=True) + EPS)
    return values * scale * gain


def silu_slope(values):
    sigmoid_value = jax.nn.sigmoid(values)
    return sigmoid_value * (1.0 + values * (1.0 - sigmoid_value))


def rope_tables(positions):
    half = HD // 2
    freqs = jnp.exp(jnp.arange(half, dtype=jnp.float32) * (-2.0 * math.log(ROPE_BASE) / HD))
    angles = positions.astype(jnp.float32)[:, None] * freqs[None, :]
    return (jnp.cos(angles)[:, None, :], jnp.sin(angles)[:, None, :])


def rotate(values, cosines, sines):
    half = values.shape[-1] // 2
    first = values[..., :half]
    second = values[..., half:]
    return jnp.concatenate(
        [first * cosines - second * sines, second * cosines + first * sines], axis=-1
    )


def matmul_t(left, right):
    return lax.dot_general(
        left, right, (((0,), (0,)), ((), ())), preferred_element_type=jnp.float32
    )


def matmul_back(left, right):
    return lax.dot_general(
        left, right, (((1,), (1,)), ((), ())), preferred_element_type=jnp.float32
    )


def step_prep(step_raw, step_bias, log_rate):
    step = jax.nn.softplus(step_raw + step_bias)
    return (step, -step * jnp.exp(log_rate))


def conv_prep(conv_blocks, tails_in, filter_rows):
    count = conv_blocks.shape[1]
    extended = jnp.concatenate([tails_in, conv_blocks], axis=1)
    conv = filter_rows[KERNEL] + filter_rows[KERNEL - 1] * conv_blocks
    for tap_index in range(KERNEL - 1):
        conv = conv + filter_rows[tap_index] * extended[:, tap_index : tap_index + count]
    return jax.nn.silu(conv)


def ssd_emit(heads_x, b_in, step, log_decay):
    cumulative = jnp.cumsum(log_decay, axis=0)
    weight = jnp.exp(cumulative[-1][None, :] - cumulative) * step
    emitted = jnp.einsum("shp,sn->hpn", heads_x * weight[:, :, None], b_in, precision=HIGH)
    return (emitted, cumulative[-1])


def ssd_output(heads_x, b_in, c_in, step, log_decay, state_in, skip_gain):
    cumulative = jnp.cumsum(log_decay, axis=0)
    count = heads_x.shape[0]
    lower = (jnp.arange(count)[:, None] >= jnp.arange(count)[None, :])[:, :, None]
    gaps = jnp.where(lower, cumulative[:, None, :] - cumulative[None, :, :], 0.0)
    kernel = (
        jnp.where(lower, jnp.exp(gaps), 0.0) * jnp.dot(c_in, b_in.T, precision=HIGH)[:, :, None]
    )
    inner = jnp.einsum("tsh,shp->thp", kernel, heads_x * step[:, :, None], precision=HIGH)
    carried = (
        jnp.einsum("hpn,tn->thp", state_in, c_in, precision=HIGH) * jnp.exp(cumulative)[:, :, None]
    )
    return inner + carried + skip_gain[None, :, None] * heads_x


def chain_fold(slot_block, my_blocks, block_second, first_len, block_rows, prefix, later):

    def fold(total, piece, start):
        count = piece.shape[0]
        same = (slot_block * block_rows >= first_len)[None, :] == block_second[:, None]
        if later:
            valid = same & (slot_block[None, :] > my_blocks[:, None])
            gaps = (
                jnp.take(prefix, slot_block, axis=0)[None, :, :]
                - jnp.take(prefix, my_blocks + 1, axis=0)[:, None, :]
            )
        else:
            valid = same & (slot_block[None, :] < my_blocks[:, None])
            gaps = (
                jnp.take(prefix, my_blocks, axis=0)[:, None, :]
                - jnp.take(prefix, slot_block + 1, axis=0)[None, :, :]
            )
        factors = jnp.where(
            valid[:, :, None], jnp.exp(jnp.where(valid[:, :, None], gaps, 0.0)), 0.0
        )
        step_size = math.gcd(count, 8)

        def add_rows(index, running):
            rows_piece = lax.dynamic_slice_in_dim(piece, index * step_size, step_size).astype(
                jnp.float32
            )
            factor_rows = lax.dynamic_slice_in_dim(factors, index * step_size, step_size, 1)
            return running + jnp.einsum("bsh,shpn->bhpn", factor_rows, rows_piece, precision=HIGH)

        return lax.fori_loop(0, count // step_size, add_rows, total)

    return fold


def in_blocks(step_fn, carry, piece):
    count = piece.shape[0]
    block_size = math.gcd(count, 512)

    def visit(block_index, state):
        sub_piece = lax.dynamic_slice_in_dim(piece, block_index * block_size, block_size)
        return step_fn(state, sub_piece, block_index * block_size)

    return lax.fori_loop(0, count // block_size, visit, carry)


def on_device(
    block_input,
    out_cotangent,
    lengths,
    slot_block,
    norm_gains,
    short_filter,
    step_bias,
    log_rate,
    skip_gain,
    mixer_in,
    mixer_out,
    attend_in,
    attend_out,
    gate_up,
    down_weight,
):
    gains_all, in_mix, out_mix, in_attend, out_attend = (
        lax.all_gather(norm_gains, "wsh", axis=1, tiled=True),
        lax.all_gather(mixer_in, "wsh", axis=0, tiled=True),
        lax.all_gather(mixer_out, "wsh", axis=1, tiled=True),
        lax.all_gather(attend_in, "wsh", axis=0, tiled=True),
        lax.all_gather(attend_out, "wsh", axis=1, tiled=True),
    )
    ctx_count = lax.axis_size("ctx")
    block_count = 2 * ctx_count
    rows = block_input.shape[1]
    block_rows = rows // 2
    kv_width = KVH * HD
    scale = 1.0 / math.sqrt(HD)
    tokens = block_input[0]
    cotangent = out_cotangent[0]
    first_len = lengths[0, 0]
    logical_ids = jnp.arange(block_count, dtype=jnp.int32)
    my_blocks = lax.dynamic_slice_in_dim(slot_block, 2 * lax.axis_index("ctx"), 2)
    block_offsets = jnp.arange(block_rows, dtype=jnp.int32)
    my_pos = (my_blocks[:, None] * block_rows + block_offsets[None, :]).reshape(rows)
    my_second = my_pos >= first_len
    seq_pos = my_pos - jnp.where(my_second, first_len, 0)
    block_second = my_blocks * block_rows >= first_len
    is_start = (my_blocks == 0) | (my_blocks * block_rows == first_len)
    key_pos = (slot_block[:, None] * block_rows + block_offsets[None, :]).reshape(
        block_count * block_rows
    )
    gain_first = gains_all[0].astype(jnp.float32)
    gain_second = gains_all[1].astype(jnp.float32)
    normed, first_norm_vjp = jax.vjp(rms_norm, tokens, gain_first)
    normed_first = normed.astype(jnp.bfloat16)
    mixed = jnp.dot(normed_first, in_mix, preferred_element_type=jnp.float32)
    gate_z = mixed[:, :DSSM]
    conv_input = mixed[:, DSSM : DSSM + CONV]
    step_raw = mixed[:, DSSM + CONV :]
    (step, log_decay), step_vjp = jax.vjp(step_prep, step_raw, step_bias, log_rate)
    step_blocks = step.reshape(2, block_rows, MHEADS)
    decay_blocks = log_decay.reshape(2, block_rows, MHEADS)
    totals = jnp.sum(decay_blocks, axis=1)
    conv_blocks = conv_input.reshape(2, block_rows, CONV)
    tails = conv_blocks[:, block_rows - (KERNEL - 1) :, :]
    all_tails, all_totals = (
        lax.all_gather(tails, "ctx", axis=0, tiled=True),
        lax.all_gather(totals, "ctx", axis=0, tiled=True),
    )
    one_hot = (slot_block[None, :] == logical_ids[:, None]).astype(jnp.float32)
    totals_logical = jnp.dot(one_hot, all_totals, precision=HIGH)
    prefix = jnp.concatenate(
        [jnp.zeros((1, MHEADS), jnp.float32), jnp.cumsum(totals_logical, axis=0)], axis=0
    )
    pred_slot = jnp.sum(
        jnp.where(slot_block[None, :] == (my_blocks - 1)[:, None], logical_ids[None, :], 0), axis=1
    )
    keep_tail = jnp.where(is_start, 0.0, 1.0).astype(jnp.float32)
    tails_in = jnp.take(all_tails, pred_slot, axis=0) * keep_tail[:, None, None]
    activated, conv_vjp = jax.vjp(conv_prep, conv_blocks, tails_in, short_filter)
    heads_x = activated[:, :, :DSSM].reshape(2, block_rows, MHEADS, HEAD_M)
    b_in = activated[:, :, DSSM : DSSM + NSTATE]
    c_in = activated[:, :, DSSM + NSTATE :]
    (emitted, emit_totals), emit_vjp = jax.vjp(
        jax.vmap(ssd_emit), heads_x, b_in, step_blocks, decay_blocks
    )
    zero_states = jnp.zeros((2, MHEADS, HEAD_M, NSTATE), jnp.float32)
    chain_forward = chain_fold(
        slot_block, my_blocks, block_second, first_len, block_rows, prefix, False
    )
    state_in = chain_forward(
        zero_states,
        lax.all_gather(emitted.astype(jnp.bfloat16), "ctx", axis=0, tiled=True),
        jnp.int32(0),
    )
    mixer_y, out_vjp = jax.vjp(
        jax.vmap(ssd_output, in_axes=(0, 0, 0, 0, 0, 0, None)),
        heads_x,
        b_in,
        c_in,
        step_blocks,
        decay_blocks,
        state_in,
        skip_gain,
    )
    mixer_flat = mixer_y.reshape(rows, DSSM)
    gated = (mixer_flat * jax.nn.silu(gate_z)).astype(jnp.bfloat16)
    mixer_branch = jnp.dot(gated, out_mix, preferred_element_type=jnp.float32)
    projected = jnp.dot(normed_first, in_attend, preferred_element_type=jnp.float32)
    cosines, sines = rope_tables(seq_pos)
    queries = rotate(projected[:, :AQ].reshape(rows, QH, HD), cosines, sines).astype(jnp.bfloat16)
    keys_rot = rotate(
        projected[:, AQ : AQ + kv_width].reshape(rows, KVH, HD), cosines, sines
    ).astype(jnp.bfloat16)
    values = projected[:, AQ + kv_width :].astype(jnp.bfloat16)
    kv_local = jnp.concatenate([keys_rot.reshape(rows, kv_width), values], axis=1)
    query_heads = queries.reshape(rows, KVH, GRP, HD)

    def allowed_at(start, count):
        piece_pos = lax.dynamic_slice_in_dim(key_pos, start, count)
        return (piece_pos[None, :] <= my_pos[:, None]) & (
            (piece_pos >= first_len)[None, :] == my_second[:, None]
        )

    def split_piece(piece):
        count = piece.shape[0]
        return (
            piece[:, :kv_width].reshape(count, KVH, HD),
            piece[:, kv_width:].reshape(count, KVH, HD),
        )

    def attend_step(carry, piece, start):
        top, denominator, running = carry
        keys_piece, values_piece = split_piece(piece)
        allowed = allowed_at(start, piece.shape[0])
        scores = (
            jnp.einsum(
                "tkgd,skd->kgts", query_heads, keys_piece, preferred_element_type=jnp.float32
            )
            * scale
        )
        masked = jnp.where(allowed, scores, NEG_LARGE)
        new_top = jnp.maximum(top, jnp.max(masked, axis=-1))
        weights = jnp.where(allowed, jnp.exp(masked - new_top[..., None]), 0.0)
        factor = jnp.exp(top - new_top)
        denominator = denominator * factor + jnp.sum(weights, axis=-1)
        running = running * factor[..., None] + jnp.einsum(
            "kgts,skd->kgtd", weights, values_piece.astype(jnp.float32), precision=HIGH
        )
        return (new_top, denominator, running)

    start_carry = (
        jnp.full((KVH, GRP, rows), NEG_LARGE, jnp.float32),
        jnp.zeros((KVH, GRP, rows), jnp.float32),
        jnp.zeros((KVH, GRP, rows, HD), jnp.float32),
    )
    top, denominator, running = in_blocks(
        attend_step, start_carry, lax.all_gather(kv_local, "ctx", axis=0, tiled=True)
    )
    log_total = top + jnp.log(denominator)
    attn_heads = running / denominator[..., None]
    attn_rows = jnp.transpose(attn_heads, (2, 0, 1, 3)).reshape(rows, AQ)
    attn_b = attn_rows.astype(jnp.bfloat16)
    attn_branch = jnp.dot(attn_b, out_attend, preferred_element_type=jnp.float32)
    hidden = tokens + mixer_branch + attn_branch
    normed2, second_norm_vjp = jax.vjp(rms_norm, hidden, gain_second)
    normed_second = normed2.astype(jnp.bfloat16)
    cot_b = cotangent.astype(jnp.bfloat16)
    gate_whole, down_rows = (
        lax.all_gather(gate_up, "wsh", axis=2, tiled=True),
        lax.all_gather(down_weight, "wsh", axis=0, tiled=True),
    )
    gate_cols = gate_whole[0]
    up_cols = gate_whole[1]
    gate_part = jnp.dot(normed_second, gate_cols, preferred_element_type=jnp.float32)
    up_part = jnp.dot(normed_second, up_cols, preferred_element_type=jnp.float32)
    mlp_act = (jax.nn.silu(gate_part) * up_part).astype(jnp.bfloat16)
    mlp_out = jnp.dot(mlp_act, down_rows, preferred_element_type=jnp.float32)
    output = hidden + mlp_out
    down_local = matmul_t(mlp_act, cot_b)
    d_mlp = matmul_back(cot_b, down_rows)
    d_gate = (d_mlp * up_part * silu_slope(gate_part)).astype(jnp.bfloat16)
    d_up = (d_mlp * jax.nn.silu(gate_part)).astype(jnp.bfloat16)
    gate_up_local = jnp.stack(
        [matmul_t(normed_second, d_gate), matmul_t(normed_second, d_up)], axis=0
    )
    d_normed_second = matmul_back(d_gate, gate_cols) + matmul_back(d_up, up_cols)
    d_hidden_norm, d_gain_second = second_norm_vjp(d_normed_second)
    hidden_grad = cotangent + d_hidden_norm
    hidden_b = hidden_grad.astype(jnp.bfloat16)
    attend_out_grad = matmul_t(attn_b, hidden_b)
    mixer_out_grad = matmul_t(gated, hidden_b)
    d_attn_b = matmul_back(hidden_b, out_attend).astype(jnp.bfloat16)
    d_gated = matmul_back(hidden_b, out_mix)
    d_heads = d_attn_b.reshape(rows, KVH, GRP, HD)
    d_heads_f = d_heads.astype(jnp.float32)
    query_f = queries.astype(jnp.float32).reshape(rows, KVH, GRP, HD)
    delta = jnp.sum(jnp.transpose(d_heads_f, (1, 2, 0, 3)) * attn_heads, axis=-1)

    def attend_back(carry, piece, start):
        query_grad, kv_grad = carry
        count = piece.shape[0]
        keys_piece, values_piece = split_piece(piece)
        allowed = allowed_at(start, count)
        scores = (
            jnp.einsum(
                "tkgd,skd->kgts", query_heads, keys_piece, preferred_element_type=jnp.float32
            )
            * scale
        )
        probs = jnp.where(
            allowed, jnp.exp(jnp.where(allowed, scores, 0.0) - log_total[..., None]), 0.0
        )
        d_probs = jnp.einsum(
            "tkgd,skd->kgts", d_heads, values_piece, preferred_element_type=jnp.float32
        )
        d_scores = probs * (d_probs - delta[..., None]) * scale
        query_grad = query_grad + jnp.einsum(
            "kgts,skd->tkgd", d_scores, keys_piece.astype(jnp.float32), precision=HIGH
        )
        key_grad = jnp.einsum("kgts,tkgd->skd", d_scores, query_f, precision=HIGH)
        value_grad = jnp.einsum("kgts,tkgd->skd", probs, d_heads_f, precision=HIGH)
        update = jnp.concatenate(
            [key_grad.reshape(count, kv_width), value_grad.reshape(count, kv_width)], axis=1
        )
        kv_grad = lax.dynamic_update_slice_in_dim(kv_grad, update, start, 0)
        return (query_grad, kv_grad)

    back_carry = (
        jnp.zeros((rows, KVH, GRP, HD), jnp.float32),
        jnp.zeros((block_count * block_rows, 2 * kv_width), jnp.float32),
    )
    query_grad, kv_grad = in_blocks(
        attend_back, back_carry, lax.all_gather(kv_local, "ctx", axis=0, tiled=True)
    )
    d_mixer = (d_gated * jax.nn.silu(gate_z)).reshape(2, block_rows, MHEADS, HEAD_M)
    d_z = d_gated * mixer_flat * silu_slope(gate_z)
    g_heads, g_b, g_c, g_step, g_decay, g_state, g_skip = out_vjp(d_mixer)
    chain_backward = chain_fold(
        slot_block, my_blocks, block_second, first_len, block_rows, prefix, True
    )
    later_sum = chain_backward(
        zero_states,
        lax.all_gather(g_state.astype(jnp.bfloat16), "ctx", axis=0, tiled=True),
        jnp.int32(0),
    )
    d_totals = jnp.exp(emit_totals) * jnp.sum(later_sum * state_in, axis=(2, 3))
    e_heads, e_b, e_step, e_decay = emit_vjp((later_sum, d_totals))
    d_activated = jnp.concatenate(
        [(g_heads + e_heads).reshape(2, block_rows, DSSM), g_b + e_b, g_c], axis=2
    )
    d_conv_blocks, d_tails, filter_grad = conv_vjp(d_activated)
    tail_buffer = (
        jnp.zeros((block_count, KERNEL - 1, CONV), jnp.float32)
        .at[pred_slot]
        .add(d_tails * keep_tail[:, None, None])
    )
    d_step_raw, step_bias_grad, log_rate_grad = step_vjp(
        ((g_step + e_step).reshape(rows, MHEADS), (g_decay + e_decay).reshape(rows, MHEADS))
    )
    kv_mine, tail_back, gate_up_part, down_part = (
        lax.psum_scatter(
            kv_grad.astype(jnp.bfloat16), "ctx", scatter_dimension=0, tiled=True
        ).astype(jnp.float32),
        lax.psum_scatter(
            tail_buffer.astype(jnp.bfloat16), "ctx", scatter_dimension=0, tiled=True
        ).astype(jnp.float32),
        lax.psum_scatter(
            gate_up_local.astype(jnp.bfloat16), "ctx", scatter_dimension=1, tiled=True
        ).astype(jnp.float32),
        lax.psum_scatter(
            down_local.astype(jnp.bfloat16), "ctx", scatter_dimension=1, tiled=True
        ).astype(jnp.float32),
    )
    d_query = rotate(query_grad.reshape(rows, QH, HD), cosines, -sines).reshape(rows, AQ)
    d_key = rotate(kv_mine[:, :kv_width].reshape(rows, KVH, HD), cosines, -sines).reshape(
        rows, kv_width
    )
    d_attend = jnp.concatenate([d_query, d_key, kv_mine[:, kv_width:]], axis=1).astype(jnp.bfloat16)
    attend_in_grad = matmul_t(normed_first, d_attend)
    d_normed_attend = matmul_back(d_attend, in_attend)
    d_conv_blocks = d_conv_blocks.at[:, block_rows - (KERNEL - 1) :, :].add(tail_back)
    d_mixed = jnp.concatenate([d_z, d_conv_blocks.reshape(rows, CONV), d_step_raw], axis=1).astype(
        jnp.bfloat16
    )
    mixer_in_grad = matmul_t(normed_first, d_mixed)
    d_normed_mix = matmul_back(d_mixed, in_mix)
    d_tokens_norm, d_gain_first = first_norm_vjp(d_normed_mix + d_normed_attend)
    input_grad = hidden_grad + d_tokens_norm
    gains_grad = jnp.stack([d_gain_first, d_gain_second], axis=0)
    step_bias_grad, log_rate_grad, skip_grad, filter_grad = lax.psum(
        (step_bias_grad, log_rate_grad, g_skip, filter_grad), ("ctx", "wsh")
    )
    gate_up_grad, down_grad = (
        lax.psum_scatter(
            gate_up_part.astype(jnp.bfloat16), "wsh", scatter_dimension=2, tiled=True
        ).astype(jnp.float32),
        lax.psum_scatter(
            down_part.astype(jnp.bfloat16), "wsh", scatter_dimension=0, tiled=True
        ).astype(jnp.float32),
    )
    results = (
        lax.psum_scatter(gains_grad, ("ctx", "wsh"), scatter_dimension=1, tiled=True),
        lax.psum_scatter(mixer_in_grad, ("ctx", "wsh"), scatter_dimension=0, tiled=True),
        lax.psum_scatter(mixer_out_grad, ("ctx", "wsh"), scatter_dimension=1, tiled=True),
        lax.psum_scatter(attend_in_grad, ("ctx", "wsh"), scatter_dimension=0, tiled=True),
        lax.psum_scatter(attend_out_grad, ("ctx", "wsh"), scatter_dimension=1, tiled=True),
    )
    return (
        output[None],
        input_grad[None],
        results[0],
        filter_grad,
        step_bias_grad,
        log_rate_grad,
        skip_grad,
        results[1],
        results[2],
        results[3],
        results[4],
        gate_up_grad,
        down_grad,
    )


def xor_pairs(count, bits):
    return [(index, index ^ bits) for index in range(count)]


def held_order(count):
    return list(range(0, count, 2)) + list(range(1, count, 2))


def gather_ctx(values):
    count = lax.axis_size("ctx")
    first_core = lax.axis_index("ctx") % 2 == 0
    near_x = lax.ppermute(values, "ctx", xor_pairs(count, 2))
    near_y = lax.ppermute(values, "ctx", xor_pairs(count, 4))
    far = lax.ppermute(
        jnp.where(first_core, near_x, near_y),
        "ctx",
        [(index, index ^ (4 if index % 2 == 0 else 2)) for index in range(count)],
    )
    mine = jnp.stack([values, near_x, near_y, far], axis=0)
    other = lax.ppermute(mine, "ctx", xor_pairs(count, 1))
    return jnp.concatenate([mine, other], axis=0)


def scatter_ctx(parts):
    count = lax.axis_size("ctx")
    half = count // 2
    first_core = lax.axis_index("ctx") % 2 == 0
    wire = lambda piece: piece.astype(jnp.bfloat16)
    sums = parts[:half] + lax.ppermute(
        wire(parts[half:]), "ctx", xor_pairs(count, 1)
    ).astype(jnp.float32)
    own, near_x, near_y, far = [sums[place] for place in range(half)]
    passed = lax.ppermute(
        wire(far), "ctx", [(index, index ^ (2 if index % 2 == 0 else 4)) for index in range(count)]
    ).astype(jnp.float32)
    near_y = near_y + jnp.where(first_core, passed, 0.0)
    near_x = near_x + jnp.where(first_core, 0.0, passed)
    return (
        own
        + lax.ppermute(wire(near_x), "ctx", xor_pairs(count, 2)).astype(jnp.float32)
        + lax.ppermute(wire(near_y), "ctx", xor_pairs(count, 4)).astype(jnp.float32)
    )


def trade_ctx(parts):
    return lax.all_to_all(parts, "ctx", 0, 0, tiled=True)


def after(values, anchor):
    return lax.optimization_barrier((values, anchor))[0]


def swap_groups(pieces):
    count = lax.axis_size("wsh")
    return [pieces[0]] + [
        lax.ppermute(pieces[k], "wsh", xor_pairs(count, k)) for k in range(1, count)
    ]


def gather_wsh(values, axis=0):
    count = lax.axis_size("wsh")
    shape = list(values.shape)
    size = shape[axis]
    shape[axis] = size * count
    whole = jnp.zeros(shape, values.dtype)
    for k, piece in enumerate(swap_groups([values] * count)):
        start = (lax.axis_index("wsh") ^ k) * size
        whole = lax.dynamic_update_slice_in_dim(whole, piece, start, axis)
    return whole


def dot_dims(left, right, left_dim, right_dim, precision=None):
    return lax.dot_general(
        left,
        right,
        (((left_dim,), (right_dim,)), ((), ())),
        precision=precision,
        preferred_element_type=jnp.float32,
    )


def spread(per_head, heads, lanes):
    return jnp.concatenate(
        [jnp.broadcast_to(item, (item.shape[0], lanes)) for item in per_head[:heads]], axis=1
    )


def turn(values, table, back=False):
    half = HD // 2
    swapped = jnp.concatenate([values[:, half:], values[:, :half]], axis=1)
    side = swapped * table[:, HD:]
    return values * table[:, :HD] - side if back else values * table[:, :HD] + side


def filtered(ext_ref, filt_ref, rows):
    conv = filt_ref[KERNEL : KERNEL + 1, :] + filt_ref[KERNEL - 1 : KERNEL, :] * ext_ref[8:, :]
    for tap in range(KERNEL - 1):
        start = 8 - (KERNEL - 1) + tap
        conv = conv + filt_ref[tap : tap + 1, :] * ext_ref[start : start + rows, :]
    return conv


def softplus(values):
    return jnp.maximum(values, 0.0) + jnp.log1p(jnp.exp(-jnp.abs(values)))


def block_decay(step_in, rate, rows):
    step = softplus(step_in)
    decay = -step * rate
    lower = lax.broadcasted_iota(jnp.int32, (rows, rows), 0) >= lax.broadcasted_iota(
        jnp.int32, (rows, rows), 1
    )
    ones = jnp.where(lower, 1.0, 0.0)
    cum = dot_dims(ones, decay, 1, 0, HIGH)
    cum_t = dot_dims(decay, ones, 0, 1, HIGH)
    return step, decay, lower, ones, cum, cum_t


def pick_kernel(heads, where_ref, *refs):
    xs, zs = refs[:heads], refs[heads : 2 * heads]
    bc0, step0, q0, k0, v0, gain_ref, out_ref = refs[2 * heads :]
    chans = heads * HEAD_M
    ctx = where_ref[0]
    gain = gain_ref[0:1, :].astype(jnp.float32)
    width = gain.shape[1]

    def put(start, values):
        scaled = values.astype(jnp.float32) * gain
        out_ref[start : start + values.shape[0], :] = scaled.astype(jnp.bfloat16)

    def half_tile(ref, odd):
        window = jnp.transpose(ref[...].astype(jnp.float32))
        return jnp.where(odd, window[HD:, :], window[:HD, :])

    for h in range(heads):
        put(h * HEAD_M, xs[h][...])
        put(256 + h * HEAD_M, zs[h][...])
    put(chans, half_tile(q0, ctx % 2 == 1))
    put(256 + chans, half_tile(k0, where_ref[1] % 2 == 1))
    put(512, bc0[...])
    put(768, half_tile(v0, where_ref[1] % 2 == 1))
    row = lax.broadcasted_iota(jnp.int32, (HEAD_M, width), 0)
    steps = jnp.where(row < MHEADS, step0[...].astype(jnp.float32), 0.0).astype(jnp.bfloat16)
    there = lax.broadcasted_iota(jnp.int32, (HEAD_M, HEAD_M), 0)
    here = lax.broadcasted_iota(jnp.int32, (HEAD_M, HEAD_M), 1)
    chosen = jnp.where((here == there + ctx * heads) & (there < heads), 1.0, 0.0)
    put(768 + HD, dot_dims(chosen.astype(jnp.bfloat16), steps, 1, 0))


def pick_columns(where, mixer_in, attend_in, gains, heads):
    width = mixer_in.shape[0]
    turned = jnp.transpose(mixer_in)
    rows_at = lambda start: pl.BlockSpec((HEAD_M, width), lambda i, s: (start(s) // HEAD_M, 0))
    tile_at = lambda start: pl.BlockSpec((width, 128), lambda i, s: (0, start(s) // 128))
    from_x = [rows_at(lambda s, h=h: DSSM + (s[0] * heads + h) * HEAD_M) for h in range(heads)]
    from_z = [rows_at(lambda s, h=h: (s[0] * heads + h) * HEAD_M) for h in range(heads)]
    return pl.pallas_call(
        partial(pick_kernel, heads),
        out_shape=jax.ShapeDtypeStruct((896, width), jnp.bfloat16),
        grid_spec=pltpu.PrefetchScalarGridSpec(
            num_scalar_prefetch=1,
            grid=(1,),
            in_specs=from_x
            + from_z
            + [
                pl.BlockSpec((2 * NSTATE, width), lambda i, s: (DSSM // NSTATE, 0)),
                rows_at(lambda s: DSSM + CONV),
                tile_at(lambda s: s[0] * HD),
                tile_at(lambda s: AQ + s[1] * HD),
                tile_at(lambda s: AQ + KVH * HD + s[1] * HD),
                pl.BlockSpec(gains.shape, lambda i, s: (0, 0)),
            ],
            out_specs=pl.BlockSpec((896, width), lambda i, s: (0, 0)),
        ),
        name="pick_columns",
    )(where, *[turned] * (2 * heads + 2), *[attend_in] * 3, gains)


def finish_in_kernel(heads, final_ref, mixer_ref, attend_ref, last_ref):
    count = final_ref.shape[0]
    chans = heads * HEAD_M
    share = final_ref.shape[1]
    parts = [final_ref[c].astype(jnp.float32) for c in range(count)]
    beside = lambda start, size: jnp.concatenate([p[:, start : start + size] for p in parts], axis=1)
    mixer_ref[:, :DSSM] = beside(256, chans)
    mixer_ref[:, DSSM : 2 * DSSM] = beside(0, chans)
    mixer_ref[:, 2 * DSSM : 2 * DSSM + 2 * NSTATE] = sum(p[:, 512:768] for p in parts)
    lane = lax.broadcasted_iota(jnp.int32, (128, MHEADS), 0)
    head = lax.broadcasted_iota(jnp.int32, (128, MHEADS), 1)
    steps = jnp.zeros((share, MHEADS), jnp.float32)
    for c in range(count):
        chosen = jnp.where((lane - HD == head - c * heads) & (lane >= HD) & (lane < HD + heads), 1.0, 0.0)
        steps = steps + dot_dims(final_ref[c, :, 768:896], chosen.astype(jnp.bfloat16), 1, 0)
    mixer_ref[:, DSSM + CONV :] = steps
    attend_ref[:, :AQ] = beside(chans, HD)
    each = count // KVH
    for start, place in ((256 + chans, AQ), (768, AQ + KVH * HD)):
        attend_ref[:, place : place + KVH * HD] = jnp.concatenate(
            [
                sum(p[:, start : start + HD] for p in parts[head_ * each : (head_ + 1) * each])
                for head_ in range(KVH)
            ],
            axis=1,
        )
    last_ref[...] = sum(p[:, 768:896] for p in parts)


def finish_in(final, heads):
    share = final.shape[1]
    return pl.pallas_call(
        partial(finish_in_kernel, heads),
        out_shape=(
            jax.ShapeDtypeStruct((share, DSSM + CONV + MHEADS), jnp.float32),
            jax.ShapeDtypeStruct((share, AQ + 2 * KVH * HD), jnp.float32),
            jax.ShapeDtypeStruct((share, 128), jnp.float32),
        ),
        name="finish_in",
    )(final)


def finish_rest_kernel(chans, mlp_ref, out_ref, gate_up_ref, down_ref, mixer_ref, attend_ref):
    count = mlp_ref.shape[0]
    units = mlp_ref.shape[2] // 3
    parts = [mlp_ref[c].astype(jnp.float32) for c in range(count)]
    gate_up_ref[0] = jnp.concatenate([p[:, :units] for p in parts], axis=1)
    gate_up_ref[1] = jnp.concatenate([p[:, units : 2 * units] for p in parts], axis=1)
    for c in range(count):
        down_ref[c * units : (c + 1) * units, :] = jnp.transpose(parts[c][:, 2 * units :])
    outs = [out_ref[c].astype(jnp.float32) for c in range(count)]
    mixer_ref[...] = jnp.concatenate([item[:, :chans] for item in outs], axis=1)
    attend_ref[...] = jnp.concatenate([item[:, chans:] for item in outs], axis=1)


def finish_rest(mlp, out, chans):
    count, share, units = mlp.shape[0], mlp.shape[1], mlp.shape[2] // 3
    return pl.pallas_call(
        partial(finish_rest_kernel, chans),
        out_shape=(
            jax.ShapeDtypeStruct((2, share, count * units), jnp.float32),
            jax.ShapeDtypeStruct((count * units, share), jnp.float32),
            jax.ShapeDtypeStruct((out.shape[1], count * chans), jnp.float32),
            jax.ShapeDtypeStruct((out.shape[1], count * HD), jnp.float32),
        ),
        name="finish_rest",
    )(mlp, out)


def forward_kernel(
    heads, base, sched_ref, proj_ref, filt_ref, table_ref, params_ref, skip_ref,
    held_ref, save_ref, state_ref, kv_ref, ext_ref, chain_ref, keys_ref, values_ref,
):
    index = pl.program_id(0)
    blocks = pl.num_programs(0)
    rows = proj_ref.shape[1]
    chans = heads * HEAD_M
    seq_start = sched_ref[blocks + index]

    @pl.when(index == 0)
    def _():
        keys_ref[...] = jnp.zeros_like(keys_ref)
        values_ref[...] = jnp.zeros_like(values_ref)

    @pl.when(seq_start == index * rows)
    def _():
        ext_ref[0:8, :] = jnp.zeros((8, ext_ref.shape[1]), jnp.float32)
        chain_ref[...] = jnp.zeros_like(chain_ref)

    proj = proj_ref[0]
    ext_ref[8:, :] = jnp.concatenate([proj[:, :256], proj[:, 512:768]], axis=1)
    conv = filtered(ext_ref, filt_ref, rows)
    ext_ref[0:8, :] = ext_ref[rows:, :]
    act = conv * jax.nn.sigmoid(conv)
    heads_x = act[:, :chans]
    b_in = act[:, 256 : 256 + NSTATE]
    c_in = act[:, 256 + NSTATE : 256 + 2 * NSTATE]
    step, _, lower, _, cum, cum_t = block_decay(
        proj[:, 768:] + params_ref[0:1, :], params_ref[1:2, :], rows
    )
    cum_cols = [cum[:, base + h : base + h + 1] for h in range(heads)]
    mix = dot_dims(c_in, b_in, 1, 1, SSD)
    fed = heads_x * spread([step[:, base + h : base + h + 1] for h in range(heads)], heads, HEAD_M)
    state = chain_ref[...]
    state_ref[0] = state
    inner = []
    for h in range(heads):
        gaps = jnp.where(lower, cum_cols[h] - cum_t[base + h : base + h + 1, :], 0.0)
        kernel = jnp.where(lower, jnp.exp(gaps), 0.0) * mix
        inner.append(dot_dims(kernel, fed[:, h * HEAD_M : (h + 1) * HEAD_M], 1, 0, SSD))
    growth = spread([jnp.exp(item) for item in cum_cols], heads, HEAD_M)
    inner = jnp.concatenate(inner, axis=1) + dot_dims(c_in, state, 1, 1, SSD) * growth
    ends = [item[rows - 1 : rows, :] for item in cum_cols]
    tail = spread([jnp.exp(end - item) for end, item in zip(ends, cum_cols)], heads, HEAD_M)
    emitted = dot_dims(fed * tail, b_in, 0, 0, SSD)
    for h in range(heads):
        part = slice(h * HEAD_M, (h + 1) * HEAD_M)
        chain_ref[part, :] = jnp.exp(ends[h]) * state[part, :] + emitted[part, :]
    gate_z = proj[:, 256 : 256 + chans]
    gated = (inner + skip_ref[0:1, :] * heads_x) * (gate_z * jax.nn.sigmoid(gate_z))

    table = table_ref[0]
    query = turn(proj[:, chans : chans + HD], table).astype(jnp.bfloat16)
    key = turn(proj[:, 256 + chans : 256 + chans + HD], table).astype(jnp.bfloat16)
    value = proj[:, 768 : 768 + HD].astype(jnp.bfloat16)
    here = pl.ds(pl.multiple_of(index * rows, rows), rows)
    keys_ref[here, :] = key
    values_ref[here, :] = value
    kv_ref[0] = jnp.concatenate([key, value], axis=1)
    total = keys_ref.shape[0]
    key_pos = lax.broadcasted_iota(jnp.int32, (rows, total), 1)
    my_pos = index * rows + lax.broadcasted_iota(jnp.int32, (rows, total), 0)
    allowed = (key_pos <= my_pos) & (key_pos >= seq_start)
    scores = jnp.where(
        allowed, dot_dims(query, keys_ref[...], 1, 1) * (1.0 / math.sqrt(HD)), NEG_LARGE
    )
    top = jnp.max(scores, axis=-1, keepdims=True)
    weights = jnp.exp(scores - top)
    denominator = jnp.sum(weights, axis=-1, keepdims=True)
    attn = dot_dims(weights.astype(jnp.bfloat16), values_ref[...], 1, 0) / denominator
    log_total = jnp.broadcast_to(top + jnp.log(denominator), (rows, 128))
    save_ref[0] = jnp.concatenate([inner, attn, log_total], axis=1)
    held_ref[0] = jnp.concatenate([gated, attn], axis=1).astype(jnp.bfloat16)


def backward_kernel(
    heads, base, sched_ref, proj_ref, before_ref, filt_ref, table_ref, params_ref, skip_ref,
    save_ref, state_ref, kv_ref, d_mix_ref,
    d_ref, filt_grad_ref, head_grad_ref, ext_ref, next_ref, later_ref, keys_ref, values_ref,
):
    blocks = pl.num_programs(0)
    turn_index = pl.program_id(0)
    index = blocks - 1 - turn_index
    rows = proj_ref.shape[1]
    chans = heads * HEAD_M
    seq_start = sched_ref[blocks + index]
    after = jnp.minimum(index + 1, blocks - 1)
    is_end = (index == blocks - 1) | (sched_ref[blocks + after] == after * rows)

    @pl.when(turn_index == 0)
    def _():
        keys_ref[...] = jnp.zeros_like(keys_ref)
        values_ref[...] = jnp.zeros_like(values_ref)
        filt_grad_ref[...] = jnp.zeros_like(filt_grad_ref)
        head_grad_ref[...] = jnp.zeros_like(head_grad_ref)

    @pl.when(is_end)
    def _():
        next_ref[rows:, :] = jnp.zeros((8, next_ref.shape[1]), jnp.float32)
        later_ref[...] = jnp.zeros_like(later_ref)

    proj = proj_ref[0]
    keep = jnp.where(seq_start == index * rows, 0.0, 1.0)
    before = before_ref[0]
    ext_ref[0:8, :] = jnp.concatenate([before[:, :256], before[:, 512:768]], axis=1) * keep
    ext_ref[8:, :] = jnp.concatenate([proj[:, :256], proj[:, 512:768]], axis=1)
    conv = filtered(ext_ref, filt_ref, rows)
    conv_sig = jax.nn.sigmoid(conv)
    act = conv * conv_sig
    heads_x = act[:, :chans]
    b_in = act[:, 256 : 256 + NSTATE]
    c_in = act[:, 256 + NSTATE : 256 + 2 * NSTATE]
    step_in = proj[:, 768:] + params_ref[0:1, :]
    rate = params_ref[1:2, :]
    step, decay, lower, ones, cum, cum_t = block_decay(step_in, rate, rows)
    cum_cols = [cum[:, base + h : base + h + 1] for h in range(heads)]
    step_cols = spread([step[:, base + h : base + h + 1] for h in range(heads)], heads, HEAD_M)
    mix = dot_dims(c_in, b_in, 1, 1, SSD)
    fed = heads_x * step_cols
    state = state_ref[0]
    later = later_ref[...]
    save = save_ref[0]
    inner = save[:, :chans]
    skip = skip_ref[0:1, :]

    d_mix = d_mix_ref[0]
    d_gated = d_mix[:, :chans]
    gate_z = proj[:, 256 : 256 + chans]
    gate_sig = jax.nn.sigmoid(gate_z)
    d_z = d_gated * (inner + skip * heads_x) * (gate_sig * (1.0 + gate_z * (1.0 - gate_sig)))
    d_y = d_gated * (gate_z * gate_sig)
    growth = spread([jnp.exp(item) for item in cum_cols], heads, HEAD_M)
    ends = [item[rows - 1 : rows, :] for item in cum_cols]
    tail = spread([jnp.exp(end - item) for end, item in zip(ends, cum_cols)], heads, HEAD_M)
    grown = d_y * growth
    fed_tail = fed * tail
    fed_inner = []
    d_mixing = jnp.zeros((rows, rows), jnp.float32)
    for h in range(heads):
        part = slice(h * HEAD_M, (h + 1) * HEAD_M)
        gaps = jnp.where(lower, cum_cols[h] - cum_t[base + h : base + h + 1, :], 0.0)
        decays = jnp.where(lower, jnp.exp(gaps), 0.0)
        fed_inner.append(dot_dims(decays * mix, d_y[:, part], 0, 0, SSD))
        d_mixing = d_mixing + dot_dims(d_y[:, part], fed[:, part], 1, 1, SSD) * decays
    fed_emit = dot_dims(b_in, later, 1, 1, SSD) * tail
    d_fed = jnp.concatenate(fed_inner, axis=1) + fed_emit
    d_c = dot_dims(d_mixing, b_in, 1, 0, SSD) + dot_dims(grown, state, 1, 0, SSD)
    d_b = dot_dims(d_mixing, c_in, 0, 0, SSD) + dot_dims(fed_tail, later, 1, 0, SSD)
    state_grad = dot_dims(grown, c_in, 0, 0, SSD)
    d_x = d_fed * step_cols + skip * d_y
    lane = lax.broadcasted_iota(jnp.int32, (1, 128), 1)
    d_cum = jnp.zeros((rows, 128), jnp.float32)
    d_step = jnp.zeros((rows, 128), jnp.float32)
    d_total = jnp.zeros((1, 128), jnp.float32)
    skip_sum = jnp.zeros((1, 128), jnp.float32)
    cum_terms = d_y * inner - fed * d_fed
    step_terms = d_fed * heads_x
    emit_terms = fed * fed_emit
    skip_terms = d_y * heads_x
    carry_terms = later * state
    for h in range(heads):
        part = slice(h * HEAD_M, (h + 1) * HEAD_M)
        mine = jnp.where(lane == base + h, 1.0, 0.0)
        growth_end = jnp.exp(ends[h])
        d_cum = d_cum + jnp.sum(cum_terms[:, part], axis=1, keepdims=True) * mine
        d_step = d_step + jnp.sum(step_terms[:, part], axis=1, keepdims=True) * mine
        carry = jnp.sum(jnp.sum(carry_terms[part, :], axis=0, keepdims=True), axis=1, keepdims=True)
        emit = jnp.sum(jnp.sum(emit_terms[:, part], axis=0, keepdims=True), axis=1, keepdims=True)
        skips = jnp.sum(jnp.sum(skip_terms[:, part], axis=0, keepdims=True), axis=1, keepdims=True)
        d_total = d_total + (growth_end * carry + emit) * mine
        skip_sum = skip_sum + skips * mine
        later_ref[part, :] = state_grad[part, :] + growth_end * later[part, :]
    d_decay = dot_dims(ones, d_cum, 0, 0, HIGH) + d_total
    d_step = (d_step - d_decay * rate) * jax.nn.sigmoid(step_in)
    d_step = jnp.where((lane >= base) & (lane < base + heads), d_step, 0.0)
    head_grad_ref[0:1, :] += jnp.sum(d_step, axis=0, keepdims=True)
    head_grad_ref[1:2, :] += jnp.sum(d_decay * decay, axis=0, keepdims=True)
    head_grad_ref[2:3, :] += skip_sum

    d_conv = jnp.concatenate([d_x, jnp.zeros((rows, 256 - chans), jnp.float32), d_b, d_c], axis=1)
    d_conv = d_conv * (conv_sig * (1.0 + conv * (1.0 - conv_sig)))
    next_ref[0:rows, :] = d_conv
    d_in = filt_ref[KERNEL - 1 : KERNEL, :] * d_conv
    for tap in range(KERNEL - 1):
        shift = KERNEL - 1 - tap
        d_in = d_in + filt_ref[tap : tap + 1, :] * next_ref[shift : shift + rows, :]
        filt_grad_ref[tap : tap + 1, :] += jnp.sum(
            d_conv * ext_ref[8 - shift : 8 - shift + rows, :], axis=0, keepdims=True
        )
    filt_grad_ref[KERNEL - 1 : KERNEL, :] += jnp.sum(d_conv * ext_ref[8:, :], axis=0, keepdims=True)
    filt_grad_ref[KERNEL : KERNEL + 1, :] += jnp.sum(d_conv, axis=0, keepdims=True)
    next_ref[rows:, :] = d_conv[0:8, :]

    table = table_ref[0]
    scale = 1.0 / math.sqrt(HD)
    query = turn(proj[:, chans : chans + HD], table).astype(jnp.bfloat16)
    keys = kv_ref[:, :HD]
    values = kv_ref[:, HD:]
    d_attn = d_mix[:, chans : chans + HD].astype(jnp.bfloat16)
    delta = jnp.sum(d_attn.astype(jnp.float32) * save[:, chans : chans + HD], axis=1, keepdims=True)
    total = keys.shape[0]
    key_pos = lax.broadcasted_iota(jnp.int32, (rows, total), 1)
    my_pos = index * rows + lax.broadcasted_iota(jnp.int32, (rows, total), 0)
    allowed = (key_pos <= my_pos) & (key_pos >= seq_start)
    scores = jnp.where(allowed, dot_dims(query, keys, 1, 1) * scale, NEG_LARGE)
    probs = jnp.exp(scores - save[:, chans + HD : chans + HD + 1])
    d_scores = (probs * (dot_dims(d_attn, values, 1, 1) - delta) * scale).astype(jnp.bfloat16)
    d_query = turn(dot_dims(d_scores, keys, 1, 0), table, back=True)
    keys_ref[...] += dot_dims(d_scores, query, 0, 0)
    values_ref[...] += dot_dims(probs.astype(jnp.bfloat16), d_attn, 0, 0)
    here = pl.ds(pl.multiple_of(index * rows, rows), rows)
    d_key = turn(keys_ref[here, :], table, back=True)
    d_value = values_ref[here, :]
    d_ref[0] = jnp.concatenate(
        [d_in[:, :chans], d_query, d_z, d_key, d_in[:, 256:], d_value, d_step[:, HD:]], axis=1
    ).astype(jnp.bfloat16)


def mixer_forward(sched, proj, filt, table, params, skip, heads, base):
    blocks, rows, wide = proj.shape
    chans = heads * HEAD_M
    held = lambda b, s: (s[b], 0, 0)
    plain = lambda b, s: (b, 0, 0)
    whole = lambda b, s: (0, 0)
    return pl.pallas_call(
        partial(forward_kernel, heads, base),
        out_shape=(
            jax.ShapeDtypeStruct((blocks, rows, 256), jnp.bfloat16),
            jax.ShapeDtypeStruct((blocks, rows, 384), jnp.float32),
            jax.ShapeDtypeStruct((blocks, chans, NSTATE), jnp.float32),
            jax.ShapeDtypeStruct((blocks, rows, 2 * HD), jnp.bfloat16),
        ),
        grid_spec=pltpu.PrefetchScalarGridSpec(
            num_scalar_prefetch=1,
            grid=(blocks,),
            in_specs=[
                pl.BlockSpec((1, rows, wide), held),
                pl.BlockSpec(filt.shape, whole),
                pl.BlockSpec((1, rows, 2 * HD), plain),
                pl.BlockSpec(params.shape, whole),
                pl.BlockSpec(skip.shape, whole),
            ],
            out_specs=(
                pl.BlockSpec((1, rows, 256), held),
                pl.BlockSpec((1, rows, 384), plain),
                pl.BlockSpec((1, chans, NSTATE), plain),
                pl.BlockSpec((1, rows, 2 * HD), plain),
            ),
            scratch_shapes=[
                pltpu.VMEM((rows + 8, 512), jnp.float32),
                pltpu.VMEM((chans, NSTATE), jnp.float32),
                pltpu.VMEM((blocks * rows, HD), jnp.bfloat16),
                pltpu.VMEM((blocks * rows, HD), jnp.bfloat16),
            ],
        ),
        cost_estimate=pl.CostEstimate(
            flops=25_000_000_000, transcendentals=0, bytes_accessed=12_000_000
        ),
        name="mixer_forward",
    )(sched, proj, filt, table, params, skip)


def mixer_backward(sched, proj, filt, table, params, skip, save, states, kv, d_mix, heads, base):
    blocks, rows, wide = proj.shape
    chans = heads * HEAD_M
    held = lambda i, s: (s[blocks - 1 - i], 0, 0)
    before = lambda i, s: (s[jnp.maximum(blocks - 2 - i, 0)], rows // 8 - 1, 0)
    plain = lambda i, s: (blocks - 1 - i, 0, 0)
    whole = lambda i, s: (0, 0)
    return pl.pallas_call(
        partial(backward_kernel, heads, base),
        out_shape=(
            jax.ShapeDtypeStruct((blocks, rows, wide), jnp.bfloat16),
            jax.ShapeDtypeStruct((8, 512), jnp.float32),
            jax.ShapeDtypeStruct((8, 128), jnp.float32),
        ),
        grid_spec=pltpu.PrefetchScalarGridSpec(
            num_scalar_prefetch=1,
            grid=(blocks,),
            in_specs=[
                pl.BlockSpec((1, rows, wide), held),
                pl.BlockSpec((1, 8, wide), before),
                pl.BlockSpec(filt.shape, whole),
                pl.BlockSpec((1, rows, 2 * HD), plain),
                pl.BlockSpec(params.shape, whole),
                pl.BlockSpec(skip.shape, whole),
                pl.BlockSpec((1, rows, 384), plain),
                pl.BlockSpec((1, chans, NSTATE), plain),
                pl.BlockSpec((blocks * rows, 2 * HD), whole),
                pl.BlockSpec((1, rows, 256), held),
            ],
            out_specs=(
                pl.BlockSpec((1, rows, wide), held),
                pl.BlockSpec((8, 512), whole),
                pl.BlockSpec((8, 128), whole),
            ),
            scratch_shapes=[
                pltpu.VMEM((rows + 8, 512), jnp.float32),
                pltpu.VMEM((rows + 8, 512), jnp.float32),
                pltpu.VMEM((chans, NSTATE), jnp.float32),
                pltpu.VMEM((blocks * rows, HD), jnp.float32),
                pltpu.VMEM((blocks * rows, HD), jnp.float32),
            ],
        ),
        cost_estimate=pl.CostEstimate(
            flops=40_000_000_000, transcendentals=0, bytes_accessed=16_000_000
        ),
        name="mixer_backward",
    )(sched, proj, proj, filt, table, params, skip, save, states, kv.reshape(-1, 2 * HD), d_mix)


def head_plan(
    block_input,
    out_cotangent,
    lengths,
    slot_block,
    norm_gains,
    short_filter,
    step_bias,
    log_rate,
    skip_gain,
    mixer_in,
    mixer_out,
    attend_in,
    attend_out,
    gate_up,
    down_weight,
):
    count = lax.axis_size("ctx")
    groups = lax.axis_size("wsh")
    ctx = lax.axis_index("ctx")
    wsh = lax.axis_index("wsh")
    rows, width = block_input.shape[1:]
    block_rows = rows // 2
    blocks = 2 * count
    total_rows = count * rows
    heads = MHEADS // count
    chans = heads * HEAD_M
    kv_head = ctx * KVH // count
    units = gate_up.shape[2] // count
    first_len = lengths[0, 0]
    tokens = block_input[0]
    cotangent = out_cotangent[0]
    cols = lambda array, start, size: lax.dynamic_slice_in_dim(array, start, size, array.ndim - 1)
    base = HD
    step_pad = 128 - base - heads

    in_cols = pick_columns(
        jnp.stack([ctx, kv_head]), mixer_in, attend_in, norm_gains, heads
    )
    in_all = gather_wsh(in_cols, 1)
    gains = gather_wsh(after(norm_gains, in_cols), 1).astype(jnp.float32)
    out_rows = jnp.concatenate(
        [
            lax.dynamic_slice_in_dim(mixer_out, ctx * chans, chans, 0),
            lax.dynamic_slice_in_dim(attend_out, ctx * HD, HD, 0),
        ],
        axis=0,
    )
    mlp_cols = cols(gate_up, ctx * units, units)
    mlp_rows = lax.dynamic_slice_in_dim(down_weight, ctx * units, units, 0)
    out_rows, mlp_cols, mlp_rows = after((out_rows, mlp_cols, mlp_rows), in_all)
    out_mine = gather_wsh(out_rows, 1)
    mlp_parts = swap_groups([mlp_cols] * groups)
    down_all = jnp.concatenate(swap_groups([mlp_rows] * groups), axis=0)
    gate_up_cols = jnp.concatenate(
        [part[0] for part in mlp_parts] + [part[1] for part in mlp_parts], axis=1
    )

    peers = ctx ^ jnp.array(held_order(count), dtype=jnp.int32)
    held = jnp.take(slot_block.reshape(count, 2), peers, axis=0, mode="clip").reshape(blocks)
    logical_ids = jnp.arange(blocks, dtype=jnp.int32)

    place = jnp.sum(
        jnp.where(held[None, :] == logical_ids[:, None], logical_ids[None, :], 0), axis=1
    )
    starts = jnp.where(logical_ids * block_rows >= first_len, first_len, 0)
    sched = jnp.concatenate([place, starts])
    positions = jnp.arange(total_rows, dtype=jnp.int32)
    seq_pos = positions - jnp.where(positions >= first_len, first_len, 0)
    half = HD // 2
    freqs = jnp.exp(jnp.arange(half, dtype=jnp.float32) * (-2.0 * math.log(ROPE_BASE) / HD))
    angles = seq_pos.astype(jnp.float32)[:, None] * freqs[None, :]
    cosines = jnp.cos(angles)
    sines = jnp.sin(angles)
    table = jnp.concatenate([cosines, cosines, -sines, sines], axis=1)
    table = table.reshape(blocks, block_rows, 2 * HD)
    filt = jnp.concatenate(
        [
            cols(short_filter, ctx * chans, chans),
            jnp.zeros((KERNEL + 1, HD), jnp.float32),
            short_filter[:, DSSM:],
        ],
        axis=1,
    )
    filt = jnp.pad(filt, ((0, 7 - KERNEL), (0, 0)))
    mine = lambda array: lax.dynamic_slice_in_dim(array, ctx * heads, heads)
    params = jnp.stack([mine(step_bias), jnp.exp(mine(log_rate))], axis=0)
    params = jnp.pad(params, ((0, 6), (base, 128 - base - heads)))
    skip = jnp.broadcast_to(jnp.repeat(mine(skip_gain), HEAD_M)[None, :], (8, chans))

    first_scale = lax.rsqrt(jnp.mean(tokens * tokens, axis=-1, keepdims=True) + EPS)
    unit_tokens = tokens * first_scale
    units_first = gather_ctx(unit_tokens.astype(jnp.bfloat16)).reshape(total_rows, width)
    cot_all = gather_ctx(after(cotangent.astype(jnp.bfloat16), units_first))
    cot_all = cot_all.reshape(total_rows, width)
    projected = matmul_back(units_first, in_all).reshape(blocks, block_rows, in_all.shape[0])
    mixed_held, saved, states, kv = mixer_forward(
        sched, projected, filt, table, params, skip, heads, base
    )
    mixed_held = mixed_held.reshape(total_rows, chans + HD)

    hidden = tokens + scatter_ctx(
        jnp.dot(mixed_held, out_mine, preferred_element_type=jnp.float32).reshape(
            count, rows, width
        )
    )

    second_scale = lax.rsqrt(jnp.mean(hidden * hidden, axis=-1, keepdims=True) + EPS)
    unit_hidden = hidden * second_scale
    normed_second = gather_ctx((unit_hidden * gains[1]).astype(jnp.bfloat16)).reshape(
        total_rows, width
    )
    both = jnp.dot(normed_second, gate_up_cols, preferred_element_type=jnp.float32)
    gate_part = both[:, : groups * units]
    up_part = both[:, groups * units :]
    silu_gate = jax.nn.silu(gate_part)
    mlp_act = (silu_gate * up_part).astype(jnp.bfloat16)
    d_mlp = matmul_back(cot_all, down_all)
    d_gate = (d_mlp * up_part * silu_slope(gate_part)).astype(jnp.bfloat16)
    d_up = (d_mlp * silu_gate).astype(jnp.bfloat16)
    d_both = jnp.concatenate([d_gate, d_up], axis=1)
    d_normed_second = scatter_ctx(matmul_back(d_both, gate_up_cols).reshape(count, rows, width))
    mlp_parts = jnp.dot(mlp_act, down_all, preferred_element_type=jnp.float32)
    mlp_parts = mlp_parts.astype(jnp.bfloat16).reshape(count, rows, width)

    def norm_back(d_normed, gain, unit, unit_scale):
        scaled = d_normed * gain
        return unit_scale * (scaled - unit * jnp.mean(scaled * unit, axis=-1, keepdims=True))

    hidden_grad = cotangent + norm_back(d_normed_second, gains[1], unit_hidden, second_scale)
    hidden_b = gather_ctx(hidden_grad.astype(jnp.bfloat16)).reshape(total_rows, width)

    both_grad = matmul_t(normed_second, d_both)
    down_grad_t = matmul_t(cot_all, mlp_act)
    gain_second_grad = jnp.sum(both_grad * gate_up_cols.astype(jnp.float32), axis=1) / gains[1]
    mlp_grads = [
        jnp.concatenate(
            [
                both_grad[:, k * units : (k + 1) * units],
                both_grad[:, (groups + k) * units : (groups + k + 1) * units],
                down_grad_t[:, k * units : (k + 1) * units],
            ],
            axis=1,
        ).astype(jnp.bfloat16)
        for k in range(groups)
    ]
    mlp_swapped = swap_groups(mlp_grads)
    mlp_sum = sum(piece.astype(jnp.float32) for piece in mlp_swapped)
    mlp_sum = mlp_sum.astype(jnp.bfloat16).reshape(count, width // count, 3 * units)

    d_mix = matmul_back(hidden_b, out_mine).reshape(blocks, block_rows, chans + HD)
    share = width // (count * groups)

    def to_groups(grad):
        parts = grad.reshape(count, groups, share, grad.shape[1])
        return [
            lax.dynamic_index_in_dim(parts, wsh ^ k, 1, keepdims=False).astype(jnp.bfloat16)
            for k in range(groups)
        ]

    mlp_parts = after(mlp_parts, hidden_b)
    places = jnp.array([held_order(count).index(k) for k in range(count)], dtype=jnp.int32)
    by_device = jnp.take(places, ctx ^ jnp.arange(count, dtype=jnp.int32), mode="clip")
    mlp_parts = jnp.take(mlp_parts, by_device, axis=0, mode="clip")
    mlp_parts = trade_ctx(mlp_parts)
    output = hidden + jnp.sum(mlp_parts.astype(jnp.float32), axis=0)
    mlp_final = trade_ctx(after(mlp_sum, mlp_parts))
    out_grads = to_groups(matmul_t(hidden_b, mixed_held))
    out_swapped = swap_groups(out_grads)
    out_sum = sum(piece.astype(jnp.float32) for piece in out_swapped)
    d_held, filt_grad, head_grad = mixer_backward(
        sched, projected, filt, table, params, skip, saved, states, kv, d_mix, heads, base
    )
    out_final = trade_ctx(after(out_sum.astype(jnp.bfloat16), mlp_parts))
    gate_up_grad, down_grad, mixer_out_grad, attend_out_grad = finish_rest(
        mlp_final, out_final, chans
    )
    mixer_out_grad = jnp.transpose(mixer_out_grad)
    attend_out_grad = jnp.transpose(attend_out_grad)
    d_held = d_held.reshape(total_rows, -1)
    d_unit_first = scatter_ctx(
        jnp.dot(d_held, in_all, preferred_element_type=jnp.float32).reshape(count, rows, width)
    )
    input_grad = hidden_grad + norm_back(d_unit_first, 1.0, unit_tokens, first_scale)

    in_grad = matmul_t(units_first, d_held)
    gain_first_grad = jnp.sum(in_grad * jnp.transpose(in_all).astype(jnp.float32), axis=1) / gains[0]
    in_grad = in_grad * gains[0][:, None]
    lane = jnp.arange(in_all.shape[0], dtype=jnp.int32)[None, :]
    gain_lane = in_all.shape[0] - step_pad
    in_grad = jnp.where(lane == gain_lane, gain_first_grad[:, None], in_grad)
    in_grad = jnp.where(lane == gain_lane + 1, gain_second_grad[:, None], in_grad)
    in_grads = to_groups(in_grad)
    in_swapped = swap_groups(in_grads)
    in_sum = sum(piece.astype(jnp.float32) for piece in in_swapped)
    mixer_in_grad, attend_in_grad, last_cols = finish_in(
        trade_ctx(after(in_sum.astype(jnp.bfloat16), (mlp_final, out_final))), heads
    )
    gain_place = gain_lane % 128
    gains_grad = jnp.transpose(last_cols[:, gain_place : gain_place + 2])
    side_by_side = lambda array: jnp.transpose(array, (1, 0, 2)).reshape(array.shape[1], -1)

    small = jnp.concatenate([filt_grad.reshape(-1, 128), head_grad], axis=0)
    small = gather_ctx(jnp.sum(gather_wsh(small[None]), axis=0))
    small = jnp.take(small, by_device, axis=0, mode="clip")
    filters = small[:, :-8].reshape(count, 8, 512)[:, : KERNEL + 1]
    filter_grad = jnp.concatenate(
        [side_by_side(filters[:, :, :chans]), jnp.sum(filters[:, :, 256:], axis=0)], axis=1
    )
    per_head = small[:, -8:-5, base : base + heads]
    step_bias_all, log_rate_all, skip_all = [per_head[:, i].reshape(-1) for i in range(3)]
    return (
        output[None],
        input_grad[None],
        gains_grad,
        filter_grad,
        step_bias_all,
        log_rate_all,
        skip_all,
        mixer_in_grad,
        mixer_out_grad,
        attend_in_grad,
        attend_out_grad,
        gate_up_grad,
        down_grad,
    )


def on_device_heads(*args):
    return head_plan(*args)


def solution(mesh):
    placed = (
        P("wsh", "ctx", None),
        P("wsh", "ctx", None),
        P("wsh", None),
        P(),
        P(None, "wsh"),
        P(),
        P(),
        P(),
        P(),
        P("wsh", None),
        P(None, "wsh"),
        P("wsh", None),
        P(None, "wsh"),
        P(None, None, "wsh"),
        P("wsh", None),
    )
    per_heads = mesh.shape["ctx"] == QH
    return jax.shard_map(
        on_device_heads if per_heads else on_device,
        mesh=mesh,
        in_specs=placed,
        out_specs=(
            P("wsh", "ctx", None),
            P("wsh", "ctx", None),
            P(None, ("ctx", "wsh")),
            P(),
            P(),
            P(),
            P(),
            P(("ctx", "wsh"), None),
            P(None, ("ctx", "wsh")),
            P(("ctx", "wsh"), None),
            P(None, ("ctx", "wsh")),
            P(None, "ctx", "wsh"),
            P("wsh", "ctx"),
        ),
        check_vma=False,
    )
```

```python
import math
from functools import partial

import jax
import jax.numpy as jnp
from jax import lax
from jax.experimental import pallas as pl
from jax.experimental.pallas import tpu as pltpu
from jax.sharding import PartitionSpec as P

MHEADS = 24
HEAD_M = 64
NSTATE = 128
QH = 8
KVH = 2
HD = 64
KERNEL = 4
DSSM = 1536
CONV = 1792
AQ = 512
GRP = 4


EPS = 1e-05
ROPE_BASE = 100000000000.0
HIGH = lax.Precision.HIGHEST
SSD = None
NEG_LARGE = -1e30
GAIN_ROW = 880


def rms_norm(values, gain):
    scale = lax.rsqrt(jnp.mean(values * values, axis=-1, keepdims=True) + EPS)
    return values * scale * gain


def silu_slope(values):
    sigmoid_value = jax.nn.sigmoid(values)
    return sigmoid_value * (1.0 + values * (1.0 - sigmoid_value))


def rope_tables(positions):
    half = HD // 2
    freqs = jnp.exp(jnp.arange(half, dtype=jnp.float32) * (-2.0 * math.log(ROPE_BASE) / HD))
    angles = positions.astype(jnp.float32)[:, None] * freqs[None, :]
    return (jnp.cos(angles)[:, None, :], jnp.sin(angles)[:, None, :])


def rotate(values, cosines, sines):
    half = values.shape[-1] // 2
    first = values[..., :half]
    second = values[..., half:]
    return jnp.concatenate(
        [first * cosines - second * sines, second * cosines + first * sines], axis=-1
    )


def matmul_t(left, right):
    return lax.dot_general(
        left, right, (((0,), (0,)), ((), ())), preferred_element_type=jnp.float32
    )


def matmul_back(left, right):
    return lax.dot_general(
        left, right, (((1,), (1,)), ((), ())), preferred_element_type=jnp.float32
    )


def step_prep(step_raw, step_bias, log_rate):
    step = jax.nn.softplus(step_raw + step_bias)
    return (step, -step * jnp.exp(log_rate))


def conv_prep(conv_blocks, tails_in, filter_rows):
    count = conv_blocks.shape[1]
    extended = jnp.concatenate([tails_in, conv_blocks], axis=1)
    conv = filter_rows[KERNEL] + filter_rows[KERNEL - 1] * conv_blocks
    for tap_index in range(KERNEL - 1):
        conv = conv + filter_rows[tap_index] * extended[:, tap_index : tap_index + count]
    return jax.nn.silu(conv)


def ssd_emit(heads_x, b_in, step, log_decay):
    cumulative = jnp.cumsum(log_decay, axis=0)
    weight = jnp.exp(cumulative[-1][None, :] - cumulative) * step
    emitted = jnp.einsum("shp,sn->hpn", heads_x * weight[:, :, None], b_in, precision=HIGH)
    return (emitted, cumulative[-1])


def ssd_output(heads_x, b_in, c_in, step, log_decay, state_in, skip_gain):
    cumulative = jnp.cumsum(log_decay, axis=0)
    count = heads_x.shape[0]
    lower = (jnp.arange(count)[:, None] >= jnp.arange(count)[None, :])[:, :, None]
    gaps = jnp.where(lower, cumulative[:, None, :] - cumulative[None, :, :], 0.0)
    kernel = (
        jnp.where(lower, jnp.exp(gaps), 0.0) * jnp.dot(c_in, b_in.T, precision=HIGH)[:, :, None]
    )
    inner = jnp.einsum("tsh,shp->thp", kernel, heads_x * step[:, :, None], precision=HIGH)
    carried = (
        jnp.einsum("hpn,tn->thp", state_in, c_in, precision=HIGH) * jnp.exp(cumulative)[:, :, None]
    )
    return inner + carried + skip_gain[None, :, None] * heads_x


def chain_fold(slot_block, my_blocks, block_second, first_len, block_rows, prefix, later):

    def fold(total, piece, start):
        count = piece.shape[0]
        same = (slot_block * block_rows >= first_len)[None, :] == block_second[:, None]
        if later:
            valid = same & (slot_block[None, :] > my_blocks[:, None])
            gaps = (
                jnp.take(prefix, slot_block, axis=0)[None, :, :]
                - jnp.take(prefix, my_blocks + 1, axis=0)[:, None, :]
            )
        else:
            valid = same & (slot_block[None, :] < my_blocks[:, None])
            gaps = (
                jnp.take(prefix, my_blocks, axis=0)[:, None, :]
                - jnp.take(prefix, slot_block + 1, axis=0)[None, :, :]
            )
        factors = jnp.where(
            valid[:, :, None], jnp.exp(jnp.where(valid[:, :, None], gaps, 0.0)), 0.0
        )
        step_size = math.gcd(count, 8)

        def add_rows(index, running):
            rows_piece = lax.dynamic_slice_in_dim(piece, index * step_size, step_size).astype(
                jnp.float32
            )
            factor_rows = lax.dynamic_slice_in_dim(factors, index * step_size, step_size, 1)
            return running + jnp.einsum("bsh,shpn->bhpn", factor_rows, rows_piece, precision=HIGH)

        return lax.fori_loop(0, count // step_size, add_rows, total)

    return fold


def in_blocks(step_fn, carry, piece):
    count = piece.shape[0]
    block_size = math.gcd(count, 512)

    def visit(block_index, state):
        sub_piece = lax.dynamic_slice_in_dim(piece, block_index * block_size, block_size)
        return step_fn(state, sub_piece, block_index * block_size)

    return lax.fori_loop(0, count // block_size, visit, carry)


def on_device(
    block_input,
    out_cotangent,
    lengths,
    slot_block,
    norm_gains,
    short_filter,
    step_bias,
    log_rate,
    skip_gain,
    mixer_in,
    mixer_out,
    attend_in,
    attend_out,
    gate_up,
    down_weight,
):
    gains_all, in_mix, out_mix, in_attend, out_attend = (
        lax.all_gather(norm_gains, "wsh", axis=1, tiled=True),
        lax.all_gather(mixer_in, "wsh", axis=0, tiled=True),
        lax.all_gather(mixer_out, "wsh", axis=1, tiled=True),
        lax.all_gather(attend_in, "wsh", axis=0, tiled=True),
        lax.all_gather(attend_out, "wsh", axis=1, tiled=True),
    )
    ctx_count = lax.axis_size("ctx")
    block_count = 2 * ctx_count
    rows = block_input.shape[1]
    block_rows = rows // 2
    kv_width = KVH * HD
    scale = 1.0 / math.sqrt(HD)
    tokens = block_input[0]
    cotangent = out_cotangent[0]
    first_len = lengths[0, 0]
    logical_ids = jnp.arange(block_count, dtype=jnp.int32)
    my_blocks = lax.dynamic_slice_in_dim(slot_block, 2 * lax.axis_index("ctx"), 2)
    block_offsets = jnp.arange(block_rows, dtype=jnp.int32)
    my_pos = (my_blocks[:, None] * block_rows + block_offsets[None, :]).reshape(rows)
    my_second = my_pos >= first_len
    seq_pos = my_pos - jnp.where(my_second, first_len, 0)
    block_second = my_blocks * block_rows >= first_len
    is_start = (my_blocks == 0) | (my_blocks * block_rows == first_len)
    key_pos = (slot_block[:, None] * block_rows + block_offsets[None, :]).reshape(
        block_count * block_rows
    )
    gain_first = gains_all[0].astype(jnp.float32)
    gain_second = gains_all[1].astype(jnp.float32)
    normed, first_norm_vjp = jax.vjp(rms_norm, tokens, gain_first)
    normed_first = normed.astype(jnp.bfloat16)
    mixed = jnp.dot(normed_first, in_mix, preferred_element_type=jnp.float32)
    gate_z = mixed[:, :DSSM]
    conv_input = mixed[:, DSSM : DSSM + CONV]
    step_raw = mixed[:, DSSM + CONV :]
    (step, log_decay), step_vjp = jax.vjp(step_prep, step_raw, step_bias, log_rate)
    step_blocks = step.reshape(2, block_rows, MHEADS)
    decay_blocks = log_decay.reshape(2, block_rows, MHEADS)
    totals = jnp.sum(decay_blocks, axis=1)
    conv_blocks = conv_input.reshape(2, block_rows, CONV)
    tails = conv_blocks[:, block_rows - (KERNEL - 1) :, :]
    all_tails, all_totals = (
        lax.all_gather(tails, "ctx", axis=0, tiled=True),
        lax.all_gather(totals, "ctx", axis=0, tiled=True),
    )
    one_hot = (slot_block[None, :] == logical_ids[:, None]).astype(jnp.float32)
    totals_logical = jnp.dot(one_hot, all_totals, precision=HIGH)
    prefix = jnp.concatenate(
        [jnp.zeros((1, MHEADS), jnp.float32), jnp.cumsum(totals_logical, axis=0)], axis=0
    )
    pred_slot = jnp.sum(
        jnp.where(slot_block[None, :] == (my_blocks - 1)[:, None], logical_ids[None, :], 0), axis=1
    )
    keep_tail = jnp.where(is_start, 0.0, 1.0).astype(jnp.float32)
    tails_in = jnp.take(all_tails, pred_slot, axis=0) * keep_tail[:, None, None]
    activated, conv_vjp = jax.vjp(conv_prep, conv_blocks, tails_in, short_filter)
    heads_x = activated[:, :, :DSSM].reshape(2, block_rows, MHEADS, HEAD_M)
    b_in = activated[:, :, DSSM : DSSM + NSTATE]
    c_in = activated[:, :, DSSM + NSTATE :]
    (emitted, emit_totals), emit_vjp = jax.vjp(
        jax.vmap(ssd_emit), heads_x, b_in, step_blocks, decay_blocks
    )
    zero_states = jnp.zeros((2, MHEADS, HEAD_M, NSTATE), jnp.float32)
    chain_forward = chain_fold(
        slot_block, my_blocks, block_second, first_len, block_rows, prefix, False
    )
    state_in = chain_forward(
        zero_states,
        lax.all_gather(emitted.astype(jnp.bfloat16), "ctx", axis=0, tiled=True),
        jnp.int32(0),
    )
    mixer_y, out_vjp = jax.vjp(
        jax.vmap(ssd_output, in_axes=(0, 0, 0, 0, 0, 0, None)),
        heads_x,
        b_in,
        c_in,
        step_blocks,
        decay_blocks,
        state_in,
        skip_gain,
    )
    mixer_flat = mixer_y.reshape(rows, DSSM)
    gated = (mixer_flat * jax.nn.silu(gate_z)).astype(jnp.bfloat16)
    mixer_branch = jnp.dot(gated, out_mix, preferred_element_type=jnp.float32)
    projected = jnp.dot(normed_first, in_attend, preferred_element_type=jnp.float32)
    cosines, sines = rope_tables(seq_pos)
    queries = rotate(projected[:, :AQ].reshape(rows, QH, HD), cosines, sines).astype(jnp.bfloat16)
    keys_rot = rotate(
        projected[:, AQ : AQ + kv_width].reshape(rows, KVH, HD), cosines, sines
    ).astype(jnp.bfloat16)
    values = projected[:, AQ + kv_width :].astype(jnp.bfloat16)
    kv_local = jnp.concatenate([keys_rot.reshape(rows, kv_width), values], axis=1)
    query_heads = queries.reshape(rows, KVH, GRP, HD)

    def allowed_at(start, count):
        piece_pos = lax.dynamic_slice_in_dim(key_pos, start, count)
        return (piece_pos[None, :] <= my_pos[:, None]) & (
            (piece_pos >= first_len)[None, :] == my_second[:, None]
        )

    def split_piece(piece):
        count = piece.shape[0]
        return (
            piece[:, :kv_width].reshape(count, KVH, HD),
            piece[:, kv_width:].reshape(count, KVH, HD),
        )

    def attend_step(carry, piece, start):
        top, denominator, running = carry
        keys_piece, values_piece = split_piece(piece)
        allowed = allowed_at(start, piece.shape[0])
        scores = (
            jnp.einsum(
                "tkgd,skd->kgts", query_heads, keys_piece, preferred_element_type=jnp.float32
            )
            * scale
        )
        masked = jnp.where(allowed, scores, NEG_LARGE)
        new_top = jnp.maximum(top, jnp.max(masked, axis=-1))
        weights = jnp.where(allowed, jnp.exp(masked - new_top[..., None]), 0.0)
        factor = jnp.exp(top - new_top)
        denominator = denominator * factor + jnp.sum(weights, axis=-1)
        running = running * factor[..., None] + jnp.einsum(
            "kgts,skd->kgtd", weights, values_piece.astype(jnp.float32), precision=HIGH
        )
        return (new_top, denominator, running)

    start_carry = (
        jnp.full((KVH, GRP, rows), NEG_LARGE, jnp.float32),
        jnp.zeros((KVH, GRP, rows), jnp.float32),
        jnp.zeros((KVH, GRP, rows, HD), jnp.float32),
    )
    top, denominator, running = in_blocks(
        attend_step, start_carry, lax.all_gather(kv_local, "ctx", axis=0, tiled=True)
    )
    log_total = top + jnp.log(denominator)
    attn_heads = running / denominator[..., None]
    attn_rows = jnp.transpose(attn_heads, (2, 0, 1, 3)).reshape(rows, AQ)
    attn_b = attn_rows.astype(jnp.bfloat16)
    attn_branch = jnp.dot(attn_b, out_attend, preferred_element_type=jnp.float32)
    hidden = tokens + mixer_branch + attn_branch
    normed2, second_norm_vjp = jax.vjp(rms_norm, hidden, gain_second)
    normed_second = normed2.astype(jnp.bfloat16)
    cot_b = cotangent.astype(jnp.bfloat16)
    gate_whole, down_rows = (
        lax.all_gather(gate_up, "wsh", axis=2, tiled=True),
        lax.all_gather(down_weight, "wsh", axis=0, tiled=True),
    )
    gate_cols = gate_whole[0]
    up_cols = gate_whole[1]
    gate_part = jnp.dot(normed_second, gate_cols, preferred_element_type=jnp.float32)
    up_part = jnp.dot(normed_second, up_cols, preferred_element_type=jnp.float32)
    mlp_act = (jax.nn.silu(gate_part) * up_part).astype(jnp.bfloat16)
    mlp_out = jnp.dot(mlp_act, down_rows, preferred_element_type=jnp.float32)
    output = hidden + mlp_out
    down_local = matmul_t(mlp_act, cot_b)
    d_mlp = matmul_back(cot_b, down_rows)
    d_gate = (d_mlp * up_part * silu_slope(gate_part)).astype(jnp.bfloat16)
    d_up = (d_mlp * jax.nn.silu(gate_part)).astype(jnp.bfloat16)
    gate_up_local = jnp.stack(
        [matmul_t(normed_second, d_gate), matmul_t(normed_second, d_up)], axis=0
    )
    d_normed_second = matmul_back(d_gate, gate_cols) + matmul_back(d_up, up_cols)
    d_hidden_norm, d_gain_second = second_norm_vjp(d_normed_second)
    hidden_grad = cotangent + d_hidden_norm
    hidden_b = hidden_grad.astype(jnp.bfloat16)
    attend_out_grad = matmul_t(attn_b, hidden_b)
    mixer_out_grad = matmul_t(gated, hidden_b)
    d_attn_b = matmul_back(hidden_b, out_attend).astype(jnp.bfloat16)
    d_gated = matmul_back(hidden_b, out_mix)
    d_heads = d_attn_b.reshape(rows, KVH, GRP, HD)
    d_heads_f = d_heads.astype(jnp.float32)
    query_f = queries.astype(jnp.float32).reshape(rows, KVH, GRP, HD)
    delta = jnp.sum(jnp.transpose(d_heads_f, (1, 2, 0, 3)) * attn_heads, axis=-1)

    def attend_back(carry, piece, start):
        query_grad, kv_grad = carry
        count = piece.shape[0]
        keys_piece, values_piece = split_piece(piece)
        allowed = allowed_at(start, count)
        scores = (
            jnp.einsum(
                "tkgd,skd->kgts", query_heads, keys_piece, preferred_element_type=jnp.float32
            )
            * scale
        )
        probs = jnp.where(
            allowed, jnp.exp(jnp.where(allowed, scores, 0.0) - log_total[..., None]), 0.0
        )
        d_probs = jnp.einsum(
            "tkgd,skd->kgts", d_heads, values_piece, preferred_element_type=jnp.float32
        )
        d_scores = probs * (d_probs - delta[..., None]) * scale
        query_grad = query_grad + jnp.einsum(
            "kgts,skd->tkgd", d_scores, keys_piece.astype(jnp.float32), precision=HIGH
        )
        key_grad = jnp.einsum("kgts,tkgd->skd", d_scores, query_f, precision=HIGH)
        value_grad = jnp.einsum("kgts,tkgd->skd", probs, d_heads_f, precision=HIGH)
        update = jnp.concatenate(
            [key_grad.reshape(count, kv_width), value_grad.reshape(count, kv_width)], axis=1
        )
        kv_grad = lax.dynamic_update_slice_in_dim(kv_grad, update, start, 0)
        return (query_grad, kv_grad)

    back_carry = (
        jnp.zeros((rows, KVH, GRP, HD), jnp.float32),
        jnp.zeros((block_count * block_rows, 2 * kv_width), jnp.float32),
    )
    query_grad, kv_grad = in_blocks(
        attend_back, back_carry, lax.all_gather(kv_local, "ctx", axis=0, tiled=True)
    )
    d_mixer = (d_gated * jax.nn.silu(gate_z)).reshape(2, block_rows, MHEADS, HEAD_M)
    d_z = d_gated * mixer_flat * silu_slope(gate_z)
    g_heads, g_b, g_c, g_step, g_decay, g_state, g_skip = out_vjp(d_mixer)
    chain_backward = chain_fold(
        slot_block, my_blocks, block_second, first_len, block_rows, prefix, True
    )
    later_sum = chain_backward(
        zero_states,
        lax.all_gather(g_state.astype(jnp.bfloat16), "ctx", axis=0, tiled=True),
        jnp.int32(0),
    )
    d_totals = jnp.exp(emit_totals) * jnp.sum(later_sum * state_in, axis=(2, 3))
    e_heads, e_b, e_step, e_decay = emit_vjp((later_sum, d_totals))
    d_activated = jnp.concatenate(
        [(g_heads + e_heads).reshape(2, block_rows, DSSM), g_b + e_b, g_c], axis=2
    )
    d_conv_blocks, d_tails, filter_grad = conv_vjp(d_activated)
    tail_buffer = (
        jnp.zeros((block_count, KERNEL - 1, CONV), jnp.float32)
        .at[pred_slot]
        .add(d_tails * keep_tail[:, None, None])
    )
    d_step_raw, step_bias_grad, log_rate_grad = step_vjp(
        ((g_step + e_step).reshape(rows, MHEADS), (g_decay + e_decay).reshape(rows, MHEADS))
    )
    kv_mine, tail_back, gate_up_part, down_part = (
        lax.psum_scatter(
            kv_grad.astype(jnp.bfloat16), "ctx", scatter_dimension=0, tiled=True
        ).astype(jnp.float32),
        lax.psum_scatter(
            tail_buffer.astype(jnp.bfloat16), "ctx", scatter_dimension=0, tiled=True
        ).astype(jnp.float32),
        lax.psum_scatter(
            gate_up_local.astype(jnp.bfloat16), "ctx", scatter_dimension=1, tiled=True
        ).astype(jnp.float32),
        lax.psum_scatter(
            down_local.astype(jnp.bfloat16), "ctx", scatter_dimension=1, tiled=True
        ).astype(jnp.float32),
    )
    d_query = rotate(query_grad.reshape(rows, QH, HD), cosines, -sines).reshape(rows, AQ)
    d_key = rotate(kv_mine[:, :kv_width].reshape(rows, KVH, HD), cosines, -sines).reshape(
        rows, kv_width
    )
    d_attend = jnp.concatenate([d_query, d_key, kv_mine[:, kv_width:]], axis=1).astype(jnp.bfloat16)
    attend_in_grad = matmul_t(normed_first, d_attend)
    d_normed_attend = matmul_back(d_attend, in_attend)
    d_conv_blocks = d_conv_blocks.at[:, block_rows - (KERNEL - 1) :, :].add(tail_back)
    d_mixed = jnp.concatenate([d_z, d_conv_blocks.reshape(rows, CONV), d_step_raw], axis=1).astype(
        jnp.bfloat16
    )
    mixer_in_grad = matmul_t(normed_first, d_mixed)
    d_normed_mix = matmul_back(d_mixed, in_mix)
    d_tokens_norm, d_gain_first = first_norm_vjp(d_normed_mix + d_normed_attend)
    input_grad = hidden_grad + d_tokens_norm
    gains_grad = jnp.stack([d_gain_first, d_gain_second], axis=0)
    step_bias_grad, log_rate_grad, skip_grad, filter_grad = lax.psum(
        (step_bias_grad, log_rate_grad, g_skip, filter_grad), ("ctx", "wsh")
    )
    gate_up_grad, down_grad = (
        lax.psum_scatter(
            gate_up_part.astype(jnp.bfloat16), "wsh", scatter_dimension=2, tiled=True
        ).astype(jnp.float32),
        lax.psum_scatter(
            down_part.astype(jnp.bfloat16), "wsh", scatter_dimension=0, tiled=True
        ).astype(jnp.float32),
    )
    results = (
        lax.psum_scatter(gains_grad, ("ctx", "wsh"), scatter_dimension=1, tiled=True),
        lax.psum_scatter(mixer_in_grad, ("ctx", "wsh"), scatter_dimension=0, tiled=True),
        lax.psum_scatter(mixer_out_grad, ("ctx", "wsh"), scatter_dimension=1, tiled=True),
        lax.psum_scatter(attend_in_grad, ("ctx", "wsh"), scatter_dimension=0, tiled=True),
        lax.psum_scatter(attend_out_grad, ("ctx", "wsh"), scatter_dimension=1, tiled=True),
    )
    return (
        output[None],
        input_grad[None],
        results[0],
        filter_grad,
        step_bias_grad,
        log_rate_grad,
        skip_grad,
        results[1],
        results[2],
        results[3],
        results[4],
        gate_up_grad,
        down_grad,
    )


def xor_pairs(count, bits):
    return [(index, index ^ bits) for index in range(count)]


def held_order(count):
    return list(range(0, count, 2)) + list(range(1, count, 2))


def gather_ctx(values, with_far=False):
    count = lax.axis_size("ctx")
    first_core = lax.axis_index("ctx") % 2 == 0
    near_x = lax.ppermute(values, "ctx", xor_pairs(count, 2))
    near_y = lax.ppermute(values, "ctx", xor_pairs(count, 4))
    far = lax.ppermute(
        jnp.where(first_core, near_x, near_y),
        "ctx",
        [(index, index ^ (4 if index % 2 == 0 else 2)) for index in range(count)],
    )
    mine = jnp.stack([values, near_x, near_y, far], axis=0)
    other = lax.ppermute(mine, "ctx", xor_pairs(count, 1))
    whole = jnp.concatenate([mine, other], axis=0)
    return (whole, far) if with_far else whole


def scatter_ctx(parts):
    count = lax.axis_size("ctx")
    half = count // 2
    first_core = lax.axis_index("ctx") % 2 == 0
    wire = lambda piece: piece.astype(jnp.bfloat16)
    crossed = lax.ppermute(wire(parts[half:]), "ctx", xor_pairs(count, 1))
    sums = parts[:half] + crossed.astype(jnp.float32)
    own, near_x, near_y, far = [sums[place] for place in range(half)]
    passed = lax.ppermute(
        wire(far), "ctx", [(index, index ^ (2 if index % 2 == 0 else 4)) for index in range(count)]
    ).astype(jnp.float32)
    near_y = near_y + jnp.where(first_core, passed, 0.0)
    near_x = near_x + jnp.where(first_core, 0.0, passed)
    return (
        own
        + lax.ppermute(wire(near_x), "ctx", xor_pairs(count, 2)).astype(jnp.float32)
        + lax.ppermute(wire(near_y), "ctx", xor_pairs(count, 4)).astype(jnp.float32)
    )


def trade_ctx(parts):
    return lax.all_to_all(parts, "ctx", 0, 0, tiled=True)


def after(values, anchor):
    return lax.optimization_barrier((values, anchor))[0]


def swap_groups(pieces):
    count = lax.axis_size("wsh")
    return [pieces[0]] + [
        lax.ppermute(pieces[k], "wsh", xor_pairs(count, k)) for k in range(1, count)
    ]


def gather_wsh(values, axis=0):
    count = lax.axis_size("wsh")
    shape = list(values.shape)
    size = shape[axis]
    shape[axis] = size * count
    whole = jnp.zeros(shape, values.dtype)
    for k, piece in enumerate(swap_groups([values] * count)):
        start = (lax.axis_index("wsh") ^ k) * size
        whole = lax.dynamic_update_slice_in_dim(whole, piece, start, axis)
    return whole


def dot_dims(left, right, left_dim, right_dim, precision=None):
    return lax.dot_general(
        left,
        right,
        (((left_dim,), (right_dim,)), ((), ())),
        precision=precision,
        preferred_element_type=jnp.float32,
    )


def spread(per_head, heads, lanes):
    return jnp.concatenate(
        [jnp.broadcast_to(item, (item.shape[0], lanes)) for item in per_head[:heads]], axis=1
    )


def turn(values, table, back=False):
    half = HD // 2
    swapped = jnp.concatenate([values[:, half:], values[:, :half]], axis=1)
    side = swapped * table[:, HD:]
    return values * table[:, :HD] - side if back else values * table[:, :HD] + side


def filtered(ext_ref, filt_ref, rows):
    conv = filt_ref[KERNEL : KERNEL + 1, :] + filt_ref[KERNEL - 1 : KERNEL, :] * ext_ref[8:, :]
    for tap in range(KERNEL - 1):
        start = 8 - (KERNEL - 1) + tap
        conv = conv + filt_ref[tap : tap + 1, :] * ext_ref[start : start + rows, :]
    return conv


def softplus(values):
    return jnp.maximum(values, 0.0) + jnp.log1p(jnp.exp(-jnp.abs(values)))


def block_decay(step_in, rate, rows):
    step = softplus(step_in)
    decay = -step * rate
    lower = lax.broadcasted_iota(jnp.int32, (rows, rows), 0) >= lax.broadcasted_iota(
        jnp.int32, (rows, rows), 1
    )
    ones = jnp.where(lower, 1.0, 0.0)
    cum = dot_dims(ones, decay, 1, 0, HIGH)
    cum_t = dot_dims(decay, ones, 0, 1, HIGH)
    return step, decay, lower, ones, cum, cum_t


def pick_kernel(heads, where_ref, *refs):
    xs, zs = refs[:heads], refs[heads : 2 * heads]
    bc0, step0, q0, k0, v0, gain_ref, out_ref = refs[2 * heads :]
    chans = heads * HEAD_M
    ctx = where_ref[0]
    gain = gain_ref[0:1, :].astype(jnp.float32)
    width = gain.shape[1]

    def put(start, values):
        scaled = values.astype(jnp.float32) * gain
        out_ref[start : start + values.shape[0], :] = scaled.astype(jnp.bfloat16)

    def half_tile(ref, odd):
        window = jnp.transpose(ref[...].astype(jnp.float32))
        return jnp.where(odd, window[HD:, :], window[:HD, :])

    for h in range(heads):
        put(h * HEAD_M, xs[h][...])
        put(256 + h * HEAD_M, zs[h][...])
    put(chans, half_tile(q0, ctx % 2 == 1))
    put(256 + chans, half_tile(k0, where_ref[1] % 2 == 1))
    put(512, bc0[...])
    put(768, half_tile(v0, where_ref[1] % 2 == 1))
    row = lax.broadcasted_iota(jnp.int32, (HEAD_M, width), 0)
    steps = jnp.where(row < MHEADS, step0[...].astype(jnp.float32), 0.0).astype(jnp.bfloat16)
    there = lax.broadcasted_iota(jnp.int32, (HEAD_M, HEAD_M), 0)
    here = lax.broadcasted_iota(jnp.int32, (HEAD_M, HEAD_M), 1)
    chosen = jnp.where((here == there + ctx * heads) & (there < heads), 1.0, 0.0)
    put(768 + HD, dot_dims(chosen.astype(jnp.bfloat16), steps, 1, 0))
    turn_row = lax.broadcasted_iota(jnp.int32, (16, width), 0)
    second = gain_ref[1:2, :].astype(jnp.float32)
    both = jnp.where(turn_row == 0, gain, jnp.where(turn_row == 1, second, 0.0))
    out_ref[GAIN_ROW : GAIN_ROW + 16, :] = both.astype(jnp.bfloat16)


def pick_columns(where, mixer_in, attend_in, gains, heads):
    width = mixer_in.shape[0]
    turned = jnp.transpose(mixer_in)
    rows_at = lambda start: pl.BlockSpec((HEAD_M, width), lambda i, s: (start(s) // HEAD_M, 0))
    tile_at = lambda start: pl.BlockSpec((width, 128), lambda i, s: (0, start(s) // 128))
    from_x = [rows_at(lambda s, h=h: DSSM + (s[0] * heads + h) * HEAD_M) for h in range(heads)]
    from_z = [rows_at(lambda s, h=h: (s[0] * heads + h) * HEAD_M) for h in range(heads)]
    return pl.pallas_call(
        partial(pick_kernel, heads),
        out_shape=jax.ShapeDtypeStruct((896, width), jnp.bfloat16),
        grid_spec=pltpu.PrefetchScalarGridSpec(
            num_scalar_prefetch=1,
            grid=(1,),
            in_specs=from_x
            + from_z
            + [
                pl.BlockSpec((2 * NSTATE, width), lambda i, s: (DSSM // NSTATE, 0)),
                rows_at(lambda s: DSSM + CONV),
                tile_at(lambda s: s[0] * HD),
                tile_at(lambda s: AQ + s[1] * HD),
                tile_at(lambda s: AQ + KVH * HD + s[1] * HD),
                pl.BlockSpec(gains.shape, lambda i, s: (0, 0)),
            ],
            out_specs=pl.BlockSpec((896, width), lambda i, s: (0, 0)),
        ),
        name="pick_columns",
    )(where, *[turned] * (2 * heads + 2), *[attend_in] * 3, gains)


def finish_in_kernel(heads, final_ref, mixer_ref, attend_ref, last_ref):
    count = final_ref.shape[0]
    chans = heads * HEAD_M
    share = final_ref.shape[1]
    parts = [final_ref[c].astype(jnp.float32) for c in range(count)]
    beside = lambda start, size: jnp.concatenate([p[:, start : start + size] for p in parts], axis=1)
    mixer_ref[:, :DSSM] = beside(256, chans)
    mixer_ref[:, DSSM : 2 * DSSM] = beside(0, chans)
    mixer_ref[:, 2 * DSSM : 2 * DSSM + 2 * NSTATE] = sum(p[:, 512:768] for p in parts)
    lane = lax.broadcasted_iota(jnp.int32, (128, MHEADS), 0)
    head = lax.broadcasted_iota(jnp.int32, (128, MHEADS), 1)
    steps = jnp.zeros((share, MHEADS), jnp.float32)
    for c in range(count):
        chosen = jnp.where((lane - HD == head - c * heads) & (lane >= HD) & (lane < HD + heads), 1.0, 0.0)
        steps = steps + dot_dims(final_ref[c, :, 768:896], chosen.astype(jnp.bfloat16), 1, 0)
    mixer_ref[:, DSSM + CONV :] = steps
    attend_ref[:, :AQ] = beside(chans, HD)
    each = count // KVH
    for start, place in ((256 + chans, AQ), (768, AQ + KVH * HD)):
        attend_ref[:, place : place + KVH * HD] = jnp.concatenate(
            [
                sum(p[:, start : start + HD] for p in parts[head_ * each : (head_ + 1) * each])
                for head_ in range(KVH)
            ],
            axis=1,
        )
    last_ref[...] = sum(p[:, 768:896] for p in parts)


def finish_in(final, heads):
    share = final.shape[1]
    return pl.pallas_call(
        partial(finish_in_kernel, heads),
        out_shape=(
            jax.ShapeDtypeStruct((share, DSSM + CONV + MHEADS), jnp.float32),
            jax.ShapeDtypeStruct((share, AQ + 2 * KVH * HD), jnp.float32),
            jax.ShapeDtypeStruct((share, 128), jnp.float32),
        ),
        name="finish_in",
    )(final)


def finish_rest_kernel(chans, units, share, parts_ref, gate_up_ref, down_ref, mixer_ref, attend_ref):
    count = parts_ref.shape[0]
    parts = [parts_ref[c].astype(jnp.float32) for c in range(count)]
    for place in range(2):
        gate_up_ref[place] = jnp.concatenate(
            [jnp.transpose(p[place * units : (place + 1) * units]) for p in parts], axis=1
        )
    outs = []
    for c, p in enumerate(parts):
        down_ref[c * units : (c + 1) * units, :] = p[2 * units : 3 * units]
        rest = range(3 * units, p.shape[0], share)
        outs.append(jnp.concatenate([p[start : start + share] for start in rest], axis=1))
    mixer_ref[...] = jnp.concatenate([item[:, :chans] for item in outs], axis=1)
    attend_ref[...] = jnp.concatenate([item[:, chans:] for item in outs], axis=1)


def finish_rest(parts, chans, units, share):
    count, _, wide = parts.shape
    return pl.pallas_call(
        partial(finish_rest_kernel, chans, units, share),
        out_shape=(
            jax.ShapeDtypeStruct((2, wide, count * units), jnp.float32),
            jax.ShapeDtypeStruct((count * units, wide), jnp.float32),
            jax.ShapeDtypeStruct((share, count * chans), jnp.float32),
            jax.ShapeDtypeStruct((share, count * HD), jnp.float32),
        ),
        name="finish_rest",
    )(parts)


def forward_kernel(
    heads, base, sched_ref, proj_ref, filt_ref, table_ref, params_ref, skip_ref,
    held_ref, save_ref, state_ref, kv_ref, ext_ref, chain_ref, keys_ref, values_ref,
):
    index = pl.program_id(0)
    blocks = pl.num_programs(0)
    rows = proj_ref.shape[1]
    chans = heads * HEAD_M
    seq_start = sched_ref[blocks + index]

    @pl.when(index == 0)
    def _():
        keys_ref[...] = jnp.zeros_like(keys_ref)
        values_ref[...] = jnp.zeros_like(values_ref)

    @pl.when(seq_start == index * rows)
    def _():
        ext_ref[0:8, :] = jnp.zeros((8, ext_ref.shape[1]), jnp.float32)
        chain_ref[...] = jnp.zeros_like(chain_ref)

    proj = proj_ref[0]
    ext_ref[8:, :] = jnp.concatenate([proj[:, :256], proj[:, 512:768]], axis=1)
    conv = filtered(ext_ref, filt_ref, rows)
    ext_ref[0:8, :] = ext_ref[rows:, :]
    act = conv * jax.nn.sigmoid(conv)
    heads_x = act[:, :chans]
    b_in = act[:, 256 : 256 + NSTATE]
    c_in = act[:, 256 + NSTATE : 256 + 2 * NSTATE]
    step, _, lower, _, cum, cum_t = block_decay(
        proj[:, 768:] + params_ref[0:1, :], params_ref[1:2, :], rows
    )
    cum_cols = [cum[:, base + h : base + h + 1] for h in range(heads)]
    mix = dot_dims(c_in, b_in, 1, 1, SSD)
    fed = heads_x * spread([step[:, base + h : base + h + 1] for h in range(heads)], heads, HEAD_M)
    state = chain_ref[...]
    state_ref[0] = state
    inner = []
    for h in range(heads):
        gaps = jnp.where(lower, cum_cols[h] - cum_t[base + h : base + h + 1, :], 0.0)
        kernel = jnp.where(lower, jnp.exp(gaps), 0.0) * mix
        inner.append(dot_dims(kernel, fed[:, h * HEAD_M : (h + 1) * HEAD_M], 1, 0, SSD))
    growth = spread([jnp.exp(item) for item in cum_cols], heads, HEAD_M)
    inner = jnp.concatenate(inner, axis=1) + dot_dims(c_in, state, 1, 1, SSD) * growth
    ends = [item[rows - 1 : rows, :] for item in cum_cols]
    tail = spread([jnp.exp(end - item) for end, item in zip(ends, cum_cols)], heads, HEAD_M)
    emitted = dot_dims(fed * tail, b_in, 0, 0, SSD)
    for h in range(heads):
        part = slice(h * HEAD_M, (h + 1) * HEAD_M)
        chain_ref[part, :] = jnp.exp(ends[h]) * state[part, :] + emitted[part, :]
    gate_z = proj[:, 256 : 256 + chans]
    gated = (inner + skip_ref[0:1, :] * heads_x) * (gate_z * jax.nn.sigmoid(gate_z))

    table = table_ref[0]
    query = turn(proj[:, chans : chans + HD], table).astype(jnp.bfloat16)
    key = turn(proj[:, 256 + chans : 256 + chans + HD], table).astype(jnp.bfloat16)
    value = proj[:, 768 : 768 + HD].astype(jnp.bfloat16)
    here = pl.ds(pl.multiple_of(index * rows, rows), rows)
    keys_ref[here, :] = key
    values_ref[here, :] = value
    kv_ref[0] = jnp.concatenate([key, value], axis=1)
    total = keys_ref.shape[0]
    key_pos = lax.broadcasted_iota(jnp.int32, (rows, total), 1)
    my_pos = index * rows + lax.broadcasted_iota(jnp.int32, (rows, total), 0)
    allowed = (key_pos <= my_pos) & (key_pos >= seq_start)
    scores = jnp.where(
        allowed, dot_dims(query, keys_ref[...], 1, 1) * (1.0 / math.sqrt(HD)), NEG_LARGE
    )
    top = jnp.max(scores, axis=-1, keepdims=True)
    weights = jnp.exp(scores - top)
    denominator = jnp.sum(weights, axis=-1, keepdims=True)
    attn = dot_dims(weights.astype(jnp.bfloat16), values_ref[...], 1, 0) / denominator
    log_total = jnp.broadcast_to(top + jnp.log(denominator), (rows, 128))
    save_ref[0] = jnp.concatenate([inner, attn, log_total], axis=1)
    held_ref[0] = jnp.concatenate([gated, attn], axis=1).astype(jnp.bfloat16)


def backward_kernel(
    heads, base, sched_ref, proj_ref, before_ref, filt_ref, table_ref, params_ref, skip_ref,
    save_ref, state_ref, kv_ref, d_mix_ref,
    d_ref, filt_grad_ref, head_grad_ref, ext_ref, next_ref, later_ref, keys_ref, values_ref,
):
    blocks = pl.num_programs(0)
    turn_index = pl.program_id(0)
    index = blocks - 1 - turn_index
    rows = proj_ref.shape[1]
    chans = heads * HEAD_M
    seq_start = sched_ref[blocks + index]
    after = jnp.minimum(index + 1, blocks - 1)
    is_end = (index == blocks - 1) | (sched_ref[blocks + after] == after * rows)

    @pl.when(turn_index == 0)
    def _():
        keys_ref[...] = jnp.zeros_like(keys_ref)
        values_ref[...] = jnp.zeros_like(values_ref)
        filt_grad_ref[...] = jnp.zeros_like(filt_grad_ref)
        head_grad_ref[...] = jnp.zeros_like(head_grad_ref)

    @pl.when(is_end)
    def _():
        next_ref[rows:, :] = jnp.zeros((8, next_ref.shape[1]), jnp.float32)
        later_ref[...] = jnp.zeros_like(later_ref)

    proj = proj_ref[0]
    keep = jnp.where(seq_start == index * rows, 0.0, 1.0)
    before = before_ref[0]
    ext_ref[0:8, :] = jnp.concatenate([before[:, :256], before[:, 512:768]], axis=1) * keep
    ext_ref[8:, :] = jnp.concatenate([proj[:, :256], proj[:, 512:768]], axis=1)
    conv = filtered(ext_ref, filt_ref, rows)
    conv_sig = jax.nn.sigmoid(conv)
    act = conv * conv_sig
    heads_x = act[:, :chans]
    b_in = act[:, 256 : 256 + NSTATE]
    c_in = act[:, 256 + NSTATE : 256 + 2 * NSTATE]
    step_in = proj[:, 768:] + params_ref[0:1, :]
    rate = params_ref[1:2, :]
    step, decay, lower, ones, cum, cum_t = block_decay(step_in, rate, rows)
    cum_cols = [cum[:, base + h : base + h + 1] for h in range(heads)]
    step_cols = spread([step[:, base + h : base + h + 1] for h in range(heads)], heads, HEAD_M)
    mix = dot_dims(c_in, b_in, 1, 1, SSD)
    fed = heads_x * step_cols
    state = state_ref[0]
    later = later_ref[...]
    save = save_ref[0]
    inner = save[:, :chans]
    skip = skip_ref[0:1, :]

    d_mix = d_mix_ref[0]
    d_gated = d_mix[:, :chans]
    gate_z = proj[:, 256 : 256 + chans]
    gate_sig = jax.nn.sigmoid(gate_z)
    d_z = d_gated * (inner + skip * heads_x) * (gate_sig * (1.0 + gate_z * (1.0 - gate_sig)))
    d_y = d_gated * (gate_z * gate_sig)
    growth = spread([jnp.exp(item) for item in cum_cols], heads, HEAD_M)
    ends = [item[rows - 1 : rows, :] for item in cum_cols]
    tail = spread([jnp.exp(end - item) for end, item in zip(ends, cum_cols)], heads, HEAD_M)
    grown = d_y * growth
    fed_tail = fed * tail
    fed_inner = []
    d_mixing = jnp.zeros((rows, rows), jnp.float32)
    for h in range(heads):
        part = slice(h * HEAD_M, (h + 1) * HEAD_M)
        gaps = jnp.where(lower, cum_cols[h] - cum_t[base + h : base + h + 1, :], 0.0)
        decays = jnp.where(lower, jnp.exp(gaps), 0.0)
        fed_inner.append(dot_dims(decays * mix, d_y[:, part], 0, 0, SSD))
        d_mixing = d_mixing + dot_dims(d_y[:, part], fed[:, part], 1, 1, SSD) * decays
    fed_emit = dot_dims(b_in, later, 1, 1, SSD) * tail
    d_fed = jnp.concatenate(fed_inner, axis=1) + fed_emit
    d_c = dot_dims(d_mixing, b_in, 1, 0, SSD) + dot_dims(grown, state, 1, 0, SSD)
    d_b = dot_dims(d_mixing, c_in, 0, 0, SSD) + dot_dims(fed_tail, later, 1, 0, SSD)
    state_grad = dot_dims(grown, c_in, 0, 0, SSD)
    d_x = d_fed * step_cols + skip * d_y
    lane = lax.broadcasted_iota(jnp.int32, (1, 128), 1)
    d_cum = jnp.zeros((rows, 128), jnp.float32)
    d_step = jnp.zeros((rows, 128), jnp.float32)
    d_total = jnp.zeros((1, 128), jnp.float32)
    skip_sum = jnp.zeros((1, 128), jnp.float32)
    cum_terms = d_y * inner - fed * d_fed
    step_terms = d_fed * heads_x
    emit_terms = fed * fed_emit
    skip_terms = d_y * heads_x
    carry_terms = later * state
    for h in range(heads):
        part = slice(h * HEAD_M, (h + 1) * HEAD_M)
        mine = jnp.where(lane == base + h, 1.0, 0.0)
        growth_end = jnp.exp(ends[h])
        d_cum = d_cum + jnp.sum(cum_terms[:, part], axis=1, keepdims=True) * mine
        d_step = d_step + jnp.sum(step_terms[:, part], axis=1, keepdims=True) * mine
        carry = jnp.sum(jnp.sum(carry_terms[part, :], axis=0, keepdims=True), axis=1, keepdims=True)
        emit = jnp.sum(jnp.sum(emit_terms[:, part], axis=0, keepdims=True), axis=1, keepdims=True)
        skips = jnp.sum(jnp.sum(skip_terms[:, part], axis=0, keepdims=True), axis=1, keepdims=True)
        d_total = d_total + (growth_end * carry + emit) * mine
        skip_sum = skip_sum + skips * mine
        later_ref[part, :] = state_grad[part, :] + growth_end * later[part, :]
    d_decay = dot_dims(ones, d_cum, 0, 0, HIGH) + d_total
    d_step = (d_step - d_decay * rate) * jax.nn.sigmoid(step_in)
    d_step = jnp.where((lane >= base) & (lane < base + heads), d_step, 0.0)
    head_grad_ref[0:1, :] += jnp.sum(d_step, axis=0, keepdims=True)
    head_grad_ref[1:2, :] += jnp.sum(d_decay * decay, axis=0, keepdims=True)
    head_grad_ref[2:3, :] += skip_sum

    d_conv = jnp.concatenate([d_x, jnp.zeros((rows, 256 - chans), jnp.float32), d_b, d_c], axis=1)
    d_conv = d_conv * (conv_sig * (1.0 + conv * (1.0 - conv_sig)))
    next_ref[0:rows, :] = d_conv
    d_in = filt_ref[KERNEL - 1 : KERNEL, :] * d_conv
    for tap in range(KERNEL - 1):
        shift = KERNEL - 1 - tap
        d_in = d_in + filt_ref[tap : tap + 1, :] * next_ref[shift : shift + rows, :]
        filt_grad_ref[tap : tap + 1, :] += jnp.sum(
            d_conv * ext_ref[8 - shift : 8 - shift + rows, :], axis=0, keepdims=True
        )
    filt_grad_ref[KERNEL - 1 : KERNEL, :] += jnp.sum(d_conv * ext_ref[8:, :], axis=0, keepdims=True)
    filt_grad_ref[KERNEL : KERNEL + 1, :] += jnp.sum(d_conv, axis=0, keepdims=True)
    next_ref[rows:, :] = d_conv[0:8, :]

    table = table_ref[0]
    scale = 1.0 / math.sqrt(HD)
    query = turn(proj[:, chans : chans + HD], table).astype(jnp.bfloat16)
    keys = kv_ref[:, :HD]
    values = kv_ref[:, HD:]
    d_attn = d_mix[:, chans : chans + HD].astype(jnp.bfloat16)
    delta = jnp.sum(d_attn.astype(jnp.float32) * save[:, chans : chans + HD], axis=1, keepdims=True)
    total = keys.shape[0]
    key_pos = lax.broadcasted_iota(jnp.int32, (rows, total), 1)
    my_pos = index * rows + lax.broadcasted_iota(jnp.int32, (rows, total), 0)
    allowed = (key_pos <= my_pos) & (key_pos >= seq_start)
    scores = jnp.where(allowed, dot_dims(query, keys, 1, 1) * scale, NEG_LARGE)
    probs = jnp.exp(scores - save[:, chans + HD : chans + HD + 1])
    d_scores = (probs * (dot_dims(d_attn, values, 1, 1) - delta) * scale).astype(jnp.bfloat16)
    d_query = turn(dot_dims(d_scores, keys, 1, 0), table, back=True)
    keys_ref[...] += dot_dims(d_scores, query, 0, 0)
    values_ref[...] += dot_dims(probs.astype(jnp.bfloat16), d_attn, 0, 0)
    here = pl.ds(pl.multiple_of(index * rows, rows), rows)
    d_key = turn(keys_ref[here, :], table, back=True)
    d_value = values_ref[here, :]
    d_ref[0] = jnp.concatenate(
        [d_in[:, :chans], d_query, d_z, d_key, d_in[:, 256:], d_value, d_step[:, HD:]], axis=1
    ).astype(jnp.bfloat16)


def mixer_forward(sched, proj, filt, table, params, skip, heads, base):
    blocks, rows, wide = proj.shape
    chans = heads * HEAD_M
    held = lambda b, s: (s[b], 0, 0)
    plain = lambda b, s: (b, 0, 0)
    whole = lambda b, s: (0, 0)
    return pl.pallas_call(
        partial(forward_kernel, heads, base),
        out_shape=(
            jax.ShapeDtypeStruct((blocks, rows, 256), jnp.bfloat16),
            jax.ShapeDtypeStruct((blocks, rows, 384), jnp.float32),
            jax.ShapeDtypeStruct((blocks, chans, NSTATE), jnp.float32),
            jax.ShapeDtypeStruct((blocks, rows, 2 * HD), jnp.bfloat16),
        ),
        grid_spec=pltpu.PrefetchScalarGridSpec(
            num_scalar_prefetch=1,
            grid=(blocks,),
            in_specs=[
                pl.BlockSpec((1, rows, wide), held),
                pl.BlockSpec(filt.shape, whole),
                pl.BlockSpec((1, rows, 2 * HD), plain),
                pl.BlockSpec(params.shape, whole),
                pl.BlockSpec(skip.shape, whole),
            ],
            out_specs=(
                pl.BlockSpec((1, rows, 256), held),
                pl.BlockSpec((1, rows, 384), plain),
                pl.BlockSpec((1, chans, NSTATE), plain),
                pl.BlockSpec((1, rows, 2 * HD), plain),
            ),
            scratch_shapes=[
                pltpu.VMEM((rows + 8, 512), jnp.float32),
                pltpu.VMEM((chans, NSTATE), jnp.float32),
                pltpu.VMEM((blocks * rows, HD), jnp.bfloat16),
                pltpu.VMEM((blocks * rows, HD), jnp.bfloat16),
            ],
        ),
        cost_estimate=pl.CostEstimate(
            flops=25_000_000_000, transcendentals=0, bytes_accessed=12_000_000
        ),
        name="mixer_forward",
    )(sched, proj, filt, table, params, skip)


def mixer_backward(sched, proj, filt, table, params, skip, save, states, kv, d_mix, heads, base):
    blocks, rows, wide = proj.shape
    chans = heads * HEAD_M
    held = lambda i, s: (s[blocks - 1 - i], 0, 0)
    before = lambda i, s: (s[jnp.maximum(blocks - 2 - i, 0)], rows // 8 - 1, 0)
    plain = lambda i, s: (blocks - 1 - i, 0, 0)
    whole = lambda i, s: (0, 0)
    return pl.pallas_call(
        partial(backward_kernel, heads, base),
        out_shape=(
            jax.ShapeDtypeStruct((blocks, rows, wide), jnp.bfloat16),
            jax.ShapeDtypeStruct((8, 512), jnp.float32),
            jax.ShapeDtypeStruct((8, 128), jnp.float32),
        ),
        grid_spec=pltpu.PrefetchScalarGridSpec(
            num_scalar_prefetch=1,
            grid=(blocks,),
            in_specs=[
                pl.BlockSpec((1, rows, wide), held),
                pl.BlockSpec((1, 8, wide), before),
                pl.BlockSpec(filt.shape, whole),
                pl.BlockSpec((1, rows, 2 * HD), plain),
                pl.BlockSpec(params.shape, whole),
                pl.BlockSpec(skip.shape, whole),
                pl.BlockSpec((1, rows, 384), plain),
                pl.BlockSpec((1, chans, NSTATE), plain),
                pl.BlockSpec((blocks * rows, 2 * HD), whole),
                pl.BlockSpec((1, rows, 256), held),
            ],
            out_specs=(
                pl.BlockSpec((1, rows, wide), held),
                pl.BlockSpec((8, 512), whole),
                pl.BlockSpec((8, 128), whole),
            ),
            scratch_shapes=[
                pltpu.VMEM((rows + 8, 512), jnp.float32),
                pltpu.VMEM((rows + 8, 512), jnp.float32),
                pltpu.VMEM((chans, NSTATE), jnp.float32),
                pltpu.VMEM((blocks * rows, HD), jnp.float32),
                pltpu.VMEM((blocks * rows, HD), jnp.float32),
            ],
        ),
        cost_estimate=pl.CostEstimate(
            flops=40_000_000_000, transcendentals=0, bytes_accessed=16_000_000
        ),
        name="mixer_backward",
    )(sched, proj, proj, filt, table, params, skip, save, states, kv.reshape(-1, 2 * HD), d_mix)


def head_plan(
    block_input,
    out_cotangent,
    lengths,
    slot_block,
    norm_gains,
    short_filter,
    step_bias,
    log_rate,
    skip_gain,
    mixer_in,
    mixer_out,
    attend_in,
    attend_out,
    gate_up,
    down_weight,
):
    count = lax.axis_size("ctx")
    groups = lax.axis_size("wsh")
    ctx = lax.axis_index("ctx")
    wsh = lax.axis_index("wsh")
    rows, width = block_input.shape[1:]
    block_rows = rows // 2
    blocks = 2 * count
    total_rows = count * rows
    heads = MHEADS // count
    chans = heads * HEAD_M
    kv_head = ctx * KVH // count
    units = gate_up.shape[2] // count
    first_len = lengths[0, 0]
    tokens = block_input[0]
    cotangent = out_cotangent[0]
    cols = lambda array, start, size: lax.dynamic_slice_in_dim(array, start, size, array.ndim - 1)
    base = HD
    step_pad = 128 - base - heads

    in_cols = pick_columns(
        jnp.stack([ctx, kv_head]), mixer_in, attend_in, norm_gains, heads
    )
    in_all = gather_wsh(in_cols, 1)
    gains = in_all[GAIN_ROW : GAIN_ROW + 2].astype(jnp.float32)
    out_rows = jnp.concatenate(
        [
            lax.dynamic_slice_in_dim(mixer_out, ctx * chans, chans, 0),
            lax.dynamic_slice_in_dim(attend_out, ctx * HD, HD, 0),
        ],
        axis=0,
    )
    mlp_pack = jnp.concatenate(
        [
            jnp.transpose(cols(gate_up[0], ctx * units, units)),
            jnp.transpose(cols(gate_up[1], ctx * units, units)),
            lax.dynamic_slice_in_dim(down_weight, ctx * units, units, 0),
        ],
        axis=0,
    )
    out_rows, mlp_pack = after((out_rows, mlp_pack), in_all)
    out_mine = gather_wsh(out_rows, 1)
    packs = swap_groups([mlp_pack] * groups)
    gate_up_rows = jnp.concatenate(
        [pack[:units] for pack in packs] + [pack[units : 2 * units] for pack in packs], axis=0
    )
    down_all = jnp.concatenate([pack[2 * units :] for pack in packs], axis=0)

    peers = ctx ^ jnp.array(held_order(count), dtype=jnp.int32)
    held = jnp.take(slot_block.reshape(count, 2), peers, axis=0, mode="clip").reshape(blocks)
    logical_ids = jnp.arange(blocks, dtype=jnp.int32)

    place = jnp.sum(
        jnp.where(held[None, :] == logical_ids[:, None], logical_ids[None, :], 0), axis=1
    )
    starts = jnp.where(logical_ids * block_rows >= first_len, first_len, 0)
    sched = jnp.concatenate([place, starts])
    positions = jnp.arange(total_rows, dtype=jnp.int32)
    seq_pos = positions - jnp.where(positions >= first_len, first_len, 0)
    half = HD // 2
    freqs = jnp.exp(jnp.arange(half, dtype=jnp.float32) * (-2.0 * math.log(ROPE_BASE) / HD))
    angles = seq_pos.astype(jnp.float32)[:, None] * freqs[None, :]
    cosines = jnp.cos(angles)
    sines = jnp.sin(angles)
    table = jnp.concatenate([cosines, cosines, -sines, sines], axis=1)
    table = table.reshape(blocks, block_rows, 2 * HD)
    filt = jnp.concatenate(
        [
            cols(short_filter, ctx * chans, chans),
            jnp.zeros((KERNEL + 1, HD), jnp.float32),
            short_filter[:, DSSM:],
        ],
        axis=1,
    )
    filt = jnp.pad(filt, ((0, 7 - KERNEL), (0, 0)))
    mine = lambda array: lax.dynamic_slice_in_dim(array, ctx * heads, heads)
    params = jnp.stack([mine(step_bias), jnp.exp(mine(log_rate))], axis=0)
    params = jnp.pad(params, ((0, 6), (base, 128 - base - heads)))
    skip = jnp.broadcast_to(jnp.repeat(mine(skip_gain), HEAD_M)[None, :], (8, chans))

    tokens = after(tokens, in_cols)
    first_scale = lax.rsqrt(jnp.mean(tokens * tokens, axis=-1, keepdims=True) + EPS)
    unit_tokens = tokens * first_scale
    units_first = gather_ctx(unit_tokens.astype(jnp.bfloat16)).reshape(total_rows, width)
    units_t = lax.optimization_barrier(jnp.transpose(units_first))
    cot_all = gather_ctx(after(cotangent.astype(jnp.bfloat16), units_first))
    cot_all = cot_all.reshape(total_rows, width)
    projected = matmul_back(units_first, in_all).reshape(blocks, block_rows, in_all.shape[0])
    mixed_held, saved, states, kv = mixer_forward(
        sched, projected, filt, table, params, skip, heads, base
    )
    mixed_held = mixed_held.reshape(total_rows, chans + HD)

    hidden = tokens + scatter_ctx(
        jnp.dot(mixed_held, out_mine, preferred_element_type=jnp.float32).reshape(
            count, rows, width
        )
    )

    second_scale = lax.rsqrt(jnp.mean(hidden * hidden, axis=-1, keepdims=True) + EPS)
    unit_hidden = hidden * second_scale
    normed_second = gather_ctx((unit_hidden * gains[1]).astype(jnp.bfloat16)).reshape(
        total_rows, width
    )
    both = matmul_back(normed_second, gate_up_rows)
    gate_part = both[:, : groups * units]
    up_part = both[:, groups * units :]
    silu_gate = jax.nn.silu(gate_part)
    mlp_act = (silu_gate * up_part).astype(jnp.bfloat16)
    d_mlp = matmul_back(cot_all, down_all)
    d_gate = (d_mlp * up_part * silu_slope(gate_part)).astype(jnp.bfloat16)
    d_up = (d_mlp * silu_gate).astype(jnp.bfloat16)
    d_both = jnp.concatenate([d_gate, d_up], axis=1)
    d_normed_second = scatter_ctx(
        jnp.dot(d_both, gate_up_rows, preferred_element_type=jnp.float32).reshape(
            count, rows, width
        )
    )

    def norm_back(d_normed, gain, unit, unit_scale):
        scaled = d_normed * gain
        return unit_scale * (scaled - unit * jnp.mean(scaled * unit, axis=-1, keepdims=True))

    hidden_grad = cotangent + norm_back(d_normed_second, gains[1], unit_hidden, second_scale)
    hidden_b, hidden_far = gather_ctx(hidden_grad.astype(jnp.bfloat16), True)
    hidden_b = hidden_b.reshape(total_rows, width)

    both_grad = matmul_t(d_both, normed_second)
    down_local = matmul_t(mlp_act, cot_all)
    gain_second_grad = jnp.sum(both_grad * gate_up_rows.astype(jnp.float32), axis=0) / gains[1]
    inner_units = groups * units
    mlp_grads = [
        jnp.concatenate(
            [
                both_grad[k * units : (k + 1) * units],
                both_grad[inner_units + k * units : inner_units + (k + 1) * units],
                down_local[k * units : (k + 1) * units],
            ],
            axis=0,
        ).astype(jnp.bfloat16)
        for k in range(groups)
    ]
    mlp_swapped = swap_groups(mlp_grads)
    mlp_sum = sum(piece.astype(jnp.float32) for piece in mlp_swapped)
    mlp_sum = jnp.transpose(
        mlp_sum.astype(jnp.bfloat16).reshape(3 * units, count, width // count), (1, 0, 2)
    )

    d_mix = matmul_back(hidden_b, out_mine).reshape(blocks, block_rows, chans + HD)
    share = width // (count * groups)

    def to_groups(grad):
        parts = grad.reshape(count, groups, share, grad.shape[1])
        return [
            lax.dynamic_index_in_dim(parts, wsh ^ k, 1, keepdims=False).astype(jnp.bfloat16)
            for k in range(groups)
        ]

    places = jnp.array([held_order(count).index(k) for k in range(count)], dtype=jnp.int32)
    by_device = jnp.take(places, ctx ^ jnp.arange(count, dtype=jnp.int32), mode="clip")
    act_by_device = jnp.take(
        mlp_act.reshape(count, rows, inner_units), by_device, axis=0, mode="clip"
    ).reshape(total_rows, inner_units)
    mlp_parts = jnp.dot(act_by_device, down_all, preferred_element_type=jnp.float32)
    mlp_parts = mlp_parts.astype(jnp.bfloat16).reshape(count, rows, width)
    mlp_parts = after(mlp_parts, hidden_far)
    mlp_parts = trade_ctx(mlp_parts)
    output = hidden + jnp.sum(mlp_parts.astype(jnp.float32), axis=0)
    out_grads = to_groups(matmul_t(hidden_b, mixed_held))
    out_swapped = swap_groups(out_grads)
    out_sum = sum(piece.astype(jnp.float32) for piece in out_swapped)
    d_held, filt_grad, head_grad = mixer_backward(
        sched, projected, filt, table, params, skip, saved, states, kv, d_mix, heads, base
    )
    out_sum = out_sum.astype(jnp.bfloat16)
    payload = jnp.concatenate(
        [mlp_sum]
        + [out_sum[:, :, start : start + 128] for start in range(0, out_sum.shape[2], 128)],
        axis=1,
    )
    payload = trade_ctx(after(payload, (mlp_parts, d_held)))
    gate_up_grad, down_grad, mixer_out_grad, attend_out_grad = finish_rest(
        payload, chans, units, share
    )
    mixer_out_grad = jnp.transpose(mixer_out_grad)
    attend_out_grad = jnp.transpose(attend_out_grad)
    d_held = d_held.reshape(total_rows, -1)
    d_unit_first = scatter_ctx(
        jnp.dot(d_held, in_all, preferred_element_type=jnp.float32).reshape(
            count, rows, width
        )
    )
    input_grad = hidden_grad + norm_back(d_unit_first, 1.0, unit_tokens, first_scale)

    in_grad = jnp.dot(units_t, d_held, preferred_element_type=jnp.float32)
    gain_first_grad = jnp.sum(in_grad * jnp.transpose(in_all).astype(jnp.float32), axis=1) / gains[0]
    in_grad = in_grad * gains[0][:, None]
    lane = jnp.arange(in_all.shape[0], dtype=jnp.int32)[None, :]
    gain_lane = in_all.shape[0] - step_pad
    in_grad = jnp.where(lane == gain_lane, gain_first_grad[:, None], in_grad)
    in_grad = jnp.where(lane == gain_lane + 1, gain_second_grad[:, None], in_grad)
    in_grads = to_groups(in_grad)
    in_swapped = swap_groups(in_grads)
    in_sum = sum(piece.astype(jnp.float32) for piece in in_swapped)
    mixer_in_grad, attend_in_grad, last_cols = finish_in(
        trade_ctx(after(in_sum.astype(jnp.bfloat16), payload)), heads
    )
    gain_place = gain_lane % 128
    gains_grad = jnp.transpose(last_cols[:, gain_place : gain_place + 2])
    side_by_side = lambda array: jnp.transpose(array, (1, 0, 2)).reshape(array.shape[1], -1)

    small = jnp.concatenate([filt_grad.reshape(-1, 128), head_grad], axis=0)
    small = gather_wsh(small[None])
    small = gather_ctx(jnp.sum(small, axis=0))
    small = jnp.take(small, by_device, axis=0, mode="clip")
    filters = small[:, :-8].reshape(count, 8, 512)[:, : KERNEL + 1]
    filter_grad = jnp.concatenate(
        [side_by_side(filters[:, :, :chans]), jnp.sum(filters[:, :, 256:], axis=0)], axis=1
    )
    per_head = small[:, -8:-5, base : base + heads]
    step_bias_all, log_rate_all, skip_all = [per_head[:, i].reshape(-1) for i in range(3)]
    return (
        output[None],
        input_grad[None],
        gains_grad,
        filter_grad,
        step_bias_all,
        log_rate_all,
        skip_all,
        mixer_in_grad,
        mixer_out_grad,
        attend_in_grad,
        attend_out_grad,
        gate_up_grad,
        down_grad,
    )


def on_device_heads(*args):
    return head_plan(*args)


def solution(mesh):
    placed = (
        P("wsh", "ctx", None),
        P("wsh", "ctx", None),
        P("wsh", None),
        P(),
        P(None, "wsh"),
        P(),
        P(),
        P(),
        P(),
        P("wsh", None),
        P(None, "wsh"),
        P("wsh", None),
        P(None, "wsh"),
        P(None, None, "wsh"),
        P("wsh", None),
    )
    per_heads = mesh.shape["ctx"] == QH
    return jax.shard_map(
        on_device_heads if per_heads else on_device,
        mesh=mesh,
        in_specs=placed,
        out_specs=(
            P("wsh", "ctx", None),
            P("wsh", "ctx", None),
            P(None, ("ctx", "wsh")),
            P(),
            P(),
            P(),
            P(),
            P(("ctx", "wsh"), None),
            P(None, ("ctx", "wsh")),
            P(("ctx", "wsh"), None),
            P(None, ("ctx", "wsh")),
            P(None, "ctx", "wsh"),
            P("wsh", "ctx"),
        ),
        check_vma=False,
    )
```

```python
import math
from functools import partial

import jax
import jax.numpy as jnp
from jax import lax
from jax.experimental import pallas as pl
from jax.experimental.pallas import tpu as pltpu
from jax.sharding import PartitionSpec as P

MHEADS = 24
HEAD_M = 64
NSTATE = 128
QH = 8
KVH = 2
HD = 64
KERNEL = 4
DSSM = 1536
CONV = 1792
AQ = 512
GRP = 4


EPS = 1e-05
ROPE_BASE = 100000000000.0
HIGH = lax.Precision.HIGHEST
SSD = None
NEG_LARGE = -1e30
GAIN_ROW = 836
SENT_ROWS = 848


def rms_norm(values, gain):
    scale = lax.rsqrt(jnp.mean(values * values, axis=-1, keepdims=True) + EPS)
    return values * scale * gain


def silu_slope(values):
    sigmoid_value = jax.nn.sigmoid(values)
    return sigmoid_value * (1.0 + values * (1.0 - sigmoid_value))


def rope_tables(positions):
    half = HD // 2
    freqs = jnp.exp(jnp.arange(half, dtype=jnp.float32) * (-2.0 * math.log(ROPE_BASE) / HD))
    angles = positions.astype(jnp.float32)[:, None] * freqs[None, :]
    return (jnp.cos(angles)[:, None, :], jnp.sin(angles)[:, None, :])


def rotate(values, cosines, sines):
    half = values.shape[-1] // 2
    first = values[..., :half]
    second = values[..., half:]
    return jnp.concatenate(
        [first * cosines - second * sines, second * cosines + first * sines], axis=-1
    )


def matmul_t(left, right):
    return lax.dot_general(
        left, right, (((0,), (0,)), ((), ())), preferred_element_type=jnp.float32
    )


def matmul_back(left, right):
    return lax.dot_general(
        left, right, (((1,), (1,)), ((), ())), preferred_element_type=jnp.float32
    )


def step_prep(step_raw, step_bias, log_rate):
    step = jax.nn.softplus(step_raw + step_bias)
    return (step, -step * jnp.exp(log_rate))


def conv_prep(conv_blocks, tails_in, filter_rows):
    count = conv_blocks.shape[1]
    extended = jnp.concatenate([tails_in, conv_blocks], axis=1)
    conv = filter_rows[KERNEL] + filter_rows[KERNEL - 1] * conv_blocks
    for tap_index in range(KERNEL - 1):
        conv = conv + filter_rows[tap_index] * extended[:, tap_index : tap_index + count]
    return jax.nn.silu(conv)


def ssd_emit(heads_x, b_in, step, log_decay):
    cumulative = jnp.cumsum(log_decay, axis=0)
    weight = jnp.exp(cumulative[-1][None, :] - cumulative) * step
    emitted = jnp.einsum("shp,sn->hpn", heads_x * weight[:, :, None], b_in, precision=HIGH)
    return (emitted, cumulative[-1])


def ssd_output(heads_x, b_in, c_in, step, log_decay, state_in, skip_gain):
    cumulative = jnp.cumsum(log_decay, axis=0)
    count = heads_x.shape[0]
    lower = (jnp.arange(count)[:, None] >= jnp.arange(count)[None, :])[:, :, None]
    gaps = jnp.where(lower, cumulative[:, None, :] - cumulative[None, :, :], 0.0)
    kernel = (
        jnp.where(lower, jnp.exp(gaps), 0.0) * jnp.dot(c_in, b_in.T, precision=HIGH)[:, :, None]
    )
    inner = jnp.einsum("tsh,shp->thp", kernel, heads_x * step[:, :, None], precision=HIGH)
    carried = (
        jnp.einsum("hpn,tn->thp", state_in, c_in, precision=HIGH) * jnp.exp(cumulative)[:, :, None]
    )
    return inner + carried + skip_gain[None, :, None] * heads_x


def chain_fold(slot_block, my_blocks, block_second, first_len, block_rows, prefix, later):

    def fold(total, piece, start):
        count = piece.shape[0]
        same = (slot_block * block_rows >= first_len)[None, :] == block_second[:, None]
        if later:
            valid = same & (slot_block[None, :] > my_blocks[:, None])
            gaps = (
                jnp.take(prefix, slot_block, axis=0)[None, :, :]
                - jnp.take(prefix, my_blocks + 1, axis=0)[:, None, :]
            )
        else:
            valid = same & (slot_block[None, :] < my_blocks[:, None])
            gaps = (
                jnp.take(prefix, my_blocks, axis=0)[:, None, :]
                - jnp.take(prefix, slot_block + 1, axis=0)[None, :, :]
            )
        factors = jnp.where(
            valid[:, :, None], jnp.exp(jnp.where(valid[:, :, None], gaps, 0.0)), 0.0
        )
        step_size = math.gcd(count, 8)

        def add_rows(index, running):
            rows_piece = lax.dynamic_slice_in_dim(piece, index * step_size, step_size).astype(
                jnp.float32
            )
            factor_rows = lax.dynamic_slice_in_dim(factors, index * step_size, step_size, 1)
            return running + jnp.einsum("bsh,shpn->bhpn", factor_rows, rows_piece, precision=HIGH)

        return lax.fori_loop(0, count // step_size, add_rows, total)

    return fold


def in_blocks(step_fn, carry, piece):
    count = piece.shape[0]
    block_size = math.gcd(count, 512)

    def visit(block_index, state):
        sub_piece = lax.dynamic_slice_in_dim(piece, block_index * block_size, block_size)
        return step_fn(state, sub_piece, block_index * block_size)

    return lax.fori_loop(0, count // block_size, visit, carry)


def on_device(
    block_input,
    out_cotangent,
    lengths,
    slot_block,
    norm_gains,
    short_filter,
    step_bias,
    log_rate,
    skip_gain,
    mixer_in,
    mixer_out,
    attend_in,
    attend_out,
    gate_up,
    down_weight,
):
    gains_all, in_mix, out_mix, in_attend, out_attend = (
        lax.all_gather(norm_gains, "wsh", axis=1, tiled=True),
        lax.all_gather(mixer_in, "wsh", axis=0, tiled=True),
        lax.all_gather(mixer_out, "wsh", axis=1, tiled=True),
        lax.all_gather(attend_in, "wsh", axis=0, tiled=True),
        lax.all_gather(attend_out, "wsh", axis=1, tiled=True),
    )
    ctx_count = lax.axis_size("ctx")
    block_count = 2 * ctx_count
    rows = block_input.shape[1]
    block_rows = rows // 2
    kv_width = KVH * HD
    scale = 1.0 / math.sqrt(HD)
    tokens = block_input[0]
    cotangent = out_cotangent[0]
    first_len = lengths[0, 0]
    logical_ids = jnp.arange(block_count, dtype=jnp.int32)
    my_blocks = lax.dynamic_slice_in_dim(slot_block, 2 * lax.axis_index("ctx"), 2)
    block_offsets = jnp.arange(block_rows, dtype=jnp.int32)
    my_pos = (my_blocks[:, None] * block_rows + block_offsets[None, :]).reshape(rows)
    my_second = my_pos >= first_len
    seq_pos = my_pos - jnp.where(my_second, first_len, 0)
    block_second = my_blocks * block_rows >= first_len
    is_start = (my_blocks == 0) | (my_blocks * block_rows == first_len)
    key_pos = (slot_block[:, None] * block_rows + block_offsets[None, :]).reshape(
        block_count * block_rows
    )
    gain_first = gains_all[0].astype(jnp.float32)
    gain_second = gains_all[1].astype(jnp.float32)
    normed, first_norm_vjp = jax.vjp(rms_norm, tokens, gain_first)
    normed_first = normed.astype(jnp.bfloat16)
    mixed = jnp.dot(normed_first, in_mix, preferred_element_type=jnp.float32)
    gate_z = mixed[:, :DSSM]
    conv_input = mixed[:, DSSM : DSSM + CONV]
    step_raw = mixed[:, DSSM + CONV :]
    (step, log_decay), step_vjp = jax.vjp(step_prep, step_raw, step_bias, log_rate)
    step_blocks = step.reshape(2, block_rows, MHEADS)
    decay_blocks = log_decay.reshape(2, block_rows, MHEADS)
    totals = jnp.sum(decay_blocks, axis=1)
    conv_blocks = conv_input.reshape(2, block_rows, CONV)
    tails = conv_blocks[:, block_rows - (KERNEL - 1) :, :]
    all_tails, all_totals = (
        lax.all_gather(tails, "ctx", axis=0, tiled=True),
        lax.all_gather(totals, "ctx", axis=0, tiled=True),
    )
    one_hot = (slot_block[None, :] == logical_ids[:, None]).astype(jnp.float32)
    totals_logical = jnp.dot(one_hot, all_totals, precision=HIGH)
    prefix = jnp.concatenate(
        [jnp.zeros((1, MHEADS), jnp.float32), jnp.cumsum(totals_logical, axis=0)], axis=0
    )
    pred_slot = jnp.sum(
        jnp.where(slot_block[None, :] == (my_blocks - 1)[:, None], logical_ids[None, :], 0), axis=1
    )
    keep_tail = jnp.where(is_start, 0.0, 1.0).astype(jnp.float32)
    tails_in = jnp.take(all_tails, pred_slot, axis=0) * keep_tail[:, None, None]
    activated, conv_vjp = jax.vjp(conv_prep, conv_blocks, tails_in, short_filter)
    heads_x = activated[:, :, :DSSM].reshape(2, block_rows, MHEADS, HEAD_M)
    b_in = activated[:, :, DSSM : DSSM + NSTATE]
    c_in = activated[:, :, DSSM + NSTATE :]
    (emitted, emit_totals), emit_vjp = jax.vjp(
        jax.vmap(ssd_emit), heads_x, b_in, step_blocks, decay_blocks
    )
    zero_states = jnp.zeros((2, MHEADS, HEAD_M, NSTATE), jnp.float32)
    chain_forward = chain_fold(
        slot_block, my_blocks, block_second, first_len, block_rows, prefix, False
    )
    state_in = chain_forward(
        zero_states,
        lax.all_gather(emitted.astype(jnp.bfloat16), "ctx", axis=0, tiled=True),
        jnp.int32(0),
    )
    mixer_y, out_vjp = jax.vjp(
        jax.vmap(ssd_output, in_axes=(0, 0, 0, 0, 0, 0, None)),
        heads_x,
        b_in,
        c_in,
        step_blocks,
        decay_blocks,
        state_in,
        skip_gain,
    )
    mixer_flat = mixer_y.reshape(rows, DSSM)
    gated = (mixer_flat * jax.nn.silu(gate_z)).astype(jnp.bfloat16)
    mixer_branch = jnp.dot(gated, out_mix, preferred_element_type=jnp.float32)
    projected = jnp.dot(normed_first, in_attend, preferred_element_type=jnp.float32)
    cosines, sines = rope_tables(seq_pos)
    queries = rotate(projected[:, :AQ].reshape(rows, QH, HD), cosines, sines).astype(jnp.bfloat16)
    keys_rot = rotate(
        projected[:, AQ : AQ + kv_width].reshape(rows, KVH, HD), cosines, sines
    ).astype(jnp.bfloat16)
    values = projected[:, AQ + kv_width :].astype(jnp.bfloat16)
    kv_local = jnp.concatenate([keys_rot.reshape(rows, kv_width), values], axis=1)
    query_heads = queries.reshape(rows, KVH, GRP, HD)

    def allowed_at(start, count):
        piece_pos = lax.dynamic_slice_in_dim(key_pos, start, count)
        return (piece_pos[None, :] <= my_pos[:, None]) & (
            (piece_pos >= first_len)[None, :] == my_second[:, None]
        )

    def split_piece(piece):
        count = piece.shape[0]
        return (
            piece[:, :kv_width].reshape(count, KVH, HD),
            piece[:, kv_width:].reshape(count, KVH, HD),
        )

    def attend_step(carry, piece, start):
        top, denominator, running = carry
        keys_piece, values_piece = split_piece(piece)
        allowed = allowed_at(start, piece.shape[0])
        scores = (
            jnp.einsum(
                "tkgd,skd->kgts", query_heads, keys_piece, preferred_element_type=jnp.float32
            )
            * scale
        )
        masked = jnp.where(allowed, scores, NEG_LARGE)
        new_top = jnp.maximum(top, jnp.max(masked, axis=-1))
        weights = jnp.where(allowed, jnp.exp(masked - new_top[..., None]), 0.0)
        factor = jnp.exp(top - new_top)
        denominator = denominator * factor + jnp.sum(weights, axis=-1)
        running = running * factor[..., None] + jnp.einsum(
            "kgts,skd->kgtd", weights, values_piece.astype(jnp.float32), precision=HIGH
        )
        return (new_top, denominator, running)

    start_carry = (
        jnp.full((KVH, GRP, rows), NEG_LARGE, jnp.float32),
        jnp.zeros((KVH, GRP, rows), jnp.float32),
        jnp.zeros((KVH, GRP, rows, HD), jnp.float32),
    )
    top, denominator, running = in_blocks(
        attend_step, start_carry, lax.all_gather(kv_local, "ctx", axis=0, tiled=True)
    )
    log_total = top + jnp.log(denominator)
    attn_heads = running / denominator[..., None]
    attn_rows = jnp.transpose(attn_heads, (2, 0, 1, 3)).reshape(rows, AQ)
    attn_b = attn_rows.astype(jnp.bfloat16)
    attn_branch = jnp.dot(attn_b, out_attend, preferred_element_type=jnp.float32)
    hidden = tokens + mixer_branch + attn_branch
    normed2, second_norm_vjp = jax.vjp(rms_norm, hidden, gain_second)
    normed_second = normed2.astype(jnp.bfloat16)
    cot_b = cotangent.astype(jnp.bfloat16)
    gate_whole, down_rows = (
        lax.all_gather(gate_up, "wsh", axis=2, tiled=True),
        lax.all_gather(down_weight, "wsh", axis=0, tiled=True),
    )
    gate_cols = gate_whole[0]
    up_cols = gate_whole[1]
    gate_part = jnp.dot(normed_second, gate_cols, preferred_element_type=jnp.float32)
    up_part = jnp.dot(normed_second, up_cols, preferred_element_type=jnp.float32)
    mlp_act = (jax.nn.silu(gate_part) * up_part).astype(jnp.bfloat16)
    mlp_out = jnp.dot(mlp_act, down_rows, preferred_element_type=jnp.float32)
    output = hidden + mlp_out
    down_local = matmul_t(mlp_act, cot_b)
    d_mlp = matmul_back(cot_b, down_rows)
    d_gate = (d_mlp * up_part * silu_slope(gate_part)).astype(jnp.bfloat16)
    d_up = (d_mlp * jax.nn.silu(gate_part)).astype(jnp.bfloat16)
    gate_up_local = jnp.stack(
        [matmul_t(normed_second, d_gate), matmul_t(normed_second, d_up)], axis=0
    )
    d_normed_second = matmul_back(d_gate, gate_cols) + matmul_back(d_up, up_cols)
    d_hidden_norm, d_gain_second = second_norm_vjp(d_normed_second)
    hidden_grad = cotangent + d_hidden_norm
    hidden_b = hidden_grad.astype(jnp.bfloat16)
    attend_out_grad = matmul_t(attn_b, hidden_b)
    mixer_out_grad = matmul_t(gated, hidden_b)
    d_attn_b = matmul_back(hidden_b, out_attend).astype(jnp.bfloat16)
    d_gated = matmul_back(hidden_b, out_mix)
    d_heads = d_attn_b.reshape(rows, KVH, GRP, HD)
    d_heads_f = d_heads.astype(jnp.float32)
    query_f = queries.astype(jnp.float32).reshape(rows, KVH, GRP, HD)
    delta = jnp.sum(jnp.transpose(d_heads_f, (1, 2, 0, 3)) * attn_heads, axis=-1)

    def attend_back(carry, piece, start):
        query_grad, kv_grad = carry
        count = piece.shape[0]
        keys_piece, values_piece = split_piece(piece)
        allowed = allowed_at(start, count)
        scores = (
            jnp.einsum(
                "tkgd,skd->kgts", query_heads, keys_piece, preferred_element_type=jnp.float32
            )
            * scale
        )
        probs = jnp.where(
            allowed, jnp.exp(jnp.where(allowed, scores, 0.0) - log_total[..., None]), 0.0
        )
        d_probs = jnp.einsum(
            "tkgd,skd->kgts", d_heads, values_piece, preferred_element_type=jnp.float32
        )
        d_scores = probs * (d_probs - delta[..., None]) * scale
        query_grad = query_grad + jnp.einsum(
            "kgts,skd->tkgd", d_scores, keys_piece.astype(jnp.float32), precision=HIGH
        )
        key_grad = jnp.einsum("kgts,tkgd->skd", d_scores, query_f, precision=HIGH)
        value_grad = jnp.einsum("kgts,tkgd->skd", probs, d_heads_f, precision=HIGH)
        update = jnp.concatenate(
            [key_grad.reshape(count, kv_width), value_grad.reshape(count, kv_width)], axis=1
        )
        kv_grad = lax.dynamic_update_slice_in_dim(kv_grad, update, start, 0)
        return (query_grad, kv_grad)

    back_carry = (
        jnp.zeros((rows, KVH, GRP, HD), jnp.float32),
        jnp.zeros((block_count * block_rows, 2 * kv_width), jnp.float32),
    )
    query_grad, kv_grad = in_blocks(
        attend_back, back_carry, lax.all_gather(kv_local, "ctx", axis=0, tiled=True)
    )
    d_mixer = (d_gated * jax.nn.silu(gate_z)).reshape(2, block_rows, MHEADS, HEAD_M)
    d_z = d_gated * mixer_flat * silu_slope(gate_z)
    g_heads, g_b, g_c, g_step, g_decay, g_state, g_skip = out_vjp(d_mixer)
    chain_backward = chain_fold(
        slot_block, my_blocks, block_second, first_len, block_rows, prefix, True
    )
    later_sum = chain_backward(
        zero_states,
        lax.all_gather(g_state.astype(jnp.bfloat16), "ctx", axis=0, tiled=True),
        jnp.int32(0),
    )
    d_totals = jnp.exp(emit_totals) * jnp.sum(later_sum * state_in, axis=(2, 3))
    e_heads, e_b, e_step, e_decay = emit_vjp((later_sum, d_totals))
    d_activated = jnp.concatenate(
        [(g_heads + e_heads).reshape(2, block_rows, DSSM), g_b + e_b, g_c], axis=2
    )
    d_conv_blocks, d_tails, filter_grad = conv_vjp(d_activated)
    tail_buffer = (
        jnp.zeros((block_count, KERNEL - 1, CONV), jnp.float32)
        .at[pred_slot]
        .add(d_tails * keep_tail[:, None, None])
    )
    d_step_raw, step_bias_grad, log_rate_grad = step_vjp(
        ((g_step + e_step).reshape(rows, MHEADS), (g_decay + e_decay).reshape(rows, MHEADS))
    )
    kv_mine, tail_back, gate_up_part, down_part = (
        lax.psum_scatter(
            kv_grad.astype(jnp.bfloat16), "ctx", scatter_dimension=0, tiled=True
        ).astype(jnp.float32),
        lax.psum_scatter(
            tail_buffer.astype(jnp.bfloat16), "ctx", scatter_dimension=0, tiled=True
        ).astype(jnp.float32),
        lax.psum_scatter(
            gate_up_local.astype(jnp.bfloat16), "ctx", scatter_dimension=1, tiled=True
        ).astype(jnp.float32),
        lax.psum_scatter(
            down_local.astype(jnp.bfloat16), "ctx", scatter_dimension=1, tiled=True
        ).astype(jnp.float32),
    )
    d_query = rotate(query_grad.reshape(rows, QH, HD), cosines, -sines).reshape(rows, AQ)
    d_key = rotate(kv_mine[:, :kv_width].reshape(rows, KVH, HD), cosines, -sines).reshape(
        rows, kv_width
    )
    d_attend = jnp.concatenate([d_query, d_key, kv_mine[:, kv_width:]], axis=1).astype(jnp.bfloat16)
    attend_in_grad = matmul_t(normed_first, d_attend)
    d_normed_attend = matmul_back(d_attend, in_attend)
    d_conv_blocks = d_conv_blocks.at[:, block_rows - (KERNEL - 1) :, :].add(tail_back)
    d_mixed = jnp.concatenate([d_z, d_conv_blocks.reshape(rows, CONV), d_step_raw], axis=1).astype(
        jnp.bfloat16
    )
    mixer_in_grad = matmul_t(normed_first, d_mixed)
    d_normed_mix = matmul_back(d_mixed, in_mix)
    d_tokens_norm, d_gain_first = first_norm_vjp(d_normed_mix + d_normed_attend)
    input_grad = hidden_grad + d_tokens_norm
    gains_grad = jnp.stack([d_gain_first, d_gain_second], axis=0)
    step_bias_grad, log_rate_grad, skip_grad, filter_grad = lax.psum(
        (step_bias_grad, log_rate_grad, g_skip, filter_grad), ("ctx", "wsh")
    )
    gate_up_grad, down_grad = (
        lax.psum_scatter(
            gate_up_part.astype(jnp.bfloat16), "wsh", scatter_dimension=2, tiled=True
        ).astype(jnp.float32),
        lax.psum_scatter(
            down_part.astype(jnp.bfloat16), "wsh", scatter_dimension=0, tiled=True
        ).astype(jnp.float32),
    )
    results = (
        lax.psum_scatter(gains_grad, ("ctx", "wsh"), scatter_dimension=1, tiled=True),
        lax.psum_scatter(mixer_in_grad, ("ctx", "wsh"), scatter_dimension=0, tiled=True),
        lax.psum_scatter(mixer_out_grad, ("ctx", "wsh"), scatter_dimension=1, tiled=True),
        lax.psum_scatter(attend_in_grad, ("ctx", "wsh"), scatter_dimension=0, tiled=True),
        lax.psum_scatter(attend_out_grad, ("ctx", "wsh"), scatter_dimension=1, tiled=True),
    )
    return (
        output[None],
        input_grad[None],
        results[0],
        filter_grad,
        step_bias_grad,
        log_rate_grad,
        skip_grad,
        results[1],
        results[2],
        results[3],
        results[4],
        gate_up_grad,
        down_grad,
    )


def xor_pairs(count, bits):
    return [(index, index ^ bits) for index in range(count)]


def held_order(count):
    return list(range(0, count, 2)) + list(range(1, count, 2))


def gather_ctx(values, with_far=False):
    count = lax.axis_size("ctx")
    first_core = lax.axis_index("ctx") % 2 == 0
    near_x = lax.ppermute(values, "ctx", xor_pairs(count, 2))
    near_y = lax.ppermute(values, "ctx", xor_pairs(count, 4))
    far = lax.ppermute(
        jnp.where(first_core, near_x, near_y),
        "ctx",
        [(index, index ^ (4 if index % 2 == 0 else 2)) for index in range(count)],
    )
    mine = jnp.stack([values, near_x, near_y, far], axis=0)
    other = lax.ppermute(mine, "ctx", xor_pairs(count, 1))
    whole = jnp.concatenate([mine, other], axis=0)
    return (whole, far) if with_far else whole


def scatter_ctx(parts):
    count = lax.axis_size("ctx")
    half = count // 2
    first_core = lax.axis_index("ctx") % 2 == 0
    wire = lambda piece: piece.astype(jnp.bfloat16)
    crossed = lax.ppermute(wire(parts[half:]), "ctx", xor_pairs(count, 1))
    sums = parts[:half] + crossed.astype(jnp.float32)
    own, near_x, near_y, far = [sums[place] for place in range(half)]
    passed = lax.ppermute(
        wire(far), "ctx", [(index, index ^ (2 if index % 2 == 0 else 4)) for index in range(count)]
    ).astype(jnp.float32)
    near_y = near_y + jnp.where(first_core, passed, 0.0)
    near_x = near_x + jnp.where(first_core, 0.0, passed)
    return (
        own
        + lax.ppermute(wire(near_x), "ctx", xor_pairs(count, 2)).astype(jnp.float32)
        + lax.ppermute(wire(near_y), "ctx", xor_pairs(count, 4)).astype(jnp.float32)
    )


def trade_ctx(parts):
    return lax.all_to_all(parts, "ctx", 0, 0, tiled=True)


def after(values, anchor):
    return lax.optimization_barrier((values, anchor))[0]


def swap_groups(pieces):
    count = lax.axis_size("wsh")
    return [pieces[0]] + [
        lax.ppermute(pieces[k], "wsh", xor_pairs(count, k)) for k in range(1, count)
    ]


def gather_wsh(values, axis=0, rows=0):
    count = lax.axis_size("wsh")
    shape = list(values.shape)
    size = shape[axis]
    shape[axis] = size * count
    shape[0] = max(shape[0], rows)
    whole = jnp.zeros(shape, values.dtype)
    for k, piece in enumerate(swap_groups([values] * count)):
        starts = [0] * values.ndim
        starts[axis] = (lax.axis_index("wsh") ^ k) * size
        whole = lax.dynamic_update_slice(whole, piece, starts)
    return whole


def dot_dims(left, right, left_dim, right_dim, precision=None):
    return lax.dot_general(
        left,
        right,
        (((left_dim,), (right_dim,)), ((), ())),
        precision=precision,
        preferred_element_type=jnp.float32,
    )


def spread(per_head, heads, lanes):
    return jnp.concatenate(
        [jnp.broadcast_to(item, (item.shape[0], lanes)) for item in per_head[:heads]], axis=1
    )


def turn(values, table, back=False):
    half = HD // 2
    swapped = jnp.concatenate([values[:, half:], values[:, :half]], axis=1)
    side = swapped * table[:, HD:]
    return values * table[:, :HD] - side if back else values * table[:, :HD] + side


def filtered(ext_ref, filt_ref, rows):
    conv = filt_ref[KERNEL : KERNEL + 1, :] + filt_ref[KERNEL - 1 : KERNEL, :] * ext_ref[8:, :]
    for tap in range(KERNEL - 1):
        start = 8 - (KERNEL - 1) + tap
        conv = conv + filt_ref[tap : tap + 1, :] * ext_ref[start : start + rows, :]
    return conv


def softplus(values):
    return jnp.maximum(values, 0.0) + jnp.log1p(jnp.exp(-jnp.abs(values)))


def block_decay(step_in, rate, rows):
    step = softplus(step_in)
    decay = -step * rate
    lower = lax.broadcasted_iota(jnp.int32, (rows, rows), 0) >= lax.broadcasted_iota(
        jnp.int32, (rows, rows), 1
    )
    ones = jnp.where(lower, 1.0, 0.0)
    cum = dot_dims(ones, decay, 1, 0, HIGH)
    cum_t = dot_dims(decay, ones, 0, 1, HIGH)
    return step, decay, lower, ones, cum, cum_t


def pick_kernel(heads, where_ref, *refs):
    xs, zs = refs[:heads], refs[heads : 2 * heads]
    bc0, step0, q0, k0, v0, gain_ref, out_ref = refs[2 * heads :]
    chans = heads * HEAD_M
    ctx = where_ref[0]
    gain = gain_ref[0:1, :].astype(jnp.float32)
    width = gain.shape[1]

    def put(start, values):
        scaled = values.astype(jnp.float32) * gain
        out_ref[start : start + values.shape[0], :] = scaled.astype(jnp.bfloat16)

    def half_tile(ref, odd):
        window = jnp.transpose(ref[...].astype(jnp.float32))
        return jnp.where(odd, window[HD:, :], window[:HD, :])

    for h in range(heads):
        put(h * HEAD_M, xs[h][...])
        put(256 + h * HEAD_M, zs[h][...])
    put(chans, half_tile(q0, ctx % 2 == 1))
    put(256 + chans, half_tile(k0, where_ref[1] % 2 == 1))
    put(512, bc0[...])
    put(768, half_tile(v0, where_ref[1] % 2 == 1))
    row = lax.broadcasted_iota(jnp.int32, (HEAD_M, width), 0)
    steps = jnp.where(row < MHEADS, step0[...].astype(jnp.float32), 0.0).astype(jnp.bfloat16)
    there = lax.broadcasted_iota(jnp.int32, (16, HEAD_M), 0)
    here = lax.broadcasted_iota(jnp.int32, (16, HEAD_M), 1)
    chosen = jnp.where((here == there + ctx * heads) & (there < heads), 1.0, 0.0)
    last = dot_dims(chosen.astype(jnp.bfloat16), steps, 1, 0) * gain
    turn_row = lax.broadcasted_iota(jnp.int32, (16, width), 0)
    second = gain_ref[1:2, :].astype(jnp.float32)
    first_row = GAIN_ROW - 768 - HD
    last = jnp.where(turn_row == first_row, gain, last)
    last = jnp.where(turn_row == first_row + 1, second, last)
    out_ref[768 + HD : SENT_ROWS, :] = last.astype(jnp.bfloat16)


def pick_columns(where, mixer_in, attend_in, gains, heads):
    width = mixer_in.shape[0]
    turned = jnp.transpose(mixer_in)
    rows_at = lambda start: pl.BlockSpec((HEAD_M, width), lambda i, s: (start(s) // HEAD_M, 0))
    tile_at = lambda start: pl.BlockSpec((width, 128), lambda i, s: (0, start(s) // 128))
    from_x = [rows_at(lambda s, h=h: DSSM + (s[0] * heads + h) * HEAD_M) for h in range(heads)]
    from_z = [rows_at(lambda s, h=h: (s[0] * heads + h) * HEAD_M) for h in range(heads)]
    return pl.pallas_call(
        partial(pick_kernel, heads),
        out_shape=jax.ShapeDtypeStruct((SENT_ROWS, width), jnp.bfloat16),
        grid_spec=pltpu.PrefetchScalarGridSpec(
            num_scalar_prefetch=1,
            grid=(1,),
            in_specs=from_x
            + from_z
            + [
                pl.BlockSpec((2 * NSTATE, width), lambda i, s: (DSSM // NSTATE, 0)),
                rows_at(lambda s: DSSM + CONV),
                tile_at(lambda s: s[0] * HD),
                tile_at(lambda s: AQ + s[1] * HD),
                tile_at(lambda s: AQ + KVH * HD + s[1] * HD),
                pl.BlockSpec(gains.shape, lambda i, s: (0, 0)),
            ],
            out_specs=pl.BlockSpec((SENT_ROWS, width), lambda i, s: (0, 0)),
        ),
        name="pick_columns",
    )(where, *[turned] * (2 * heads + 2), *[attend_in] * 3, gains)


def finish_in_kernel(heads, final_ref, mixer_ref, attend_ref, last_ref):
    count = final_ref.shape[0]
    chans = heads * HEAD_M
    share = final_ref.shape[1]
    parts = [final_ref[c].astype(jnp.float32) for c in range(count)]
    beside = lambda start, size: jnp.concatenate([p[:, start : start + size] for p in parts], axis=1)
    mixer_ref[:, :DSSM] = beside(256, chans)
    mixer_ref[:, DSSM : 2 * DSSM] = beside(0, chans)
    mixer_ref[:, 2 * DSSM : 2 * DSSM + 2 * NSTATE] = sum(p[:, 512:768] for p in parts)
    lane = lax.broadcasted_iota(jnp.int32, (128, MHEADS), 0)
    head = lax.broadcasted_iota(jnp.int32, (128, MHEADS), 1)
    steps = jnp.zeros((share, MHEADS), jnp.float32)
    for c in range(count):
        chosen = jnp.where((lane - HD == head - c * heads) & (lane >= HD) & (lane < HD + heads), 1.0, 0.0)
        steps = steps + dot_dims(final_ref[c, :, 768:896], chosen.astype(jnp.bfloat16), 1, 0)
    mixer_ref[:, DSSM + CONV :] = steps
    attend_ref[:, :AQ] = beside(chans, HD)
    each = count // KVH
    for start, place in ((256 + chans, AQ), (768, AQ + KVH * HD)):
        attend_ref[:, place : place + KVH * HD] = jnp.concatenate(
            [
                sum(p[:, start : start + HD] for p in parts[head_ * each : (head_ + 1) * each])
                for head_ in range(KVH)
            ],
            axis=1,
        )
    last_ref[...] = sum(p[:, 768:896] for p in parts)


def finish_in(final, heads):
    share = final.shape[1]
    return pl.pallas_call(
        partial(finish_in_kernel, heads),
        out_shape=(
            jax.ShapeDtypeStruct((share, DSSM + CONV + MHEADS), jnp.float32),
            jax.ShapeDtypeStruct((share, AQ + 2 * KVH * HD), jnp.float32),
            jax.ShapeDtypeStruct((share, 128), jnp.float32),
        ),
        name="finish_in",
    )(final)


def finish_rest_kernel(chans, units, share, parts_ref, gate_up_ref, down_ref, mixer_ref, attend_ref):
    count = parts_ref.shape[0]
    parts = [parts_ref[c].astype(jnp.float32) for c in range(count)]
    for place in range(2):
        gate_up_ref[place] = jnp.concatenate(
            [jnp.transpose(p[place * units : (place + 1) * units]) for p in parts], axis=1
        )
    outs = []
    for c, p in enumerate(parts):
        down_ref[c * units : (c + 1) * units, :] = p[2 * units : 3 * units]
        rest = range(3 * units, p.shape[0], share)
        outs.append(jnp.concatenate([p[start : start + share] for start in rest], axis=1))
    mixer_ref[...] = jnp.concatenate([item[:, :chans] for item in outs], axis=1)
    attend_ref[...] = jnp.concatenate([item[:, chans:] for item in outs], axis=1)


def finish_rest(parts, chans, units, share):
    count, _, wide = parts.shape
    return pl.pallas_call(
        partial(finish_rest_kernel, chans, units, share),
        out_shape=(
            jax.ShapeDtypeStruct((2, wide, count * units), jnp.float32),
            jax.ShapeDtypeStruct((count * units, wide), jnp.float32),
            jax.ShapeDtypeStruct((share, count * chans), jnp.float32),
            jax.ShapeDtypeStruct((share, count * HD), jnp.float32),
        ),
        name="finish_rest",
    )(parts)


def forward_kernel(
    heads, base, sched_ref, proj_ref, filt_ref, table_ref, params_ref, skip_ref,
    held_ref, save_ref, state_ref, kv_ref, ext_ref, chain_ref, keys_ref, values_ref,
):
    index = pl.program_id(0)
    blocks = pl.num_programs(0)
    rows = proj_ref.shape[1]
    chans = heads * HEAD_M
    seq_start = sched_ref[blocks + index]

    @pl.when(index == 0)
    def _():
        keys_ref[...] = jnp.zeros_like(keys_ref)
        values_ref[...] = jnp.zeros_like(values_ref)

    @pl.when(seq_start == index * rows)
    def _():
        ext_ref[0:8, :] = jnp.zeros((8, ext_ref.shape[1]), jnp.float32)
        chain_ref[...] = jnp.zeros_like(chain_ref)

    proj = proj_ref[0]
    ext_ref[8:, :] = jnp.concatenate([proj[:, :256], proj[:, 512:768]], axis=1)
    conv = filtered(ext_ref, filt_ref, rows)
    ext_ref[0:8, :] = ext_ref[rows:, :]
    act = conv * jax.nn.sigmoid(conv)
    heads_x = act[:, :chans]
    b_in = act[:, 256 : 256 + NSTATE]
    c_in = act[:, 256 + NSTATE : 256 + 2 * NSTATE]
    step, _, lower, _, cum, cum_t = block_decay(
        proj[:, 768:] + params_ref[0:1, :], params_ref[1:2, :], rows
    )
    cum_cols = [cum[:, base + h : base + h + 1] for h in range(heads)]
    mix = dot_dims(c_in, b_in, 1, 1, SSD)
    fed = heads_x * spread([step[:, base + h : base + h + 1] for h in range(heads)], heads, HEAD_M)
    state = chain_ref[...]
    state_ref[0] = state
    inner = []
    for h in range(heads):
        gaps = jnp.where(lower, cum_cols[h] - cum_t[base + h : base + h + 1, :], 0.0)
        kernel = jnp.where(lower, jnp.exp(gaps), 0.0) * mix
        inner.append(dot_dims(kernel, fed[:, h * HEAD_M : (h + 1) * HEAD_M], 1, 0, SSD))
    growth = spread([jnp.exp(item) for item in cum_cols], heads, HEAD_M)
    inner = jnp.concatenate(inner, axis=1) + dot_dims(c_in, state, 1, 1, SSD) * growth
    ends = [item[rows - 1 : rows, :] for item in cum_cols]
    tail = spread([jnp.exp(end - item) for end, item in zip(ends, cum_cols)], heads, HEAD_M)
    emitted = dot_dims(fed * tail, b_in, 0, 0, SSD)
    for h in range(heads):
        part = slice(h * HEAD_M, (h + 1) * HEAD_M)
        chain_ref[part, :] = jnp.exp(ends[h]) * state[part, :] + emitted[part, :]
    gate_z = proj[:, 256 : 256 + chans]
    gated = (inner + skip_ref[0:1, :] * heads_x) * (gate_z * jax.nn.sigmoid(gate_z))

    table = table_ref[0]
    query = turn(proj[:, chans : chans + HD], table).astype(jnp.bfloat16)
    key = turn(proj[:, 256 + chans : 256 + chans + HD], table).astype(jnp.bfloat16)
    value = proj[:, 768 : 768 + HD].astype(jnp.bfloat16)
    here = pl.ds(pl.multiple_of(index * rows, rows), rows)
    keys_ref[here, :] = key
    values_ref[here, :] = value
    kv_ref[0] = jnp.concatenate([key, value], axis=1)
    total = keys_ref.shape[0]
    key_pos = lax.broadcasted_iota(jnp.int32, (rows, total), 1)
    my_pos = index * rows + lax.broadcasted_iota(jnp.int32, (rows, total), 0)
    allowed = (key_pos <= my_pos) & (key_pos >= seq_start)
    scores = jnp.where(
        allowed, dot_dims(query, keys_ref[...], 1, 1) * (1.0 / math.sqrt(HD)), NEG_LARGE
    )
    top = jnp.max(scores, axis=-1, keepdims=True)
    weights = jnp.exp(scores - top)
    denominator = jnp.sum(weights, axis=-1, keepdims=True)
    attn = dot_dims(weights.astype(jnp.bfloat16), values_ref[...], 1, 0) / denominator
    log_total = jnp.broadcast_to(top + jnp.log(denominator), (rows, 128))
    save_ref[0] = jnp.concatenate([inner, attn, log_total], axis=1)
    held_ref[0] = jnp.concatenate([gated, attn], axis=1).astype(jnp.bfloat16)


def backward_kernel(
    heads, base, sched_ref, proj_ref, before_ref, filt_ref, table_ref, params_ref, skip_ref,
    save_ref, state_ref, kv_ref, d_mix_ref,
    d_ref, filt_grad_ref, head_grad_ref, ext_ref, next_ref, later_ref, keys_ref, values_ref,
):
    blocks = pl.num_programs(0)
    turn_index = pl.program_id(0)
    index = blocks - 1 - turn_index
    rows = proj_ref.shape[1]
    chans = heads * HEAD_M
    seq_start = sched_ref[blocks + index]
    after = jnp.minimum(index + 1, blocks - 1)
    is_end = (index == blocks - 1) | (sched_ref[blocks + after] == after * rows)

    @pl.when(turn_index == 0)
    def _():
        keys_ref[...] = jnp.zeros_like(keys_ref)
        values_ref[...] = jnp.zeros_like(values_ref)
        filt_grad_ref[...] = jnp.zeros_like(filt_grad_ref)
        head_grad_ref[...] = jnp.zeros_like(head_grad_ref)

    @pl.when(is_end)
    def _():
        next_ref[rows:, :] = jnp.zeros((8, next_ref.shape[1]), jnp.float32)
        later_ref[...] = jnp.zeros_like(later_ref)

    proj = proj_ref[0]
    keep = jnp.where(seq_start == index * rows, 0.0, 1.0)
    before = before_ref[0]
    ext_ref[0:8, :] = jnp.concatenate([before[:, :256], before[:, 512:768]], axis=1) * keep
    ext_ref[8:, :] = jnp.concatenate([proj[:, :256], proj[:, 512:768]], axis=1)
    conv = filtered(ext_ref, filt_ref, rows)
    conv_sig = jax.nn.sigmoid(conv)
    act = conv * conv_sig
    heads_x = act[:, :chans]
    b_in = act[:, 256 : 256 + NSTATE]
    c_in = act[:, 256 + NSTATE : 256 + 2 * NSTATE]
    step_in = proj[:, 768:] + params_ref[0:1, :]
    rate = params_ref[1:2, :]
    step, decay, lower, ones, cum, cum_t = block_decay(step_in, rate, rows)
    cum_cols = [cum[:, base + h : base + h + 1] for h in range(heads)]
    step_cols = spread([step[:, base + h : base + h + 1] for h in range(heads)], heads, HEAD_M)
    mix = dot_dims(c_in, b_in, 1, 1, SSD)
    fed = heads_x * step_cols
    state = state_ref[0]
    later = later_ref[...]
    save = save_ref[0]
    inner = save[:, :chans]
    skip = skip_ref[0:1, :]

    d_mix = d_mix_ref[0]
    d_gated = d_mix[:, :chans]
    gate_z = proj[:, 256 : 256 + chans]
    gate_sig = jax.nn.sigmoid(gate_z)
    d_z = d_gated * (inner + skip * heads_x) * (gate_sig * (1.0 + gate_z * (1.0 - gate_sig)))
    d_y = d_gated * (gate_z * gate_sig)
    growth = spread([jnp.exp(item) for item in cum_cols], heads, HEAD_M)
    ends = [item[rows - 1 : rows, :] for item in cum_cols]
    tail = spread([jnp.exp(end - item) for end, item in zip(ends, cum_cols)], heads, HEAD_M)
    grown = d_y * growth
    fed_tail = fed * tail
    fed_inner = []
    d_mixing = jnp.zeros((rows, rows), jnp.float32)
    for h in range(heads):
        part = slice(h * HEAD_M, (h + 1) * HEAD_M)
        gaps = jnp.where(lower, cum_cols[h] - cum_t[base + h : base + h + 1, :], 0.0)
        decays = jnp.where(lower, jnp.exp(gaps), 0.0)
        fed_inner.append(dot_dims(decays * mix, d_y[:, part], 0, 0, SSD))
        d_mixing = d_mixing + dot_dims(d_y[:, part], fed[:, part], 1, 1, SSD) * decays
    fed_emit = dot_dims(b_in, later, 1, 1, SSD) * tail
    d_fed = jnp.concatenate(fed_inner, axis=1) + fed_emit
    d_c = dot_dims(d_mixing, b_in, 1, 0, SSD) + dot_dims(grown, state, 1, 0, SSD)
    d_b = dot_dims(d_mixing, c_in, 0, 0, SSD) + dot_dims(fed_tail, later, 1, 0, SSD)
    state_grad = dot_dims(grown, c_in, 0, 0, SSD)
    d_x = d_fed * step_cols + skip * d_y
    lane = lax.broadcasted_iota(jnp.int32, (1, 128), 1)
    d_cum = jnp.zeros((rows, 128), jnp.float32)
    d_step = jnp.zeros((rows, 128), jnp.float32)
    d_total = jnp.zeros((1, 128), jnp.float32)
    skip_sum = jnp.zeros((1, 128), jnp.float32)
    cum_terms = d_y * inner - fed * d_fed
    step_terms = d_fed * heads_x
    emit_terms = fed * fed_emit
    skip_terms = d_y * heads_x
    carry_terms = later * state
    for h in range(heads):
        part = slice(h * HEAD_M, (h + 1) * HEAD_M)
        mine = jnp.where(lane == base + h, 1.0, 0.0)
        growth_end = jnp.exp(ends[h])
        d_cum = d_cum + jnp.sum(cum_terms[:, part], axis=1, keepdims=True) * mine
        d_step = d_step + jnp.sum(step_terms[:, part], axis=1, keepdims=True) * mine
        carry = jnp.sum(jnp.sum(carry_terms[part, :], axis=0, keepdims=True), axis=1, keepdims=True)
        emit = jnp.sum(jnp.sum(emit_terms[:, part], axis=0, keepdims=True), axis=1, keepdims=True)
        skips = jnp.sum(jnp.sum(skip_terms[:, part], axis=0, keepdims=True), axis=1, keepdims=True)
        d_total = d_total + (growth_end * carry + emit) * mine
        skip_sum = skip_sum + skips * mine
        later_ref[part, :] = state_grad[part, :] + growth_end * later[part, :]
    d_decay = dot_dims(ones, d_cum, 0, 0, HIGH) + d_total
    d_step = (d_step - d_decay * rate) * jax.nn.sigmoid(step_in)
    d_step = jnp.where((lane >= base) & (lane < base + heads), d_step, 0.0)
    head_grad_ref[0:1, :] += jnp.sum(d_step, axis=0, keepdims=True)
    head_grad_ref[1:2, :] += jnp.sum(d_decay * decay, axis=0, keepdims=True)
    head_grad_ref[2:3, :] += skip_sum

    d_conv = jnp.concatenate([d_x, jnp.zeros((rows, 256 - chans), jnp.float32), d_b, d_c], axis=1)
    d_conv = d_conv * (conv_sig * (1.0 + conv * (1.0 - conv_sig)))
    next_ref[0:rows, :] = d_conv
    d_in = filt_ref[KERNEL - 1 : KERNEL, :] * d_conv
    for tap in range(KERNEL - 1):
        shift = KERNEL - 1 - tap
        d_in = d_in + filt_ref[tap : tap + 1, :] * next_ref[shift : shift + rows, :]
        filt_grad_ref[tap : tap + 1, :] += jnp.sum(
            d_conv * ext_ref[8 - shift : 8 - shift + rows, :], axis=0, keepdims=True
        )
    filt_grad_ref[KERNEL - 1 : KERNEL, :] += jnp.sum(d_conv * ext_ref[8:, :], axis=0, keepdims=True)
    filt_grad_ref[KERNEL : KERNEL + 1, :] += jnp.sum(d_conv, axis=0, keepdims=True)
    next_ref[rows:, :] = d_conv[0:8, :]

    table = table_ref[0]
    scale = 1.0 / math.sqrt(HD)
    query = turn(proj[:, chans : chans + HD], table).astype(jnp.bfloat16)
    keys = kv_ref[:, :HD]
    values = kv_ref[:, HD:]
    d_attn = d_mix[:, chans : chans + HD].astype(jnp.bfloat16)
    delta = jnp.sum(d_attn.astype(jnp.float32) * save[:, chans : chans + HD], axis=1, keepdims=True)
    total = keys.shape[0]
    key_pos = lax.broadcasted_iota(jnp.int32, (rows, total), 1)
    my_pos = index * rows + lax.broadcasted_iota(jnp.int32, (rows, total), 0)
    allowed = (key_pos <= my_pos) & (key_pos >= seq_start)
    scores = jnp.where(allowed, dot_dims(query, keys, 1, 1) * scale, NEG_LARGE)
    probs = jnp.exp(scores - save[:, chans + HD : chans + HD + 1])
    d_scores = (probs * (dot_dims(d_attn, values, 1, 1) - delta) * scale).astype(jnp.bfloat16)
    d_query = turn(dot_dims(d_scores, keys, 1, 0), table, back=True)
    keys_ref[...] += dot_dims(d_scores, query, 0, 0)
    values_ref[...] += dot_dims(probs.astype(jnp.bfloat16), d_attn, 0, 0)
    here = pl.ds(pl.multiple_of(index * rows, rows), rows)
    d_key = turn(keys_ref[here, :], table, back=True)
    d_value = values_ref[here, :]
    d_ref[0] = jnp.concatenate(
        [d_in[:, :chans], d_query, d_z, d_key, d_in[:, 256:], d_value, d_step[:, HD:]], axis=1
    ).astype(jnp.bfloat16)


def mixer_forward(sched, proj, filt, table, params, skip, heads, base):
    blocks, rows, wide = proj.shape
    chans = heads * HEAD_M
    held = lambda b, s: (s[b], 0, 0)
    plain = lambda b, s: (b, 0, 0)
    whole = lambda b, s: (0, 0)
    return pl.pallas_call(
        partial(forward_kernel, heads, base),
        out_shape=(
            jax.ShapeDtypeStruct((blocks, rows, 256), jnp.bfloat16),
            jax.ShapeDtypeStruct((blocks, rows, 384), jnp.float32),
            jax.ShapeDtypeStruct((blocks, chans, NSTATE), jnp.float32),
            jax.ShapeDtypeStruct((blocks, rows, 2 * HD), jnp.bfloat16),
        ),
        grid_spec=pltpu.PrefetchScalarGridSpec(
            num_scalar_prefetch=1,
            grid=(blocks,),
            in_specs=[
                pl.BlockSpec((1, rows, wide), held),
                pl.BlockSpec(filt.shape, whole),
                pl.BlockSpec((1, rows, 2 * HD), plain),
                pl.BlockSpec(params.shape, whole),
                pl.BlockSpec(skip.shape, whole),
            ],
            out_specs=(
                pl.BlockSpec((1, rows, 256), held),
                pl.BlockSpec((1, rows, 384), plain),
                pl.BlockSpec((1, chans, NSTATE), plain),
                pl.BlockSpec((1, rows, 2 * HD), plain),
            ),
            scratch_shapes=[
                pltpu.VMEM((rows + 8, 512), jnp.float32),
                pltpu.VMEM((chans, NSTATE), jnp.float32),
                pltpu.VMEM((blocks * rows, HD), jnp.bfloat16),
                pltpu.VMEM((blocks * rows, HD), jnp.bfloat16),
            ],
        ),
        cost_estimate=pl.CostEstimate(
            flops=25_000_000_000, transcendentals=0, bytes_accessed=12_000_000
        ),
        name="mixer_forward",
    )(sched, proj, filt, table, params, skip)


def mixer_backward(sched, proj, filt, table, params, skip, save, states, kv, d_mix, heads, base):
    blocks, rows, wide = proj.shape
    chans = heads * HEAD_M
    held = lambda i, s: (s[blocks - 1 - i], 0, 0)
    before = lambda i, s: (s[jnp.maximum(blocks - 2 - i, 0)], rows // 8 - 1, 0)
    plain = lambda i, s: (blocks - 1 - i, 0, 0)
    whole = lambda i, s: (0, 0)
    return pl.pallas_call(
        partial(backward_kernel, heads, base),
        out_shape=(
            jax.ShapeDtypeStruct((blocks, rows, wide), jnp.bfloat16),
            jax.ShapeDtypeStruct((8, 512), jnp.float32),
            jax.ShapeDtypeStruct((8, 128), jnp.float32),
        ),
        grid_spec=pltpu.PrefetchScalarGridSpec(
            num_scalar_prefetch=1,
            grid=(blocks,),
            in_specs=[
                pl.BlockSpec((1, rows, wide), held),
                pl.BlockSpec((1, 8, wide), before),
                pl.BlockSpec(filt.shape, whole),
                pl.BlockSpec((1, rows, 2 * HD), plain),
                pl.BlockSpec(params.shape, whole),
                pl.BlockSpec(skip.shape, whole),
                pl.BlockSpec((1, rows, 384), plain),
                pl.BlockSpec((1, chans, NSTATE), plain),
                pl.BlockSpec((blocks * rows, 2 * HD), whole),
                pl.BlockSpec((1, rows, 256), held),
            ],
            out_specs=(
                pl.BlockSpec((1, rows, wide), held),
                pl.BlockSpec((8, 512), whole),
                pl.BlockSpec((8, 128), whole),
            ),
            scratch_shapes=[
                pltpu.VMEM((rows + 8, 512), jnp.float32),
                pltpu.VMEM((rows + 8, 512), jnp.float32),
                pltpu.VMEM((chans, NSTATE), jnp.float32),
                pltpu.VMEM((blocks * rows, HD), jnp.float32),
                pltpu.VMEM((blocks * rows, HD), jnp.float32),
            ],
        ),
        cost_estimate=pl.CostEstimate(
            flops=40_000_000_000, transcendentals=0, bytes_accessed=16_000_000
        ),
        name="mixer_backward",
    )(sched, proj, proj, filt, table, params, skip, save, states, kv.reshape(-1, 2 * HD), d_mix)


def head_plan(
    block_input,
    out_cotangent,
    lengths,
    slot_block,
    norm_gains,
    short_filter,
    step_bias,
    log_rate,
    skip_gain,
    mixer_in,
    mixer_out,
    attend_in,
    attend_out,
    gate_up,
    down_weight,
):
    count = lax.axis_size("ctx")
    groups = lax.axis_size("wsh")
    ctx = lax.axis_index("ctx")
    wsh = lax.axis_index("wsh")
    rows, width = block_input.shape[1:]
    block_rows = rows // 2
    blocks = 2 * count
    total_rows = count * rows
    heads = MHEADS // count
    chans = heads * HEAD_M
    kv_head = ctx * KVH // count
    units = gate_up.shape[2] // count
    first_len = lengths[0, 0]
    tokens = block_input[0]
    cotangent = out_cotangent[0]
    cols = lambda array, start, size: lax.dynamic_slice_in_dim(array, start, size, array.ndim - 1)
    base = HD
    step_pad = 128 - base - heads

    in_cols = pick_columns(
        jnp.stack([ctx, kv_head]), mixer_in, attend_in, norm_gains, heads
    )
    in_all = gather_wsh(in_cols, 1, 896)
    gains = in_all[GAIN_ROW : GAIN_ROW + 2].astype(jnp.float32)
    out_rows = jnp.concatenate(
        [
            lax.dynamic_slice_in_dim(mixer_out, ctx * chans, chans, 0),
            lax.dynamic_slice_in_dim(attend_out, ctx * HD, HD, 0),
        ],
        axis=0,
    )
    mlp_pack = jnp.concatenate(
        [
            jnp.transpose(cols(gate_up[0], ctx * units, units)),
            jnp.transpose(cols(gate_up[1], ctx * units, units)),
            lax.dynamic_slice_in_dim(down_weight, ctx * units, units, 0),
        ],
        axis=0,
    )
    out_rows, mlp_pack = after((out_rows, mlp_pack), in_all)
    out_mine = gather_wsh(out_rows, 1)
    packs = swap_groups([mlp_pack] * groups)
    gate_up_rows = jnp.concatenate(
        [pack[:units] for pack in packs] + [pack[units : 2 * units] for pack in packs], axis=0
    )
    down_all = jnp.concatenate([pack[2 * units :] for pack in packs], axis=0)

    peers = ctx ^ jnp.array(held_order(count), dtype=jnp.int32)
    held = jnp.take(slot_block.reshape(count, 2), peers, axis=0, mode="clip").reshape(blocks)
    logical_ids = jnp.arange(blocks, dtype=jnp.int32)

    place = jnp.sum(
        jnp.where(held[None, :] == logical_ids[:, None], logical_ids[None, :], 0), axis=1
    )
    starts = jnp.where(logical_ids * block_rows >= first_len, first_len, 0)
    sched = jnp.concatenate([place, starts])
    positions = jnp.arange(total_rows, dtype=jnp.int32)
    seq_pos = positions - jnp.where(positions >= first_len, first_len, 0)
    half = HD // 2
    freqs = jnp.exp(jnp.arange(half, dtype=jnp.float32) * (-2.0 * math.log(ROPE_BASE) / HD))
    angles = seq_pos.astype(jnp.float32)[:, None] * freqs[None, :]
    cosines = jnp.cos(angles)
    sines = jnp.sin(angles)
    table = jnp.concatenate([cosines, cosines, -sines, sines], axis=1)
    table = table.reshape(blocks, block_rows, 2 * HD)
    filt = jnp.concatenate(
        [
            cols(short_filter, ctx * chans, chans),
            jnp.zeros((KERNEL + 1, HD), jnp.float32),
            short_filter[:, DSSM:],
        ],
        axis=1,
    )
    filt = jnp.pad(filt, ((0, 7 - KERNEL), (0, 0)))
    mine = lambda array: lax.dynamic_slice_in_dim(array, ctx * heads, heads)
    params = jnp.stack([mine(step_bias), jnp.exp(mine(log_rate))], axis=0)
    params = jnp.pad(params, ((0, 6), (base, 128 - base - heads)))
    skip = jnp.broadcast_to(jnp.repeat(mine(skip_gain), HEAD_M)[None, :], (8, chans))

    tokens = after(tokens, in_cols)
    first_scale = lax.rsqrt(jnp.mean(tokens * tokens, axis=-1, keepdims=True) + EPS)
    unit_tokens = tokens * first_scale
    units_first = gather_ctx(unit_tokens.astype(jnp.bfloat16)).reshape(total_rows, width)
    units_t = lax.optimization_barrier(jnp.transpose(units_first))
    cot_all = gather_ctx(after(cotangent.astype(jnp.bfloat16), units_first))
    cot_all = cot_all.reshape(total_rows, width)
    projected = matmul_back(units_first, in_all).reshape(blocks, block_rows, in_all.shape[0])
    mixed_held, saved, states, kv = mixer_forward(
        sched, projected, filt, table, params, skip, heads, base
    )
    mixed_held = mixed_held.reshape(total_rows, chans + HD)

    hidden = tokens + scatter_ctx(
        jnp.dot(mixed_held, out_mine, preferred_element_type=jnp.float32).reshape(
            count, rows, width
        )
    )

    second_scale = lax.rsqrt(jnp.mean(hidden * hidden, axis=-1, keepdims=True) + EPS)
    unit_hidden = hidden * second_scale
    normed_second = gather_ctx((unit_hidden * gains[1]).astype(jnp.bfloat16)).reshape(
        total_rows, width
    )
    both = matmul_back(normed_second, gate_up_rows)
    gate_part = both[:, : groups * units]
    up_part = both[:, groups * units :]
    silu_gate = jax.nn.silu(gate_part)
    mlp_act = (silu_gate * up_part).astype(jnp.bfloat16)
    d_mlp = matmul_back(cot_all, down_all)
    d_gate = (d_mlp * up_part * silu_slope(gate_part)).astype(jnp.bfloat16)
    d_up = (d_mlp * silu_gate).astype(jnp.bfloat16)
    d_both = jnp.concatenate([d_gate, d_up], axis=1)
    d_normed_second = scatter_ctx(
        jnp.dot(d_both, gate_up_rows, preferred_element_type=jnp.float32).reshape(
            count, rows, width
        )
    )

    def norm_back(d_normed, gain, unit, unit_scale):
        scaled = d_normed * gain
        return unit_scale * (scaled - unit * jnp.mean(scaled * unit, axis=-1, keepdims=True))

    hidden_grad = cotangent + norm_back(d_normed_second, gains[1], unit_hidden, second_scale)
    hidden_b, hidden_far = gather_ctx(hidden_grad.astype(jnp.bfloat16), True)
    hidden_b = hidden_b.reshape(total_rows, width)

    both_grad = matmul_t(d_both, normed_second)
    down_local = matmul_t(mlp_act, cot_all)
    gain_second_grad = jnp.sum(both_grad * gate_up_rows.astype(jnp.float32), axis=0) / gains[1]
    inner_units = groups * units
    mlp_grads = [
        jnp.concatenate(
            [
                both_grad[k * units : (k + 1) * units],
                both_grad[inner_units + k * units : inner_units + (k + 1) * units],
                down_local[k * units : (k + 1) * units],
            ],
            axis=0,
        ).astype(jnp.bfloat16)
        for k in range(groups)
    ]
    mlp_swapped = swap_groups(mlp_grads)
    mlp_sum = sum(piece.astype(jnp.float32) for piece in mlp_swapped)
    mlp_sum = jnp.transpose(
        mlp_sum.astype(jnp.bfloat16).reshape(3 * units, count, width // count), (1, 0, 2)
    )

    d_mix = matmul_back(hidden_b, out_mine).reshape(blocks, block_rows, chans + HD)
    share = width // (count * groups)

    def to_groups(grad):
        parts = grad.reshape(count, groups, share, grad.shape[1])
        return [
            lax.dynamic_index_in_dim(parts, wsh ^ k, 1, keepdims=False).astype(jnp.bfloat16)
            for k in range(groups)
        ]

    places = jnp.array([held_order(count).index(k) for k in range(count)], dtype=jnp.int32)
    by_device = jnp.take(places, ctx ^ jnp.arange(count, dtype=jnp.int32), mode="clip")
    act_by_device = jnp.take(
        mlp_act.reshape(count, rows, inner_units), by_device, axis=0, mode="clip"
    ).reshape(total_rows, inner_units)
    mlp_parts = jnp.dot(act_by_device, down_all, preferred_element_type=jnp.float32)
    mlp_parts = mlp_parts.astype(jnp.bfloat16).reshape(count, rows, width)
    mlp_parts = after(mlp_parts, hidden_far)
    mlp_parts = trade_ctx(mlp_parts)
    output = hidden + jnp.sum(mlp_parts.astype(jnp.float32), axis=0)
    out_grads = to_groups(matmul_t(hidden_b, mixed_held))
    out_swapped = swap_groups(out_grads)
    out_sum = sum(piece.astype(jnp.float32) for piece in out_swapped)
    d_held, filt_grad, head_grad = mixer_backward(
        sched, projected, filt, table, params, skip, saved, states, kv, d_mix, heads, base
    )
    out_sum = out_sum.astype(jnp.bfloat16)
    payload = jnp.concatenate(
        [mlp_sum]
        + [out_sum[:, :, start : start + 128] for start in range(0, out_sum.shape[2], 128)],
        axis=1,
    )
    payload = trade_ctx(after(payload, (mlp_parts, d_held)))
    gate_up_grad, down_grad, mixer_out_grad, attend_out_grad = finish_rest(
        payload, chans, units, share
    )
    mixer_out_grad = jnp.transpose(mixer_out_grad)
    attend_out_grad = jnp.transpose(attend_out_grad)
    d_held = d_held.reshape(total_rows, -1)
    d_unit_first = scatter_ctx(
        jnp.dot(d_held, in_all, preferred_element_type=jnp.float32).reshape(
            count, rows, width
        )
    )
    input_grad = hidden_grad + norm_back(d_unit_first, 1.0, unit_tokens, first_scale)

    in_grad = jnp.dot(units_t, d_held, preferred_element_type=jnp.float32)
    gain_first_grad = jnp.sum(in_grad * jnp.transpose(in_all).astype(jnp.float32), axis=1) / gains[0]
    in_grad = in_grad * gains[0][:, None]
    lane = jnp.arange(in_all.shape[0], dtype=jnp.int32)[None, :]
    gain_lane = in_all.shape[0] - step_pad
    in_grad = jnp.where(lane == gain_lane, gain_first_grad[:, None], in_grad)
    in_grad = jnp.where(lane == gain_lane + 1, gain_second_grad[:, None], in_grad)
    in_grads = to_groups(in_grad)
    in_swapped = swap_groups(in_grads)
    in_sum = sum(piece.astype(jnp.float32) for piece in in_swapped)
    mixer_in_grad, attend_in_grad, last_cols = finish_in(
        trade_ctx(after(in_sum.astype(jnp.bfloat16), payload)), heads
    )
    gain_place = gain_lane % 128
    gains_grad = jnp.transpose(last_cols[:, gain_place : gain_place + 2])
    side_by_side = lambda array: jnp.transpose(array, (1, 0, 2)).reshape(array.shape[1], -1)

    small = jnp.concatenate([filt_grad.reshape(-1, 128), head_grad], axis=0)
    small = gather_wsh(small[None])
    small = gather_ctx(jnp.sum(small, axis=0))
    small = jnp.take(small, by_device, axis=0, mode="clip")
    filters = small[:, :-8].reshape(count, 8, 512)[:, : KERNEL + 1]
    filter_grad = jnp.concatenate(
        [side_by_side(filters[:, :, :chans]), jnp.sum(filters[:, :, 256:], axis=0)], axis=1
    )
    per_head = small[:, -8:-5, base : base + heads]
    step_bias_all, log_rate_all, skip_all = [per_head[:, i].reshape(-1) for i in range(3)]
    return (
        output[None],
        input_grad[None],
        gains_grad,
        filter_grad,
        step_bias_all,
        log_rate_all,
        skip_all,
        mixer_in_grad,
        mixer_out_grad,
        attend_in_grad,
        attend_out_grad,
        gate_up_grad,
        down_grad,
    )


def on_device_heads(*args):
    return head_plan(*args)


def solution(mesh):
    placed = (
        P("wsh", "ctx", None),
        P("wsh", "ctx", None),
        P("wsh", None),
        P(),
        P(None, "wsh"),
        P(),
        P(),
        P(),
        P(),
        P("wsh", None),
        P(None, "wsh"),
        P("wsh", None),
        P(None, "wsh"),
        P(None, None, "wsh"),
        P("wsh", None),
    )
    per_heads = mesh.shape["ctx"] == QH
    return jax.shard_map(
        on_device_heads if per_heads else on_device,
        mesh=mesh,
        in_specs=placed,
        out_specs=(
            P("wsh", "ctx", None),
            P("wsh", "ctx", None),
            P(None, ("ctx", "wsh")),
            P(),
            P(),
            P(),
            P(),
            P(("ctx", "wsh"), None),
            P(None, ("ctx", "wsh")),
            P(("ctx", "wsh"), None),
            P(None, ("ctx", "wsh")),
            P(None, "ctx", "wsh"),
            P("wsh", "ctx"),
        ),
        check_vma=False,
    )
```

```python
import math
from functools import partial

import jax
import jax.numpy as jnp
from jax import lax
from jax.experimental import pallas as pl
from jax.experimental.pallas import tpu as pltpu
from jax.sharding import PartitionSpec as P

MHEADS = 24
HEAD_M = 64
NSTATE = 128
QH = 8
KVH = 2
HD = 64
KERNEL = 4
DSSM = 1536
CONV = 1792
AQ = 512
GRP = 4


EPS = 1e-05
ROPE_BASE = 100000000000.0
HIGH = lax.Precision.HIGHEST
SSD = None
NEG_LARGE = -1e30
GAIN_ROW = 880


def rms_norm(values, gain):
    scale = lax.rsqrt(jnp.mean(values * values, axis=-1, keepdims=True) + EPS)
    return values * scale * gain


def silu_slope(values):
    sigmoid_value = jax.nn.sigmoid(values)
    return sigmoid_value * (1.0 + values * (1.0 - sigmoid_value))


def rope_tables(positions):
    half = HD // 2
    freqs = jnp.exp(jnp.arange(half, dtype=jnp.float32) * (-2.0 * math.log(ROPE_BASE) / HD))
    angles = positions.astype(jnp.float32)[:, None] * freqs[None, :]
    return (jnp.cos(angles)[:, None, :], jnp.sin(angles)[:, None, :])


def rotate(values, cosines, sines):
    half = values.shape[-1] // 2
    first = values[..., :half]
    second = values[..., half:]
    return jnp.concatenate(
        [first * cosines - second * sines, second * cosines + first * sines], axis=-1
    )


def matmul_t(left, right):
    return lax.dot_general(
        left, right, (((0,), (0,)), ((), ())), preferred_element_type=jnp.float32
    )


def matmul_back(left, right):
    return lax.dot_general(
        left, right, (((1,), (1,)), ((), ())), preferred_element_type=jnp.float32
    )


def step_prep(step_raw, step_bias, log_rate):
    step = jax.nn.softplus(step_raw + step_bias)
    return (step, -step * jnp.exp(log_rate))


def conv_prep(conv_blocks, tails_in, filter_rows):
    count = conv_blocks.shape[1]
    extended = jnp.concatenate([tails_in, conv_blocks], axis=1)
    conv = filter_rows[KERNEL] + filter_rows[KERNEL - 1] * conv_blocks
    for tap_index in range(KERNEL - 1):
        conv = conv + filter_rows[tap_index] * extended[:, tap_index : tap_index + count]
    return jax.nn.silu(conv)


def ssd_emit(heads_x, b_in, step, log_decay):
    cumulative = jnp.cumsum(log_decay, axis=0)
    weight = jnp.exp(cumulative[-1][None, :] - cumulative) * step
    emitted = jnp.einsum("shp,sn->hpn", heads_x * weight[:, :, None], b_in, precision=HIGH)
    return (emitted, cumulative[-1])


def ssd_output(heads_x, b_in, c_in, step, log_decay, state_in, skip_gain):
    cumulative = jnp.cumsum(log_decay, axis=0)
    count = heads_x.shape[0]
    lower = (jnp.arange(count)[:, None] >= jnp.arange(count)[None, :])[:, :, None]
    gaps = jnp.where(lower, cumulative[:, None, :] - cumulative[None, :, :], 0.0)
    kernel = (
        jnp.where(lower, jnp.exp(gaps), 0.0) * jnp.dot(c_in, b_in.T, precision=HIGH)[:, :, None]
    )
    inner = jnp.einsum("tsh,shp->thp", kernel, heads_x * step[:, :, None], precision=HIGH)
    carried = (
        jnp.einsum("hpn,tn->thp", state_in, c_in, precision=HIGH) * jnp.exp(cumulative)[:, :, None]
    )
    return inner + carried + skip_gain[None, :, None] * heads_x


def chain_fold(slot_block, my_blocks, block_second, first_len, block_rows, prefix, later):

    def fold(total, piece, start):
        count = piece.shape[0]
        same = (slot_block * block_rows >= first_len)[None, :] == block_second[:, None]
        if later:
            valid = same & (slot_block[None, :] > my_blocks[:, None])
            gaps = (
                jnp.take(prefix, slot_block, axis=0)[None, :, :]
                - jnp.take(prefix, my_blocks + 1, axis=0)[:, None, :]
            )
        else:
            valid = same & (slot_block[None, :] < my_blocks[:, None])
            gaps = (
                jnp.take(prefix, my_blocks, axis=0)[:, None, :]
                - jnp.take(prefix, slot_block + 1, axis=0)[None, :, :]
            )
        factors = jnp.where(
            valid[:, :, None], jnp.exp(jnp.where(valid[:, :, None], gaps, 0.0)), 0.0
        )
        step_size = math.gcd(count, 8)

        def add_rows(index, running):
            rows_piece = lax.dynamic_slice_in_dim(piece, index * step_size, step_size).astype(
                jnp.float32
            )
            factor_rows = lax.dynamic_slice_in_dim(factors, index * step_size, step_size, 1)
            return running + jnp.einsum("bsh,shpn->bhpn", factor_rows, rows_piece, precision=HIGH)

        return lax.fori_loop(0, count // step_size, add_rows, total)

    return fold


def in_blocks(step_fn, carry, piece):
    count = piece.shape[0]
    block_size = math.gcd(count, 512)

    def visit(block_index, state):
        sub_piece = lax.dynamic_slice_in_dim(piece, block_index * block_size, block_size)
        return step_fn(state, sub_piece, block_index * block_size)

    return lax.fori_loop(0, count // block_size, visit, carry)


def on_device(
    block_input,
    out_cotangent,
    lengths,
    slot_block,
    norm_gains,
    short_filter,
    step_bias,
    log_rate,
    skip_gain,
    mixer_in,
    mixer_out,
    attend_in,
    attend_out,
    gate_up,
    down_weight,
):
    gains_all, in_mix, out_mix, in_attend, out_attend = (
        lax.all_gather(norm_gains, "wsh", axis=1, tiled=True),
        lax.all_gather(mixer_in, "wsh", axis=0, tiled=True),
        lax.all_gather(mixer_out, "wsh", axis=1, tiled=True),
        lax.all_gather(attend_in, "wsh", axis=0, tiled=True),
        lax.all_gather(attend_out, "wsh", axis=1, tiled=True),
    )
    ctx_count = lax.axis_size("ctx")
    block_count = 2 * ctx_count
    rows = block_input.shape[1]
    block_rows = rows // 2
    kv_width = KVH * HD
    scale = 1.0 / math.sqrt(HD)
    tokens = block_input[0]
    cotangent = out_cotangent[0]
    first_len = lengths[0, 0]
    logical_ids = jnp.arange(block_count, dtype=jnp.int32)
    my_blocks = lax.dynamic_slice_in_dim(slot_block, 2 * lax.axis_index("ctx"), 2)
    block_offsets = jnp.arange(block_rows, dtype=jnp.int32)
    my_pos = (my_blocks[:, None] * block_rows + block_offsets[None, :]).reshape(rows)
    my_second = my_pos >= first_len
    seq_pos = my_pos - jnp.where(my_second, first_len, 0)
    block_second = my_blocks * block_rows >= first_len
    is_start = (my_blocks == 0) | (my_blocks * block_rows == first_len)
    key_pos = (slot_block[:, None] * block_rows + block_offsets[None, :]).reshape(
        block_count * block_rows
    )
    gain_first = gains_all[0].astype(jnp.float32)
    gain_second = gains_all[1].astype(jnp.float32)
    normed, first_norm_vjp = jax.vjp(rms_norm, tokens, gain_first)
    normed_first = normed.astype(jnp.bfloat16)
    mixed = jnp.dot(normed_first, in_mix, preferred_element_type=jnp.float32)
    gate_z = mixed[:, :DSSM]
    conv_input = mixed[:, DSSM : DSSM + CONV]
    step_raw = mixed[:, DSSM + CONV :]
    (step, log_decay), step_vjp = jax.vjp(step_prep, step_raw, step_bias, log_rate)
    step_blocks = step.reshape(2, block_rows, MHEADS)
    decay_blocks = log_decay.reshape(2, block_rows, MHEADS)
    totals = jnp.sum(decay_blocks, axis=1)
    conv_blocks = conv_input.reshape(2, block_rows, CONV)
    tails = conv_blocks[:, block_rows - (KERNEL - 1) :, :]
    all_tails, all_totals = (
        lax.all_gather(tails, "ctx", axis=0, tiled=True),
        lax.all_gather(totals, "ctx", axis=0, tiled=True),
    )
    one_hot = (slot_block[None, :] == logical_ids[:, None]).astype(jnp.float32)
    totals_logical = jnp.dot(one_hot, all_totals, precision=HIGH)
    prefix = jnp.concatenate(
        [jnp.zeros((1, MHEADS), jnp.float32), jnp.cumsum(totals_logical, axis=0)], axis=0
    )
    pred_slot = jnp.sum(
        jnp.where(slot_block[None, :] == (my_blocks - 1)[:, None], logical_ids[None, :], 0), axis=1
    )
    keep_tail = jnp.where(is_start, 0.0, 1.0).astype(jnp.float32)
    tails_in = jnp.take(all_tails, pred_slot, axis=0) * keep_tail[:, None, None]
    activated, conv_vjp = jax.vjp(conv_prep, conv_blocks, tails_in, short_filter)
    heads_x = activated[:, :, :DSSM].reshape(2, block_rows, MHEADS, HEAD_M)
    b_in = activated[:, :, DSSM : DSSM + NSTATE]
    c_in = activated[:, :, DSSM + NSTATE :]
    (emitted, emit_totals), emit_vjp = jax.vjp(
        jax.vmap(ssd_emit), heads_x, b_in, step_blocks, decay_blocks
    )
    zero_states = jnp.zeros((2, MHEADS, HEAD_M, NSTATE), jnp.float32)
    chain_forward = chain_fold(
        slot_block, my_blocks, block_second, first_len, block_rows, prefix, False
    )
    state_in = chain_forward(
        zero_states,
        lax.all_gather(emitted.astype(jnp.bfloat16), "ctx", axis=0, tiled=True),
        jnp.int32(0),
    )
    mixer_y, out_vjp = jax.vjp(
        jax.vmap(ssd_output, in_axes=(0, 0, 0, 0, 0, 0, None)),
        heads_x,
        b_in,
        c_in,
        step_blocks,
        decay_blocks,
        state_in,
        skip_gain,
    )
    mixer_flat = mixer_y.reshape(rows, DSSM)
    gated = (mixer_flat * jax.nn.silu(gate_z)).astype(jnp.bfloat16)
    mixer_branch = jnp.dot(gated, out_mix, preferred_element_type=jnp.float32)
    projected = jnp.dot(normed_first, in_attend, preferred_element_type=jnp.float32)
    cosines, sines = rope_tables(seq_pos)
    queries = rotate(projected[:, :AQ].reshape(rows, QH, HD), cosines, sines).astype(jnp.bfloat16)
    keys_rot = rotate(
        projected[:, AQ : AQ + kv_width].reshape(rows, KVH, HD), cosines, sines
    ).astype(jnp.bfloat16)
    values = projected[:, AQ + kv_width :].astype(jnp.bfloat16)
    kv_local = jnp.concatenate([keys_rot.reshape(rows, kv_width), values], axis=1)
    query_heads = queries.reshape(rows, KVH, GRP, HD)

    def allowed_at(start, count):
        piece_pos = lax.dynamic_slice_in_dim(key_pos, start, count)
        return (piece_pos[None, :] <= my_pos[:, None]) & (
            (piece_pos >= first_len)[None, :] == my_second[:, None]
        )

    def split_piece(piece):
        count = piece.shape[0]
        return (
            piece[:, :kv_width].reshape(count, KVH, HD),
            piece[:, kv_width:].reshape(count, KVH, HD),
        )

    def attend_step(carry, piece, start):
        top, denominator, running = carry
        keys_piece, values_piece = split_piece(piece)
        allowed = allowed_at(start, piece.shape[0])
        scores = (
            jnp.einsum(
                "tkgd,skd->kgts", query_heads, keys_piece, preferred_element_type=jnp.float32
            )
            * scale
        )
        masked = jnp.where(allowed, scores, NEG_LARGE)
        new_top = jnp.maximum(top, jnp.max(masked, axis=-1))
        weights = jnp.where(allowed, jnp.exp(masked - new_top[..., None]), 0.0)
        factor = jnp.exp(top - new_top)
        denominator = denominator * factor + jnp.sum(weights, axis=-1)
        running = running * factor[..., None] + jnp.einsum(
            "kgts,skd->kgtd", weights, values_piece.astype(jnp.float32), precision=HIGH
        )
        return (new_top, denominator, running)

    start_carry = (
        jnp.full((KVH, GRP, rows), NEG_LARGE, jnp.float32),
        jnp.zeros((KVH, GRP, rows), jnp.float32),
        jnp.zeros((KVH, GRP, rows, HD), jnp.float32),
    )
    top, denominator, running = in_blocks(
        attend_step, start_carry, lax.all_gather(kv_local, "ctx", axis=0, tiled=True)
    )
    log_total = top + jnp.log(denominator)
    attn_heads = running / denominator[..., None]
    attn_rows = jnp.transpose(attn_heads, (2, 0, 1, 3)).reshape(rows, AQ)
    attn_b = attn_rows.astype(jnp.bfloat16)
    attn_branch = jnp.dot(attn_b, out_attend, preferred_element_type=jnp.float32)
    hidden = tokens + mixer_branch + attn_branch
    normed2, second_norm_vjp = jax.vjp(rms_norm, hidden, gain_second)
    normed_second = normed2.astype(jnp.bfloat16)
    cot_b = cotangent.astype(jnp.bfloat16)
    gate_whole, down_rows = (
        lax.all_gather(gate_up, "wsh", axis=2, tiled=True),
        lax.all_gather(down_weight, "wsh", axis=0, tiled=True),
    )
    gate_cols = gate_whole[0]
    up_cols = gate_whole[1]
    gate_part = jnp.dot(normed_second, gate_cols, preferred_element_type=jnp.float32)
    up_part = jnp.dot(normed_second, up_cols, preferred_element_type=jnp.float32)
    mlp_act = (jax.nn.silu(gate_part) * up_part).astype(jnp.bfloat16)
    mlp_out = jnp.dot(mlp_act, down_rows, preferred_element_type=jnp.float32)
    output = hidden + mlp_out
    down_local = matmul_t(mlp_act, cot_b)
    d_mlp = matmul_back(cot_b, down_rows)
    d_gate = (d_mlp * up_part * silu_slope(gate_part)).astype(jnp.bfloat16)
    d_up = (d_mlp * jax.nn.silu(gate_part)).astype(jnp.bfloat16)
    gate_up_local = jnp.stack(
        [matmul_t(normed_second, d_gate), matmul_t(normed_second, d_up)], axis=0
    )
    d_normed_second = matmul_back(d_gate, gate_cols) + matmul_back(d_up, up_cols)
    d_hidden_norm, d_gain_second = second_norm_vjp(d_normed_second)
    hidden_grad = cotangent + d_hidden_norm
    hidden_b = hidden_grad.astype(jnp.bfloat16)
    attend_out_grad = matmul_t(attn_b, hidden_b)
    mixer_out_grad = matmul_t(gated, hidden_b)
    d_attn_b = matmul_back(hidden_b, out_attend).astype(jnp.bfloat16)
    d_gated = matmul_back(hidden_b, out_mix)
    d_heads = d_attn_b.reshape(rows, KVH, GRP, HD)
    d_heads_f = d_heads.astype(jnp.float32)
    query_f = queries.astype(jnp.float32).reshape(rows, KVH, GRP, HD)
    delta = jnp.sum(jnp.transpose(d_heads_f, (1, 2, 0, 3)) * attn_heads, axis=-1)

    def attend_back(carry, piece, start):
        query_grad, kv_grad = carry
        count = piece.shape[0]
        keys_piece, values_piece = split_piece(piece)
        allowed = allowed_at(start, count)
        scores = (
            jnp.einsum(
                "tkgd,skd->kgts", query_heads, keys_piece, preferred_element_type=jnp.float32
            )
            * scale
        )
        probs = jnp.where(
            allowed, jnp.exp(jnp.where(allowed, scores, 0.0) - log_total[..., None]), 0.0
        )
        d_probs = jnp.einsum(
            "tkgd,skd->kgts", d_heads, values_piece, preferred_element_type=jnp.float32
        )
        d_scores = probs * (d_probs - delta[..., None]) * scale
        query_grad = query_grad + jnp.einsum(
            "kgts,skd->tkgd", d_scores, keys_piece.astype(jnp.float32), precision=HIGH
        )
        key_grad = jnp.einsum("kgts,tkgd->skd", d_scores, query_f, precision=HIGH)
        value_grad = jnp.einsum("kgts,tkgd->skd", probs, d_heads_f, precision=HIGH)
        update = jnp.concatenate(
            [key_grad.reshape(count, kv_width), value_grad.reshape(count, kv_width)], axis=1
        )
        kv_grad = lax.dynamic_update_slice_in_dim(kv_grad, update, start, 0)
        return (query_grad, kv_grad)

    back_carry = (
        jnp.zeros((rows, KVH, GRP, HD), jnp.float32),
        jnp.zeros((block_count * block_rows, 2 * kv_width), jnp.float32),
    )
    query_grad, kv_grad = in_blocks(
        attend_back, back_carry, lax.all_gather(kv_local, "ctx", axis=0, tiled=True)
    )
    d_mixer = (d_gated * jax.nn.silu(gate_z)).reshape(2, block_rows, MHEADS, HEAD_M)
    d_z = d_gated * mixer_flat * silu_slope(gate_z)
    g_heads, g_b, g_c, g_step, g_decay, g_state, g_skip = out_vjp(d_mixer)
    chain_backward = chain_fold(
        slot_block, my_blocks, block_second, first_len, block_rows, prefix, True
    )
    later_sum = chain_backward(
        zero_states,
        lax.all_gather(g_state.astype(jnp.bfloat16), "ctx", axis=0, tiled=True),
        jnp.int32(0),
    )
    d_totals = jnp.exp(emit_totals) * jnp.sum(later_sum * state_in, axis=(2, 3))
    e_heads, e_b, e_step, e_decay = emit_vjp((later_sum, d_totals))
    d_activated = jnp.concatenate(
        [(g_heads + e_heads).reshape(2, block_rows, DSSM), g_b + e_b, g_c], axis=2
    )
    d_conv_blocks, d_tails, filter_grad = conv_vjp(d_activated)
    tail_buffer = (
        jnp.zeros((block_count, KERNEL - 1, CONV), jnp.float32)
        .at[pred_slot]
        .add(d_tails * keep_tail[:, None, None])
    )
    d_step_raw, step_bias_grad, log_rate_grad = step_vjp(
        ((g_step + e_step).reshape(rows, MHEADS), (g_decay + e_decay).reshape(rows, MHEADS))
    )
    kv_mine, tail_back, gate_up_part, down_part = (
        lax.psum_scatter(
            kv_grad.astype(jnp.bfloat16), "ctx", scatter_dimension=0, tiled=True
        ).astype(jnp.float32),
        lax.psum_scatter(
            tail_buffer.astype(jnp.bfloat16), "ctx", scatter_dimension=0, tiled=True
        ).astype(jnp.float32),
        lax.psum_scatter(
            gate_up_local.astype(jnp.bfloat16), "ctx", scatter_dimension=1, tiled=True
        ).astype(jnp.float32),
        lax.psum_scatter(
            down_local.astype(jnp.bfloat16), "ctx", scatter_dimension=1, tiled=True
        ).astype(jnp.float32),
    )
    d_query = rotate(query_grad.reshape(rows, QH, HD), cosines, -sines).reshape(rows, AQ)
    d_key = rotate(kv_mine[:, :kv_width].reshape(rows, KVH, HD), cosines, -sines).reshape(
        rows, kv_width
    )
    d_attend = jnp.concatenate([d_query, d_key, kv_mine[:, kv_width:]], axis=1).astype(jnp.bfloat16)
    attend_in_grad = matmul_t(normed_first, d_attend)
    d_normed_attend = matmul_back(d_attend, in_attend)
    d_conv_blocks = d_conv_blocks.at[:, block_rows - (KERNEL - 1) :, :].add(tail_back)
    d_mixed = jnp.concatenate([d_z, d_conv_blocks.reshape(rows, CONV), d_step_raw], axis=1).astype(
        jnp.bfloat16
    )
    mixer_in_grad = matmul_t(normed_first, d_mixed)
    d_normed_mix = matmul_back(d_mixed, in_mix)
    d_tokens_norm, d_gain_first = first_norm_vjp(d_normed_mix + d_normed_attend)
    input_grad = hidden_grad + d_tokens_norm
    gains_grad = jnp.stack([d_gain_first, d_gain_second], axis=0)
    step_bias_grad, log_rate_grad, skip_grad, filter_grad = lax.psum(
        (step_bias_grad, log_rate_grad, g_skip, filter_grad), ("ctx", "wsh")
    )
    gate_up_grad, down_grad = (
        lax.psum_scatter(
            gate_up_part.astype(jnp.bfloat16), "wsh", scatter_dimension=2, tiled=True
        ).astype(jnp.float32),
        lax.psum_scatter(
            down_part.astype(jnp.bfloat16), "wsh", scatter_dimension=0, tiled=True
        ).astype(jnp.float32),
    )
    results = (
        lax.psum_scatter(gains_grad, ("ctx", "wsh"), scatter_dimension=1, tiled=True),
        lax.psum_scatter(mixer_in_grad, ("ctx", "wsh"), scatter_dimension=0, tiled=True),
        lax.psum_scatter(mixer_out_grad, ("ctx", "wsh"), scatter_dimension=1, tiled=True),
        lax.psum_scatter(attend_in_grad, ("ctx", "wsh"), scatter_dimension=0, tiled=True),
        lax.psum_scatter(attend_out_grad, ("ctx", "wsh"), scatter_dimension=1, tiled=True),
    )
    return (
        output[None],
        input_grad[None],
        results[0],
        filter_grad,
        step_bias_grad,
        log_rate_grad,
        skip_grad,
        results[1],
        results[2],
        results[3],
        results[4],
        gate_up_grad,
        down_grad,
    )


def xor_pairs(count, bits):
    return [(index, index ^ bits) for index in range(count)]


def held_order(count):
    return list(range(0, count, 2)) + list(range(1, count, 2))


def gather_ctx(values, with_far=False):
    count = lax.axis_size("ctx")
    first_core = lax.axis_index("ctx") % 2 == 0
    near_x = lax.ppermute(values, "ctx", xor_pairs(count, 2))
    near_y = lax.ppermute(values, "ctx", xor_pairs(count, 4))
    far = lax.ppermute(
        jnp.where(first_core, near_x, near_y),
        "ctx",
        [(index, index ^ (4 if index % 2 == 0 else 2)) for index in range(count)],
    )
    mine = jnp.stack([values, near_x, near_y, far], axis=0)
    other = lax.ppermute(mine, "ctx", xor_pairs(count, 1))
    whole = jnp.concatenate([mine, other], axis=0)
    return (whole, far) if with_far else whole


def scatter_ctx(parts):
    count = lax.axis_size("ctx")
    half = count // 2
    first_core = lax.axis_index("ctx") % 2 == 0
    wire = lambda piece: piece.astype(jnp.bfloat16)
    crossed = lax.ppermute(wire(parts[half:]), "ctx", xor_pairs(count, 1))
    sums = parts[:half] + crossed.astype(jnp.float32)
    own, near_x, near_y, far = [sums[place] for place in range(half)]
    passed = lax.ppermute(
        wire(far), "ctx", [(index, index ^ (2 if index % 2 == 0 else 4)) for index in range(count)]
    ).astype(jnp.float32)
    near_y = near_y + jnp.where(first_core, passed, 0.0)
    near_x = near_x + jnp.where(first_core, 0.0, passed)
    return (
        own
        + lax.ppermute(wire(near_x), "ctx", xor_pairs(count, 2)).astype(jnp.float32)
        + lax.ppermute(wire(near_y), "ctx", xor_pairs(count, 4)).astype(jnp.float32)
    )


def trade_ctx(parts):
    return lax.all_to_all(parts, "ctx", 0, 0, tiled=True)


def after(values, anchor):
    return lax.optimization_barrier((values, anchor))[0]


def swap_groups(pieces):
    count = lax.axis_size("wsh")
    return [pieces[0]] + [
        lax.ppermute(pieces[k], "wsh", xor_pairs(count, k)) for k in range(1, count)
    ]


def gather_wsh(values, axis=0):
    count = lax.axis_size("wsh")
    shape = list(values.shape)
    size = shape[axis]
    shape[axis] = size * count
    whole = jnp.zeros(shape, values.dtype)
    for k, piece in enumerate(swap_groups([values] * count)):
        start = (lax.axis_index("wsh") ^ k) * size
        whole = lax.dynamic_update_slice_in_dim(whole, piece, start, axis)
    return whole


def dot_dims(left, right, left_dim, right_dim, precision=None):
    return lax.dot_general(
        left,
        right,
        (((left_dim,), (right_dim,)), ((), ())),
        precision=precision,
        preferred_element_type=jnp.float32,
    )


def spread(per_head, heads, lanes):
    return jnp.concatenate(
        [jnp.broadcast_to(item, (item.shape[0], lanes)) for item in per_head[:heads]], axis=1
    )


def turn(values, table, back=False):
    half = HD // 2
    swapped = jnp.concatenate([values[:, half:], values[:, :half]], axis=1)
    side = swapped * table[:, HD:]
    return values * table[:, :HD] - side if back else values * table[:, :HD] + side


def filtered(ext_ref, filt_ref, rows):
    conv = filt_ref[KERNEL : KERNEL + 1, :] + filt_ref[KERNEL - 1 : KERNEL, :] * ext_ref[8:, :]
    for tap in range(KERNEL - 1):
        start = 8 - (KERNEL - 1) + tap
        conv = conv + filt_ref[tap : tap + 1, :] * ext_ref[start : start + rows, :]
    return conv


def softplus(values):
    return jnp.maximum(values, 0.0) + jnp.log1p(jnp.exp(-jnp.abs(values)))


def block_decay(step_in, rate, rows):
    step = softplus(step_in)
    decay = -step * rate
    lower = lax.broadcasted_iota(jnp.int32, (rows, rows), 0) >= lax.broadcasted_iota(
        jnp.int32, (rows, rows), 1
    )
    ones = jnp.where(lower, 1.0, 0.0)
    cum = dot_dims(ones, decay, 1, 0, HIGH)
    cum_t = dot_dims(decay, ones, 0, 1, HIGH)
    return step, decay, lower, ones, cum, cum_t


def pick_kernel(heads, where_ref, *refs):
    xs, zs = refs[:heads], refs[heads : 2 * heads]
    bc0, step0, q0, k0, v0, gain_ref, out_ref, all_ref = refs[2 * heads :]
    chans = heads * HEAD_M
    ctx = where_ref[0]
    gain = gain_ref[0:1, :].astype(jnp.float32)
    width = gain.shape[1]

    def put(start, values):
        all_ref[start : start + values.shape[0], :] = values.astype(jnp.float32) * gain

    def half_tile(ref, odd):
        window = jnp.transpose(ref[...].astype(jnp.float32))
        return jnp.where(odd, window[HD:, :], window[:HD, :])

    for h in range(heads):
        put(h * HEAD_M, xs[h][...])
        put(256 + h * HEAD_M, zs[h][...])
    put(chans, half_tile(q0, ctx % 2 == 1))
    put(256 + chans, half_tile(k0, where_ref[1] % 2 == 1))
    put(512, bc0[...])
    put(768, half_tile(v0, where_ref[1] % 2 == 1))
    row = lax.broadcasted_iota(jnp.int32, (HEAD_M, width), 0)
    steps = jnp.where(row < MHEADS, step0[...].astype(jnp.float32), 0.0).astype(jnp.bfloat16)
    there = lax.broadcasted_iota(jnp.int32, (HEAD_M, HEAD_M), 0)
    here = lax.broadcasted_iota(jnp.int32, (HEAD_M, HEAD_M), 1)
    chosen = jnp.where((here == there + ctx * heads) & (there < heads), 1.0, 0.0)
    put(768 + HD, dot_dims(chosen.astype(jnp.bfloat16), steps, 1, 0))
    turn_row = lax.broadcasted_iota(jnp.int32, (16, width), 0)
    second = gain_ref[1:2, :].astype(jnp.float32)
    both = jnp.where(turn_row == 0, gain, jnp.where(turn_row == 1, second, 0.0))
    all_ref[GAIN_ROW : GAIN_ROW + 16, :] = both
    out_ref[...] = jnp.transpose(all_ref[...]).astype(jnp.bfloat16)


def pick_columns(where, mixer_in, attend_in, gains, heads):
    width = mixer_in.shape[0]
    turned = jnp.transpose(mixer_in)
    rows_at = lambda start: pl.BlockSpec((HEAD_M, width), lambda i, s: (start(s) // HEAD_M, 0))
    tile_at = lambda start: pl.BlockSpec((width, 128), lambda i, s: (0, start(s) // 128))
    from_x = [rows_at(lambda s, h=h: DSSM + (s[0] * heads + h) * HEAD_M) for h in range(heads)]
    from_z = [rows_at(lambda s, h=h: (s[0] * heads + h) * HEAD_M) for h in range(heads)]
    return pl.pallas_call(
        partial(pick_kernel, heads),
        out_shape=jax.ShapeDtypeStruct((width, 896), jnp.bfloat16),
        grid_spec=pltpu.PrefetchScalarGridSpec(
            num_scalar_prefetch=1,
            grid=(1,),
            in_specs=from_x
            + from_z
            + [
                pl.BlockSpec((2 * NSTATE, width), lambda i, s: (DSSM // NSTATE, 0)),
                rows_at(lambda s: DSSM + CONV),
                tile_at(lambda s: s[0] * HD),
                tile_at(lambda s: AQ + s[1] * HD),
                tile_at(lambda s: AQ + KVH * HD + s[1] * HD),
                pl.BlockSpec(gains.shape, lambda i, s: (0, 0)),
            ],
            out_specs=pl.BlockSpec((width, 896), lambda i, s: (0, 0)),
            scratch_shapes=[pltpu.VMEM((896, width), jnp.float32)],
        ),
        name="pick_columns",
    )(where, *[turned] * (2 * heads + 2), *[attend_in] * 3, gains)


def finish_in_kernel(heads, final_ref, mixer_ref, attend_ref, last_ref):
    count = final_ref.shape[0]
    chans = heads * HEAD_M
    share = final_ref.shape[1]
    parts = [final_ref[c].astype(jnp.float32) for c in range(count)]
    beside = lambda start, size: jnp.concatenate([p[:, start : start + size] for p in parts], axis=1)
    mixer_ref[:, :DSSM] = beside(256, chans)
    mixer_ref[:, DSSM : 2 * DSSM] = beside(0, chans)
    mixer_ref[:, 2 * DSSM : 2 * DSSM + 2 * NSTATE] = sum(p[:, 512:768] for p in parts)
    lane = lax.broadcasted_iota(jnp.int32, (128, MHEADS), 0)
    head = lax.broadcasted_iota(jnp.int32, (128, MHEADS), 1)
    steps = jnp.zeros((share, MHEADS), jnp.float32)
    for c in range(count):
        chosen = jnp.where((lane - HD == head - c * heads) & (lane >= HD) & (lane < HD + heads), 1.0, 0.0)
        steps = steps + dot_dims(final_ref[c, :, 768:896], chosen.astype(jnp.bfloat16), 1, 0)
    mixer_ref[:, DSSM + CONV :] = steps
    attend_ref[:, :AQ] = beside(chans, HD)
    each = count // KVH
    for start, place in ((256 + chans, AQ), (768, AQ + KVH * HD)):
        attend_ref[:, place : place + KVH * HD] = jnp.concatenate(
            [
                sum(p[:, start : start + HD] for p in parts[head_ * each : (head_ + 1) * each])
                for head_ in range(KVH)
            ],
            axis=1,
        )
    last_ref[...] = sum(p[:, 768:896] for p in parts)


def finish_in(final, heads):
    share = final.shape[1]
    return pl.pallas_call(
        partial(finish_in_kernel, heads),
        out_shape=(
            jax.ShapeDtypeStruct((share, DSSM + CONV + MHEADS), jnp.float32),
            jax.ShapeDtypeStruct((share, AQ + 2 * KVH * HD), jnp.float32),
            jax.ShapeDtypeStruct((share, 128), jnp.float32),
        ),
        name="finish_in",
    )(final)


def finish_rest_kernel(chans, units, share, parts_ref, gate_up_ref, down_ref, mixer_ref, attend_ref):
    count = parts_ref.shape[0]
    parts = [parts_ref[c].astype(jnp.float32) for c in range(count)]
    for place in range(2):
        gate_up_ref[place] = jnp.concatenate(
            [jnp.transpose(p[place * units : (place + 1) * units]) for p in parts], axis=1
        )
    outs = []
    for c, p in enumerate(parts):
        down_ref[c * units : (c + 1) * units, :] = p[2 * units : 3 * units]
        rest = range(3 * units, p.shape[0], share)
        outs.append(jnp.concatenate([p[start : start + share] for start in rest], axis=1))
    mixer_ref[...] = jnp.concatenate([item[:, :chans] for item in outs], axis=1)
    attend_ref[...] = jnp.concatenate([item[:, chans:] for item in outs], axis=1)


def finish_rest(parts, chans, units, share):
    count, _, wide = parts.shape
    return pl.pallas_call(
        partial(finish_rest_kernel, chans, units, share),
        out_shape=(
            jax.ShapeDtypeStruct((2, wide, count * units), jnp.float32),
            jax.ShapeDtypeStruct((count * units, wide), jnp.float32),
            jax.ShapeDtypeStruct((share, count * chans), jnp.float32),
            jax.ShapeDtypeStruct((share, count * HD), jnp.float32),
        ),
        name="finish_rest",
    )(parts)


def forward_kernel(
    heads, base, sched_ref, proj_ref, filt_ref, table_ref, params_ref, skip_ref,
    held_ref, save_ref, state_ref, kv_ref, ext_ref, chain_ref, keys_ref, values_ref,
):
    index = pl.program_id(0)
    blocks = pl.num_programs(0)
    rows = proj_ref.shape[1]
    chans = heads * HEAD_M
    seq_start = sched_ref[blocks + index]

    @pl.when(index == 0)
    def _():
        keys_ref[...] = jnp.zeros_like(keys_ref)
        values_ref[...] = jnp.zeros_like(values_ref)

    @pl.when(seq_start == index * rows)
    def _():
        ext_ref[0:8, :] = jnp.zeros((8, ext_ref.shape[1]), jnp.float32)
        chain_ref[...] = jnp.zeros_like(chain_ref)

    proj = proj_ref[0]
    ext_ref[8:, :] = jnp.concatenate([proj[:, :256], proj[:, 512:768]], axis=1)
    conv = filtered(ext_ref, filt_ref, rows)
    ext_ref[0:8, :] = ext_ref[rows:, :]
    act = conv * jax.nn.sigmoid(conv)
    heads_x = act[:, :chans]
    b_in = act[:, 256 : 256 + NSTATE]
    c_in = act[:, 256 + NSTATE : 256 + 2 * NSTATE]
    step, _, lower, _, cum, cum_t = block_decay(
        proj[:, 768:] + params_ref[0:1, :], params_ref[1:2, :], rows
    )
    cum_cols = [cum[:, base + h : base + h + 1] for h in range(heads)]
    mix = dot_dims(c_in, b_in, 1, 1, SSD)
    fed = heads_x * spread([step[:, base + h : base + h + 1] for h in range(heads)], heads, HEAD_M)
    state = chain_ref[...]
    state_ref[0] = state
    inner = []
    for h in range(heads):
        gaps = jnp.where(lower, cum_cols[h] - cum_t[base + h : base + h + 1, :], 0.0)
        kernel = jnp.where(lower, jnp.exp(gaps), 0.0) * mix
        inner.append(dot_dims(kernel, fed[:, h * HEAD_M : (h + 1) * HEAD_M], 1, 0, SSD))
    growth = spread([jnp.exp(item) for item in cum_cols], heads, HEAD_M)
    inner = jnp.concatenate(inner, axis=1) + dot_dims(c_in, state, 1, 1, SSD) * growth
    ends = [item[rows - 1 : rows, :] for item in cum_cols]
    tail = spread([jnp.exp(end - item) for end, item in zip(ends, cum_cols)], heads, HEAD_M)
    emitted = dot_dims(fed * tail, b_in, 0, 0, SSD)
    for h in range(heads):
        part = slice(h * HEAD_M, (h + 1) * HEAD_M)
        chain_ref[part, :] = jnp.exp(ends[h]) * state[part, :] + emitted[part, :]
    gate_z = proj[:, 256 : 256 + chans]
    gated = (inner + skip_ref[0:1, :] * heads_x) * (gate_z * jax.nn.sigmoid(gate_z))

    table = table_ref[0]
    query = turn(proj[:, chans : chans + HD], table).astype(jnp.bfloat16)
    key = turn(proj[:, 256 + chans : 256 + chans + HD], table).astype(jnp.bfloat16)
    value = proj[:, 768 : 768 + HD].astype(jnp.bfloat16)
    here = pl.ds(pl.multiple_of(index * rows, rows), rows)
    keys_ref[here, :] = key
    values_ref[here, :] = value
    kv_ref[0] = jnp.concatenate([key, value], axis=1)
    total = keys_ref.shape[0]
    key_pos = lax.broadcasted_iota(jnp.int32, (rows, total), 1)
    my_pos = index * rows + lax.broadcasted_iota(jnp.int32, (rows, total), 0)
    allowed = (key_pos <= my_pos) & (key_pos >= seq_start)
    scores = jnp.where(
        allowed, dot_dims(query, keys_ref[...], 1, 1) * (1.0 / math.sqrt(HD)), NEG_LARGE
    )
    top = jnp.max(scores, axis=-1, keepdims=True)
    weights = jnp.exp(scores - top)
    denominator = jnp.sum(weights, axis=-1, keepdims=True)
    attn = dot_dims(weights.astype(jnp.bfloat16), values_ref[...], 1, 0) / denominator
    log_total = jnp.broadcast_to(top + jnp.log(denominator), (rows, 128))
    save_ref[0] = jnp.concatenate([inner, attn, log_total], axis=1)
    held_ref[0] = jnp.concatenate([gated, attn], axis=1).astype(jnp.bfloat16)


def backward_kernel(
    heads, base, sched_ref, proj_ref, before_ref, filt_ref, table_ref, params_ref, skip_ref,
    save_ref, state_ref, kv_ref, d_mix_ref,
    d_ref, filt_grad_ref, head_grad_ref, ext_ref, next_ref, later_ref, keys_ref, values_ref,
):
    blocks = pl.num_programs(0)
    turn_index = pl.program_id(0)
    index = blocks - 1 - turn_index
    rows = proj_ref.shape[1]
    chans = heads * HEAD_M
    seq_start = sched_ref[blocks + index]
    after = jnp.minimum(index + 1, blocks - 1)
    is_end = (index == blocks - 1) | (sched_ref[blocks + after] == after * rows)

    @pl.when(turn_index == 0)
    def _():
        keys_ref[...] = jnp.zeros_like(keys_ref)
        values_ref[...] = jnp.zeros_like(values_ref)
        filt_grad_ref[...] = jnp.zeros_like(filt_grad_ref)
        head_grad_ref[...] = jnp.zeros_like(head_grad_ref)

    @pl.when(is_end)
    def _():
        next_ref[rows:, :] = jnp.zeros((8, next_ref.shape[1]), jnp.float32)
        later_ref[...] = jnp.zeros_like(later_ref)

    proj = proj_ref[0]
    keep = jnp.where(seq_start == index * rows, 0.0, 1.0)
    before = before_ref[0]
    ext_ref[0:8, :] = jnp.concatenate([before[:, :256], before[:, 512:768]], axis=1) * keep
    ext_ref[8:, :] = jnp.concatenate([proj[:, :256], proj[:, 512:768]], axis=1)
    conv = filtered(ext_ref, filt_ref, rows)
    conv_sig = jax.nn.sigmoid(conv)
    act = conv * conv_sig
    heads_x = act[:, :chans]
    b_in = act[:, 256 : 256 + NSTATE]
    c_in = act[:, 256 + NSTATE : 256 + 2 * NSTATE]
    step_in = proj[:, 768:] + params_ref[0:1, :]
    rate = params_ref[1:2, :]
    step, decay, lower, ones, cum, cum_t = block_decay(step_in, rate, rows)
    cum_cols = [cum[:, base + h : base + h + 1] for h in range(heads)]
    step_cols = spread([step[:, base + h : base + h + 1] for h in range(heads)], heads, HEAD_M)
    mix = dot_dims(c_in, b_in, 1, 1, SSD)
    fed = heads_x * step_cols
    state = state_ref[0]
    later = later_ref[...]
    save = save_ref[0]
    inner = save[:, :chans]
    skip = skip_ref[0:1, :]

    d_mix = d_mix_ref[0]
    d_gated = d_mix[:, :chans]
    gate_z = proj[:, 256 : 256 + chans]
    gate_sig = jax.nn.sigmoid(gate_z)
    d_z = d_gated * (inner + skip * heads_x) * (gate_sig * (1.0 + gate_z * (1.0 - gate_sig)))
    d_y = d_gated * (gate_z * gate_sig)
    growth = spread([jnp.exp(item) for item in cum_cols], heads, HEAD_M)
    ends = [item[rows - 1 : rows, :] for item in cum_cols]
    tail = spread([jnp.exp(end - item) for end, item in zip(ends, cum_cols)], heads, HEAD_M)
    grown = d_y * growth
    fed_tail = fed * tail
    fed_inner = []
    d_mixing = jnp.zeros((rows, rows), jnp.float32)
    for h in range(heads):
        part = slice(h * HEAD_M, (h + 1) * HEAD_M)
        gaps = jnp.where(lower, cum_cols[h] - cum_t[base + h : base + h + 1, :], 0.0)
        decays = jnp.where(lower, jnp.exp(gaps), 0.0)
        fed_inner.append(dot_dims(decays * mix, d_y[:, part], 0, 0, SSD))
        d_mixing = d_mixing + dot_dims(d_y[:, part], fed[:, part], 1, 1, SSD) * decays
    fed_emit = dot_dims(b_in, later, 1, 1, SSD) * tail
    d_fed = jnp.concatenate(fed_inner, axis=1) + fed_emit
    d_c = dot_dims(d_mixing, b_in, 1, 0, SSD) + dot_dims(grown, state, 1, 0, SSD)
    d_b = dot_dims(d_mixing, c_in, 0, 0, SSD) + dot_dims(fed_tail, later, 1, 0, SSD)
    state_grad = dot_dims(grown, c_in, 0, 0, SSD)
    d_x = d_fed * step_cols + skip * d_y
    lane = lax.broadcasted_iota(jnp.int32, (1, 128), 1)
    d_cum = jnp.zeros((rows, 128), jnp.float32)
    d_step = jnp.zeros((rows, 128), jnp.float32)
    d_total = jnp.zeros((1, 128), jnp.float32)
    skip_sum = jnp.zeros((1, 128), jnp.float32)
    cum_terms = d_y * inner - fed * d_fed
    step_terms = d_fed * heads_x
    emit_terms = fed * fed_emit
    skip_terms = d_y * heads_x
    carry_terms = later * state
    for h in range(heads):
        part = slice(h * HEAD_M, (h + 1) * HEAD_M)
        mine = jnp.where(lane == base + h, 1.0, 0.0)
        growth_end = jnp.exp(ends[h])
        d_cum = d_cum + jnp.sum(cum_terms[:, part], axis=1, keepdims=True) * mine
        d_step = d_step + jnp.sum(step_terms[:, part], axis=1, keepdims=True) * mine
        carry = jnp.sum(jnp.sum(carry_terms[part, :], axis=0, keepdims=True), axis=1, keepdims=True)
        emit = jnp.sum(jnp.sum(emit_terms[:, part], axis=0, keepdims=True), axis=1, keepdims=True)
        skips = jnp.sum(jnp.sum(skip_terms[:, part], axis=0, keepdims=True), axis=1, keepdims=True)
        d_total = d_total + (growth_end * carry + emit) * mine
        skip_sum = skip_sum + skips * mine
        later_ref[part, :] = state_grad[part, :] + growth_end * later[part, :]
    d_decay = dot_dims(ones, d_cum, 0, 0, HIGH) + d_total
    d_step = (d_step - d_decay * rate) * jax.nn.sigmoid(step_in)
    d_step = jnp.where((lane >= base) & (lane < base + heads), d_step, 0.0)
    head_grad_ref[0:1, :] += jnp.sum(d_step, axis=0, keepdims=True)
    head_grad_ref[1:2, :] += jnp.sum(d_decay * decay, axis=0, keepdims=True)
    head_grad_ref[2:3, :] += skip_sum

    d_conv = jnp.concatenate([d_x, jnp.zeros((rows, 256 - chans), jnp.float32), d_b, d_c], axis=1)
    d_conv = d_conv * (conv_sig * (1.0 + conv * (1.0 - conv_sig)))
    next_ref[0:rows, :] = d_conv
    d_in = filt_ref[KERNEL - 1 : KERNEL, :] * d_conv
    for tap in range(KERNEL - 1):
        shift = KERNEL - 1 - tap
        d_in = d_in + filt_ref[tap : tap + 1, :] * next_ref[shift : shift + rows, :]
        filt_grad_ref[tap : tap + 1, :] += jnp.sum(
            d_conv * ext_ref[8 - shift : 8 - shift + rows, :], axis=0, keepdims=True
        )
    filt_grad_ref[KERNEL - 1 : KERNEL, :] += jnp.sum(d_conv * ext_ref[8:, :], axis=0, keepdims=True)
    filt_grad_ref[KERNEL : KERNEL + 1, :] += jnp.sum(d_conv, axis=0, keepdims=True)
    next_ref[rows:, :] = d_conv[0:8, :]

    table = table_ref[0]
    scale = 1.0 / math.sqrt(HD)
    query = turn(proj[:, chans : chans + HD], table).astype(jnp.bfloat16)
    keys = kv_ref[:, :HD]
    values = kv_ref[:, HD:]
    d_attn = d_mix[:, chans : chans + HD].astype(jnp.bfloat16)
    delta = jnp.sum(d_attn.astype(jnp.float32) * save[:, chans : chans + HD], axis=1, keepdims=True)
    total = keys.shape[0]
    key_pos = lax.broadcasted_iota(jnp.int32, (rows, total), 1)
    my_pos = index * rows + lax.broadcasted_iota(jnp.int32, (rows, total), 0)
    allowed = (key_pos <= my_pos) & (key_pos >= seq_start)
    scores = jnp.where(allowed, dot_dims(query, keys, 1, 1) * scale, NEG_LARGE)
    probs = jnp.exp(scores - save[:, chans + HD : chans + HD + 1])
    d_scores = (probs * (dot_dims(d_attn, values, 1, 1) - delta) * scale).astype(jnp.bfloat16)
    d_query = turn(dot_dims(d_scores, keys, 1, 0), table, back=True)
    keys_ref[...] += dot_dims(d_scores, query, 0, 0)
    values_ref[...] += dot_dims(probs.astype(jnp.bfloat16), d_attn, 0, 0)
    here = pl.ds(pl.multiple_of(index * rows, rows), rows)
    d_key = turn(keys_ref[here, :], table, back=True)
    d_value = values_ref[here, :]
    d_ref[0] = jnp.concatenate(
        [d_in[:, :chans], d_query, d_z, d_key, d_in[:, 256:], d_value, d_step[:, HD:]], axis=1
    ).astype(jnp.bfloat16)


def mixer_forward(sched, proj, filt, table, params, skip, heads, base):
    blocks, rows, wide = proj.shape
    chans = heads * HEAD_M
    held = lambda b, s: (s[b], 0, 0)
    plain = lambda b, s: (b, 0, 0)
    whole = lambda b, s: (0, 0)
    return pl.pallas_call(
        partial(forward_kernel, heads, base),
        out_shape=(
            jax.ShapeDtypeStruct((blocks, rows, 256), jnp.bfloat16),
            jax.ShapeDtypeStruct((blocks, rows, 384), jnp.float32),
            jax.ShapeDtypeStruct((blocks, chans, NSTATE), jnp.float32),
            jax.ShapeDtypeStruct((blocks, rows, 2 * HD), jnp.bfloat16),
        ),
        grid_spec=pltpu.PrefetchScalarGridSpec(
            num_scalar_prefetch=1,
            grid=(blocks,),
            in_specs=[
                pl.BlockSpec((1, rows, wide), held),
                pl.BlockSpec(filt.shape, whole),
                pl.BlockSpec((1, rows, 2 * HD), plain),
                pl.BlockSpec(params.shape, whole),
                pl.BlockSpec(skip.shape, whole),
            ],
            out_specs=(
                pl.BlockSpec((1, rows, 256), held),
                pl.BlockSpec((1, rows, 384), plain),
                pl.BlockSpec((1, chans, NSTATE), plain),
                pl.BlockSpec((1, rows, 2 * HD), plain),
            ),
            scratch_shapes=[
                pltpu.VMEM((rows + 8, 512), jnp.float32),
                pltpu.VMEM((chans, NSTATE), jnp.float32),
                pltpu.VMEM((blocks * rows, HD), jnp.bfloat16),
                pltpu.VMEM((blocks * rows, HD), jnp.bfloat16),
            ],
        ),
        cost_estimate=pl.CostEstimate(
            flops=25_000_000_000, transcendentals=0, bytes_accessed=12_000_000
        ),
        name="mixer_forward",
    )(sched, proj, filt, table, params, skip)


def mixer_backward(sched, proj, filt, table, params, skip, save, states, kv, d_mix, heads, base):
    blocks, rows, wide = proj.shape
    chans = heads * HEAD_M
    held = lambda i, s: (s[blocks - 1 - i], 0, 0)
    before = lambda i, s: (s[jnp.maximum(blocks - 2 - i, 0)], rows // 8 - 1, 0)
    plain = lambda i, s: (blocks - 1 - i, 0, 0)
    whole = lambda i, s: (0, 0)
    return pl.pallas_call(
        partial(backward_kernel, heads, base),
        out_shape=(
            jax.ShapeDtypeStruct((blocks, rows, wide), jnp.bfloat16),
            jax.ShapeDtypeStruct((8, 512), jnp.float32),
            jax.ShapeDtypeStruct((8, 128), jnp.float32),
        ),
        grid_spec=pltpu.PrefetchScalarGridSpec(
            num_scalar_prefetch=1,
            grid=(blocks,),
            in_specs=[
                pl.BlockSpec((1, rows, wide), held),
                pl.BlockSpec((1, 8, wide), before),
                pl.BlockSpec(filt.shape, whole),
                pl.BlockSpec((1, rows, 2 * HD), plain),
                pl.BlockSpec(params.shape, whole),
                pl.BlockSpec(skip.shape, whole),
                pl.BlockSpec((1, rows, 384), plain),
                pl.BlockSpec((1, chans, NSTATE), plain),
                pl.BlockSpec((blocks * rows, 2 * HD), whole),
                pl.BlockSpec((1, rows, 256), held),
            ],
            out_specs=(
                pl.BlockSpec((1, rows, wide), held),
                pl.BlockSpec((8, 512), whole),
                pl.BlockSpec((8, 128), whole),
            ),
            scratch_shapes=[
                pltpu.VMEM((rows + 8, 512), jnp.float32),
                pltpu.VMEM((rows + 8, 512), jnp.float32),
                pltpu.VMEM((chans, NSTATE), jnp.float32),
                pltpu.VMEM((blocks * rows, HD), jnp.float32),
                pltpu.VMEM((blocks * rows, HD), jnp.float32),
            ],
        ),
        cost_estimate=pl.CostEstimate(
            flops=40_000_000_000, transcendentals=0, bytes_accessed=16_000_000
        ),
        name="mixer_backward",
    )(sched, proj, proj, filt, table, params, skip, save, states, kv.reshape(-1, 2 * HD), d_mix)


def head_plan(
    block_input,
    out_cotangent,
    lengths,
    slot_block,
    norm_gains,
    short_filter,
    step_bias,
    log_rate,
    skip_gain,
    mixer_in,
    mixer_out,
    attend_in,
    attend_out,
    gate_up,
    down_weight,
):
    count = lax.axis_size("ctx")
    groups = lax.axis_size("wsh")
    ctx = lax.axis_index("ctx")
    wsh = lax.axis_index("wsh")
    rows, width = block_input.shape[1:]
    block_rows = rows // 2
    blocks = 2 * count
    total_rows = count * rows
    heads = MHEADS // count
    chans = heads * HEAD_M
    kv_head = ctx * KVH // count
    units = gate_up.shape[2] // count
    first_len = lengths[0, 0]
    tokens = block_input[0]
    cotangent = out_cotangent[0]
    cols = lambda array, start, size: lax.dynamic_slice_in_dim(array, start, size, array.ndim - 1)
    base = HD
    step_pad = 128 - base - heads

    in_cols = pick_columns(
        jnp.stack([ctx, kv_head]), mixer_in, attend_in, norm_gains, heads
    )
    in_all = gather_wsh(in_cols)
    gains = jnp.transpose(in_all[:, GAIN_ROW : GAIN_ROW + 2].astype(jnp.float32))
    out_rows = jnp.concatenate(
        [
            lax.dynamic_slice_in_dim(mixer_out, ctx * chans, chans, 0),
            lax.dynamic_slice_in_dim(attend_out, ctx * HD, HD, 0),
        ],
        axis=0,
    )
    mlp_pack = jnp.concatenate(
        [
            jnp.transpose(cols(gate_up[0], ctx * units, units)),
            jnp.transpose(cols(gate_up[1], ctx * units, units)),
            lax.dynamic_slice_in_dim(down_weight, ctx * units, units, 0),
        ],
        axis=0,
    )
    out_rows, mlp_pack = after((out_rows, mlp_pack), in_all)
    out_mine = gather_wsh(out_rows, 1)
    packs = swap_groups([mlp_pack] * groups)
    gate_up_rows = jnp.concatenate(
        [pack[:units] for pack in packs] + [pack[units : 2 * units] for pack in packs], axis=0
    )
    down_all = jnp.concatenate([pack[2 * units :] for pack in packs], axis=0)

    peers = ctx ^ jnp.array(held_order(count), dtype=jnp.int32)
    held = jnp.take(slot_block.reshape(count, 2), peers, axis=0, mode="clip").reshape(blocks)
    logical_ids = jnp.arange(blocks, dtype=jnp.int32)

    place = jnp.sum(
        jnp.where(held[None, :] == logical_ids[:, None], logical_ids[None, :], 0), axis=1
    )
    starts = jnp.where(logical_ids * block_rows >= first_len, first_len, 0)
    sched = jnp.concatenate([place, starts])
    positions = jnp.arange(total_rows, dtype=jnp.int32)
    seq_pos = positions - jnp.where(positions >= first_len, first_len, 0)
    half = HD // 2
    freqs = jnp.exp(jnp.arange(half, dtype=jnp.float32) * (-2.0 * math.log(ROPE_BASE) / HD))
    angles = seq_pos.astype(jnp.float32)[:, None] * freqs[None, :]
    cosines = jnp.cos(angles)
    sines = jnp.sin(angles)
    table = jnp.concatenate([cosines, cosines, -sines, sines], axis=1)
    table = table.reshape(blocks, block_rows, 2 * HD)
    filt = jnp.concatenate(
        [
            cols(short_filter, ctx * chans, chans),
            jnp.zeros((KERNEL + 1, HD), jnp.float32),
            short_filter[:, DSSM:],
        ],
        axis=1,
    )
    filt = jnp.pad(filt, ((0, 7 - KERNEL), (0, 0)))
    mine = lambda array: lax.dynamic_slice_in_dim(array, ctx * heads, heads)
    params = jnp.stack([mine(step_bias), jnp.exp(mine(log_rate))], axis=0)
    params = jnp.pad(params, ((0, 6), (base, 128 - base - heads)))
    skip = jnp.broadcast_to(jnp.repeat(mine(skip_gain), HEAD_M)[None, :], (8, chans))

    tokens = after(tokens, in_cols)
    first_scale = lax.rsqrt(jnp.mean(tokens * tokens, axis=-1, keepdims=True) + EPS)
    unit_tokens = tokens * first_scale
    units_first = gather_ctx(unit_tokens.astype(jnp.bfloat16)).reshape(total_rows, width)
    units_t = lax.optimization_barrier(jnp.transpose(units_first))
    cot_all = gather_ctx(after(cotangent.astype(jnp.bfloat16), units_first))
    cot_all = cot_all.reshape(total_rows, width)
    projected = jnp.dot(units_first, in_all, preferred_element_type=jnp.float32)
    projected = projected.reshape(blocks, block_rows, in_all.shape[1])
    mixed_held, saved, states, kv = mixer_forward(
        sched, projected, filt, table, params, skip, heads, base
    )
    mixed_held = mixed_held.reshape(total_rows, chans + HD)

    hidden = tokens + scatter_ctx(
        jnp.dot(mixed_held, out_mine, preferred_element_type=jnp.float32).reshape(
            count, rows, width
        )
    )

    second_scale = lax.rsqrt(jnp.mean(hidden * hidden, axis=-1, keepdims=True) + EPS)
    unit_hidden = hidden * second_scale
    normed_second = gather_ctx((unit_hidden * gains[1]).astype(jnp.bfloat16)).reshape(
        total_rows, width
    )
    both = matmul_back(normed_second, gate_up_rows)
    gate_part = both[:, : groups * units]
    up_part = both[:, groups * units :]
    silu_gate = jax.nn.silu(gate_part)
    mlp_act = (silu_gate * up_part).astype(jnp.bfloat16)
    d_mlp = matmul_back(cot_all, down_all)
    d_gate = (d_mlp * up_part * silu_slope(gate_part)).astype(jnp.bfloat16)
    d_up = (d_mlp * silu_gate).astype(jnp.bfloat16)
    d_both = jnp.concatenate([d_gate, d_up], axis=1)
    d_normed_second = scatter_ctx(
        jnp.dot(d_both, gate_up_rows, preferred_element_type=jnp.float32).reshape(
            count, rows, width
        )
    )

    def norm_back(d_normed, gain, unit, unit_scale):
        scaled = d_normed * gain
        return unit_scale * (scaled - unit * jnp.mean(scaled * unit, axis=-1, keepdims=True))

    hidden_grad = cotangent + norm_back(d_normed_second, gains[1], unit_hidden, second_scale)
    hidden_b, hidden_far = gather_ctx(hidden_grad.astype(jnp.bfloat16), True)
    hidden_b = hidden_b.reshape(total_rows, width)

    both_grad = matmul_t(d_both, normed_second)
    down_local = matmul_t(mlp_act, cot_all)
    gain_second_grad = jnp.sum(both_grad * gate_up_rows.astype(jnp.float32), axis=0) / gains[1]
    inner_units = groups * units
    mlp_grads = [
        jnp.concatenate(
            [
                both_grad[k * units : (k + 1) * units],
                both_grad[inner_units + k * units : inner_units + (k + 1) * units],
                down_local[k * units : (k + 1) * units],
            ],
            axis=0,
        ).astype(jnp.bfloat16)
        for k in range(groups)
    ]
    mlp_swapped = swap_groups(mlp_grads)
    mlp_sum = sum(piece.astype(jnp.float32) for piece in mlp_swapped)
    mlp_sum = jnp.transpose(
        mlp_sum.astype(jnp.bfloat16).reshape(3 * units, count, width // count), (1, 0, 2)
    )

    d_mix = matmul_back(hidden_b, out_mine).reshape(blocks, block_rows, chans + HD)
    share = width // (count * groups)

    def to_groups(grad):
        parts = grad.reshape(count, groups, share, grad.shape[1])
        return [
            lax.dynamic_index_in_dim(parts, wsh ^ k, 1, keepdims=False).astype(jnp.bfloat16)
            for k in range(groups)
        ]

    places = jnp.array([held_order(count).index(k) for k in range(count)], dtype=jnp.int32)
    by_device = jnp.take(places, ctx ^ jnp.arange(count, dtype=jnp.int32), mode="clip")
    act_by_device = jnp.take(
        mlp_act.reshape(count, rows, inner_units), by_device, axis=0, mode="clip"
    ).reshape(total_rows, inner_units)
    mlp_parts = jnp.dot(act_by_device, down_all, preferred_element_type=jnp.float32)
    mlp_parts = mlp_parts.astype(jnp.bfloat16).reshape(count, rows, width)
    mlp_parts = after(mlp_parts, hidden_far)
    mlp_parts = trade_ctx(mlp_parts)
    output = hidden + jnp.sum(mlp_parts.astype(jnp.float32), axis=0)
    out_grads = to_groups(matmul_t(hidden_b, mixed_held))
    out_swapped = swap_groups(out_grads)
    out_sum = sum(piece.astype(jnp.float32) for piece in out_swapped)
    d_held, filt_grad, head_grad = mixer_backward(
        sched, projected, filt, table, params, skip, saved, states, kv, d_mix, heads, base
    )
    out_sum = out_sum.astype(jnp.bfloat16)
    payload = jnp.concatenate(
        [mlp_sum]
        + [out_sum[:, :, start : start + 128] for start in range(0, out_sum.shape[2], 128)],
        axis=1,
    )
    payload = trade_ctx(after(payload, (mlp_parts, d_held)))
    gate_up_grad, down_grad, mixer_out_grad, attend_out_grad = finish_rest(
        payload, chans, units, share
    )
    mixer_out_grad = jnp.transpose(mixer_out_grad)
    attend_out_grad = jnp.transpose(attend_out_grad)
    d_held = d_held.reshape(total_rows, -1)
    d_unit_first = scatter_ctx(
        matmul_back(d_held, in_all).reshape(count, rows, width)
    )
    input_grad = hidden_grad + norm_back(d_unit_first, 1.0, unit_tokens, first_scale)

    in_grad = jnp.dot(units_t, d_held, preferred_element_type=jnp.float32)
    gain_first_grad = jnp.sum(in_grad * in_all.astype(jnp.float32), axis=1) / gains[0]
    in_grad = in_grad * gains[0][:, None]
    lane = jnp.arange(in_all.shape[1], dtype=jnp.int32)[None, :]
    gain_lane = in_all.shape[1] - step_pad
    in_grad = jnp.where(lane == gain_lane, gain_first_grad[:, None], in_grad)
    in_grad = jnp.where(lane == gain_lane + 1, gain_second_grad[:, None], in_grad)
    in_grads = to_groups(in_grad)
    in_swapped = swap_groups(in_grads)
    in_sum = sum(piece.astype(jnp.float32) for piece in in_swapped)
    mixer_in_grad, attend_in_grad, last_cols = finish_in(
        trade_ctx(after(in_sum.astype(jnp.bfloat16), payload)), heads
    )
    gain_place = gain_lane % 128
    gains_grad = jnp.transpose(last_cols[:, gain_place : gain_place + 2])
    side_by_side = lambda array: jnp.transpose(array, (1, 0, 2)).reshape(array.shape[1], -1)

    small = jnp.concatenate([filt_grad.reshape(-1, 128), head_grad], axis=0)
    small = gather_wsh(small[None])
    small = gather_ctx(jnp.sum(small, axis=0))
    small = jnp.take(small, by_device, axis=0, mode="clip")
    filters = small[:, :-8].reshape(count, 8, 512)[:, : KERNEL + 1]
    filter_grad = jnp.concatenate(
        [side_by_side(filters[:, :, :chans]), jnp.sum(filters[:, :, 256:], axis=0)], axis=1
    )
    per_head = small[:, -8:-5, base : base + heads]
    step_bias_all, log_rate_all, skip_all = [per_head[:, i].reshape(-1) for i in range(3)]
    return (
        output[None],
        input_grad[None],
        gains_grad,
        filter_grad,
        step_bias_all,
        log_rate_all,
        skip_all,
        mixer_in_grad,
        mixer_out_grad,
        attend_in_grad,
        attend_out_grad,
        gate_up_grad,
        down_grad,
    )


def on_device_heads(*args):
    return head_plan(*args)


def solution(mesh):
    placed = (
        P("wsh", "ctx", None),
        P("wsh", "ctx", None),
        P("wsh", None),
        P(),
        P(None, "wsh"),
        P(),
        P(),
        P(),
        P(),
        P("wsh", None),
        P(None, "wsh"),
        P("wsh", None),
        P(None, "wsh"),
        P(None, None, "wsh"),
        P("wsh", None),
    )
    per_heads = mesh.shape["ctx"] == QH
    return jax.shard_map(
        on_device_heads if per_heads else on_device,
        mesh=mesh,
        in_specs=placed,
        out_specs=(
            P("wsh", "ctx", None),
            P("wsh", "ctx", None),
            P(None, ("ctx", "wsh")),
            P(),
            P(),
            P(),
            P(),
            P(("ctx", "wsh"), None),
            P(None, ("ctx", "wsh")),
            P(("ctx", "wsh"), None),
            P(None, ("ctx", "wsh")),
            P(None, "ctx", "wsh"),
            P("wsh", "ctx"),
        ),
        check_vma=False,
    )
```
